32 devices in a mesh: groups: 2 (over x), seq: 8 (over z, y), pipe: 2 (over core).
Axes of the slice: x: 2, y: 2, z: 4, core: 2. Of those that a mesh axis runs over, the one named last changes fastest.
Arguments:
- tokens: bfloat16 [2, 2048, 1440], P('pipe', ('groups', 'seq')), parts along dimension 1, may hold values from -6 to 6
- routes: int32 [2, 2048, 4], P('pipe', ('groups', 'seq')), parts along dimension 1, may hold values from 0 to 15, all different within a row; in each aligned block of 128 rows (0 to 127, 128 to 255, ..., all dimensions but the last counted through in order) at most 48 rows name the same one
- route_weights: float32 [2, 2048, 4], P('pipe', ('groups', 'seq')), parts along dimension 1, may hold values from 0.1 to 1
- moe_gain: float32 [1440], replicated, may hold values from 0.5 to 1.5
- gate_up: bfloat16 [32, 1440, 1440], P('seq'), may hold values from -0.15625 to 0.15625
- down_proj: bfloat16 [32, 720, 1440], P('seq'), may hold values from -0.15625 to 0.15625
- attn_gain: float32 [1440], replicated, may hold values from 0.5 to 1.5
- qkv_proj: bfloat16 [1440, 2560], P('seq'), may hold values from -0.15625 to 0.15625
- head_sink_logits: float32 [32], replicated, may hold values from 3 to 6
- out_proj: bfloat16 [2048, 1440], P('seq'), may hold values from -0.125 to 0.125
Outputs:
- layer_output: bfloat16 [2, 2048, 1440], P('pipe', ('groups', 'seq')), parts along dimension 1
The draws below stay inside these ranges and needn't reach their ends.
There are 2 independent parts, one for each index of `groups`. The reference program is written for one: setup_inputs(seed, part) draws one part's arguments, and reference() takes and returns one part's arrays. A program takes and returns all parts, laid end to end along the dimension named above; an argument that names none is the same for every part. Nothing has to cross between parts.
Inputs may be any that keep to these rules, and one draw needn't show every extreme that they name: `routes`: within the 128 positions of one micro-batch on one index of seq, a token names each of its 4 experts once, and each expert is named by at most 48 tokens; one expert is named by exactly 48 of them.
All inputs are finite; a program needn't handle non-finite values.
Results may differ from the reference program's by a relative error of at most 0.0085.
Values may be sent and summed in bfloat16 or wider, within the bound.
No kernel may reach another device: no remote copies, remote signals or barrier semaphores. Data moves between devices by JAX's collectives and lax.ppermute only.
A program may use at most 128 MiB of HBM per device.

```python
import math
import jax
import jax.numpy as jnp
import numpy as np
from jax import lax

D = 1440
E = 16
H = 1440
TOP = 4
QUERY_HEADS = 32
KEY_VALUE_HEADS = 4
HEAD_SIZE = 64
WINDOW_SPAN = 128
TOK_DEV = 128
HALF = 720
SLABS = 32
CAP = 48
MB = 2
TOKENS = 1024
QKV = 2560
N_SEQ = 8


def shard_levels(stream_key, extent, shards, least, top_value):
    def one(position, shards_of):
        steps = jax.random.uniform(jax.random.fold_in(jax.random.fold_in(stream_key, 6), position), (shards_of,), jnp.float32, least / len(shards), top_value / len(shards))
        return jnp.repeat(jnp.exp(steps), extent[position] // shards_of).reshape((-1,) + (1,) * (len(extent) - position - 1))

    loudness = one(*shards[0])
    for cut in shards[1:]:
        loudness = loudness * one(*cut)
    return loudness


def deal_out(key, own, number, rows, amount, top, most, lean):
    sequence = jax.random.permutation(key, amount)
    packed, usual = load_shares(amount, rows * top, most, lean, True), load_shares(amount, rows * top, most, lean, False)
    places = jnp.arange(amount)

    def named(sizes, rotation):
        used = int((sizes > 0).sum())
        fixed = max(1, used // 4)
        moved = fixed + (places - fixed + rotation * (used - fixed)) % max(1, amount - fixed)
        return jnp.zeros((amount,), jnp.int32).at[sequence[jnp.where(places < fixed, places, moved)]].set(jnp.asarray(sizes, jnp.int32))

    sizes = jnp.where(number % 4 == 0, named(packed, number // 4), named(usual, number - number // 4 - 1))
    mixed = jax.random.permutation(jax.random.fold_in(own, 3), amount)
    source_of, sink = mixed[0:amount // 2 * 2:2], mixed[1:amount // 2 * 2:2]
    slack = jnp.minimum(sizes[source_of] - 1, most - sizes[sink]) // 2
    slack = jnp.where((source_of == sequence[0]) | (sink == sequence[0]) | (sizes[sink] == 0), 0, jnp.maximum(slack, 0))
    moved = jax.random.randint(jax.random.fold_in(own, 4), (amount // 2,), 0, 1 << 20) % (slack + 1)
    sizes = sizes.at[source_of].add(-moved).at[sink].add(moved)
    items = jnp.searchsorted(jnp.cumsum(sizes), jnp.arange(rows * top), side="right").astype(jnp.int32)
    grid = items.reshape(top, rows).T
    grid = grid[jax.random.permutation(jax.random.fold_in(own, 1), rows)]
    rotation = jax.random.randint(jax.random.fold_in(own, 2), (rows, 1), 0, top)
    return jnp.take_along_axis(grid, (jnp.arange(top)[None, :] + rotation) % top, axis=1)


def load_shares(amount, total, bound, slope, full):
    loads = [(1 << 20) // math.isqrt(grade ** slope) + 1 for grade in range(1, amount + 1)]
    largest = bound if full else min(bound, max(-(-total // amount), total * loads[0] // sum(loads)))
    least = 1 if total - largest >= amount - 1 else 0
    counts, spare = [largest] + [least] * (amount - 1), total - largest - least * (amount - 1)
    while spare > 0:
        free = [i for i in range(1, amount) if counts[i] < largest] or [i for i in range(1, amount) if counts[i] < bound]
        pool, remaining = sum([loads[i] for i in free]), spare
        for i in free:
            addition = min(bound - counts[i], max(1, remaining * loads[i] // pool), spare)
            counts[i] = counts[i] + addition
            spare = spare - addition
    return np.array(counts)


def centred(rng, dims, width, most, shards=(), kind=jnp.bfloat16):
    loudness = shard_levels(rng, dims, shards, -0.22, 0.18) if shards else 1.0
    entries = jax.random.normal(rng, dims, jnp.float32) * width * loudness
    return jnp.minimum(jnp.maximum(entries, -most), most).astype(kind)


def setup_inputs(seed: int = 0, part: int = 0) -> dict:
    keys = jax.random.split(jax.random.key(seed), 11)
    own_keys = jax.random.split(jax.random.fold_in(keys[10], part), 11)
    tokens = centred(own_keys[0], (MB, TOKENS, D), 1.0, 6.0, ((0, 2), (1, 8)))
    routes_keys = jax.random.split(jax.random.fold_in(own_keys[1], 1), MB * TOKENS // TOK_DEV)
    routes_turns = jax.random.permutation(jax.random.fold_in(own_keys[1], 3), MB * TOKENS // TOK_DEV)
    routes = jax.vmap(lambda own, number: deal_out(jax.random.fold_in(own_keys[1], 2), own, number, TOK_DEV, E, TOP, CAP, 2))(routes_keys, routes_turns).reshape((MB, TOKENS, TOP))
    route_weights = jnp.clip(0.1 + 0.9 * jax.random.uniform(own_keys[2], (MB, TOKENS, TOP), jnp.float32) ** shard_levels(own_keys[2], (MB, TOKENS, TOP), ((0, 2), (1, 8)), -0.2, 0.2), 0.1, 1.0)
    moe_gain = jnp.clip(1.0 + 0.1 * jax.random.normal(keys[3], (D,), jnp.float32), 0.5, 1.5)
    gate_up = centred(keys[4], (SLABS, D, 2 * HALF), D ** -0.5, 0.15625, ((0, 8),))
    down_proj = centred(keys[5], (SLABS, HALF, D), H ** -0.5, 0.15625, ((0, 8),))
    attn_gain = jnp.clip(1.0 + 0.1 * jax.random.normal(keys[6], (D,), jnp.float32), 0.5, 1.5)
    qkv_proj = centred(keys[7], (D, QKV), D ** -0.5, 0.15625, ((0, 8),))
    head_sink_logits = jnp.clip(jax.random.uniform(keys[8], (QUERY_HEADS,), jnp.float32, 3.0, 6.0), 3.0, 6.0)
    out_proj = centred(keys[9], (QUERY_HEADS * HEAD_SIZE, D), (QUERY_HEADS * HEAD_SIZE) ** -0.5, 0.125, ((0, 8),))
    return {"tokens": tokens, "routes": routes, "route_weights": route_weights, "moe_gain": moe_gain, "gate_up": gate_up, "down_proj": down_proj, "attn_gain": attn_gain, "qkv_proj": qkv_proj, "head_sink_logits": head_sink_logits, "out_proj": out_proj}


eps = 1e-05

def rms_scale(value_matrix, gain):
    widened = value_matrix.astype(jnp.float32)
    mean_square = lax.optimization_barrier(jnp.mean(widened * widened, axis=-1, keepdims=True))
    return (widened * lax.rsqrt(mean_square + eps) * gain).astype(jnp.bfloat16)

def slot_positions(route_rows):
    flat = route_rows.reshape(-1).astype(jnp.int32)
    onehot = (flat[:, None] == jnp.arange(E, dtype=jnp.int32)[None, :]).astype(jnp.int32)
    earlier = jnp.cumsum(onehot, axis=0) - onehot
    return (flat * CAP + lax.optimization_barrier(jnp.sum(earlier * onehot, axis=1))).astype(jnp.int32)

def expert_apply(items):
    rows, pair_gate_up, pair_down = items
    gate_matrix = jnp.concatenate([pair_gate_up[0][:, :HALF], pair_gate_up[1][:, :HALF]], axis=1)
    up_matrix = jnp.concatenate([pair_gate_up[0][:, HALF:], pair_gate_up[1][:, HALF:]], axis=1)
    down_matrix = jnp.concatenate([pair_down[0], pair_down[1]], axis=0)
    gate = jnp.dot(rows, gate_matrix, preferred_element_type=jnp.float32)
    upper = jnp.dot(rows, up_matrix, preferred_element_type=jnp.float32)
    hidden = (gate * jax.nn.sigmoid(1.702 * gate) * (upper + 1.0)).astype(jnp.bfloat16)
    return jnp.dot(hidden, down_matrix, preferred_element_type=jnp.float32).astype(jnp.bfloat16)

def dispatch_block(items):
    rows, route_rows = items
    positions = slot_positions(route_rows)
    source = jnp.repeat(rows, TOP, axis=0)
    table = jnp.zeros((E * CAP, D), jnp.bfloat16).at[positions].set(source)
    return (table, positions)

def pick_rows(results, positions):
    return results[positions]

def moe_block(tokens_mb, routes_mb, weights_mb, moe_gain, gate_up, down_proj):
    normed = rms_scale(tokens_mb, moe_gain)
    blocks = normed.reshape(N_SEQ, TOK_DEV, D)
    route_blocks = routes_mb.reshape(N_SEQ, TOK_DEV, TOP)
    tables, positions = lax.map(dispatch_block, (blocks, route_blocks))
    per_expert = tables.reshape(N_SEQ, E, CAP, D).transpose(1, 0, 2, 3).reshape(E, N_SEQ * CAP, D)
    results = lax.map(expert_apply, (per_expert, gate_up.reshape(E, 2, D, 2 * HALF), down_proj.reshape(E, 2, HALF, D)))
    results = results.reshape(E, N_SEQ, CAP, D).transpose(1, 0, 2, 3).reshape(N_SEQ, E * CAP, D)
    picked = jax.vmap(pick_rows)(results, positions)
    picked = picked.reshape(TOKENS, TOP, D).astype(jnp.float32)
    summed = tokens_mb.astype(jnp.float32) + lax.optimization_barrier(jnp.sum(picked * weights_mb[:, :, None], axis=1))
    return summed.astype(jnp.bfloat16)

def attention_all(hidden_all, attn_gain, qkv_proj, head_sink_logits, out_proj):
    length = hidden_all.shape[0]
    query_groups = QUERY_HEADS // KEY_VALUE_HEADS
    normed = rms_scale(hidden_all, attn_gain)
    packed_heads = lax.optimization_barrier(jnp.dot(normed, qkv_proj, preferred_element_type=jnp.float32).astype(jnp.bfloat16)).astype(jnp.float32)
    query_matrix = packed_heads[:, :QUERY_HEADS * HEAD_SIZE]
    key_matrix = packed_heads[:, QUERY_HEADS * HEAD_SIZE:(QUERY_HEADS + KEY_VALUE_HEADS) * HEAD_SIZE]
    value_matrix = packed_heads[:, (QUERY_HEADS + KEY_VALUE_HEADS) * HEAD_SIZE:]
    padding_rows = jnp.zeros((WINDOW_SPAN, KEY_VALUE_HEADS * HEAD_SIZE), jnp.float32)
    keys_extended = jnp.concatenate([padding_rows, key_matrix], axis=0)
    values_extended = jnp.concatenate([padding_rows, value_matrix], axis=0)
    scale = float(HEAD_SIZE) ** (-0.5)
    sink_mass_total = jnp.exp(head_sink_logits).reshape(KEY_VALUE_HEADS, query_groups, 1, 1)

    def one_block(index):
        start_position = (index * WINDOW_SPAN).astype(jnp.int32)
        rows_of_queries = lax.dynamic_slice_in_dim(query_matrix, start_position, WINDOW_SPAN, 0).reshape(WINDOW_SPAN, KEY_VALUE_HEADS, query_groups, HEAD_SIZE)
        rows_of_keys = lax.dynamic_slice_in_dim(keys_extended, start_position, 2 * WINDOW_SPAN, 0).reshape(2 * WINDOW_SPAN, KEY_VALUE_HEADS, HEAD_SIZE)
        rows_of_values = lax.dynamic_slice_in_dim(values_extended, start_position, 2 * WINDOW_SPAN, 0).reshape(2 * WINDOW_SPAN, KEY_VALUE_HEADS, HEAD_SIZE)
        scores = jnp.einsum('qhgd,khd->hgqk', rows_of_queries, rows_of_keys) * scale
        query_pos = start_position + jnp.arange(WINDOW_SPAN, dtype=jnp.int32)
        key_pos = start_position - WINDOW_SPAN + jnp.arange(2 * WINDOW_SPAN, dtype=jnp.int32)
        distance = query_pos[:, None] - key_pos[None, :]
        allowed = (distance >= 0) & (distance < WINDOW_SPAN) & (key_pos[None, :] >= 0)
        weights = jnp.where(allowed, jnp.exp(scores), 0.0)
        total = lax.optimization_barrier(jnp.sum(weights, axis=-1, keepdims=True)) + sink_mass_total
        probs = lax.optimization_barrier((weights / total).astype(jnp.bfloat16)).astype(jnp.float32)
        mixed = jnp.einsum('hgqk,khd->qhgd', probs, rows_of_values)
        return mixed.reshape(WINDOW_SPAN, QUERY_HEADS * HEAD_SIZE).astype(jnp.bfloat16)
    attended = lax.map(one_block, jnp.arange(length // WINDOW_SPAN, dtype=jnp.int32)).reshape(length, QUERY_HEADS * HEAD_SIZE)
    projected = jnp.dot(attended, out_proj, preferred_element_type=jnp.float32)
    return (hidden_all.astype(jnp.float32) + projected).astype(jnp.bfloat16)

def reference(tokens, routes, route_weights, moe_gain, gate_up, down_proj, attn_gain, qkv_proj, head_sink_logits, out_proj):
    sections = []
    for index in range(MB):
        sections.append(moe_block(tokens[index], routes[index], route_weights[index], moe_gain, gate_up, down_proj))
    whole = jnp.stack(sections).reshape(MB * TOKENS, D)
    result = attention_all(whole, attn_gain, qkv_proj, head_sink_logits, out_proj)
    return result.reshape(MB, TOKENS, D)
```

```python
import functools

import jax
import jax.numpy as jnp
from jax import lax
from jax.experimental import pallas as pl
from jax.experimental.pallas import tpu as pltpu
from jax.sharding import PartitionSpec as P

E = 16
TOP = 4
QUERY_HEADS = 32
KEY_VALUE_HEADS = 4
HEAD_SIZE = 64
WINDOW_SPAN = 128
HALF = 720
CAP = 48


eps = 1e-05


F32 = jnp.float32
BF16 = jnp.bfloat16
VMEM = pl.BlockSpec(memory_space=pltpu.VMEM)
SMEM = pl.BlockSpec(memory_space=pltpu.SMEM)
ANY = pl.BlockSpec(memory_space=pl.ANY)


def route_slots(routes_ref):
    tok_count = routes_ref.shape[1]
    expert = lax.broadcasted_iota(jnp.int32, (E, tok_count), 0)
    member = jnp.zeros((E, tok_count), jnp.bool_)
    for k in range(routes_ref.shape[0]):
        member = member | (routes_ref[k : k + 1, :] == expert)
    first = lax.broadcasted_iota(jnp.int32, (tok_count, tok_count), 0)
    second = lax.broadcasted_iota(jnp.int32, (tok_count, tok_count), 1)
    before = jnp.where(first < second, 1.0, 0.0).astype(BF16)
    flags = jnp.where(member, 1.0, 0.0)
    rank = jnp.dot(flags.astype(BF16), before, preferred_element_type=F32)
    return flags, jnp.where(flags > 0.0, rank, -1.0)


def dispatch_kernel(tokens_ref, routes_ref, gain_ref, table_ref):
    tok_count = tokens_ref.shape[1]
    value = tokens_ref[...].astype(F32).T
    mean_square = jnp.mean(value * value, axis=-1, keepdims=True)
    normed = (value * lax.rsqrt(mean_square + eps) * gain_ref[...]).astype(BF16)
    _, rank = route_slots(routes_ref)
    slot = lax.broadcasted_iota(jnp.int32, (CAP, tok_count), 0).astype(F32)
    for expert in range(E):
        select = jnp.where(slot == rank[expert : expert + 1, :], 1.0, 0.0).astype(BF16)
        table_ref[expert] = jnp.dot(select, normed, preferred_element_type=F32).astype(BF16)


def dispatch(tokens_t, routes_t, gain):
    width = tokens_t.shape[0]
    return pl.pallas_call(
        dispatch_kernel,
        out_shape=jax.ShapeDtypeStruct((E, CAP, width), BF16),
        in_specs=[VMEM] * 3,
        out_specs=VMEM,
        name="dispatch",
    )(tokens_t, routes_t, gain)


def returns_kernel(tokens_ref, routes_ref, scale_ref, residual_ref, coarse_ref, fine_ref):
    tok_count = tokens_ref.shape[1]
    residual_ref[...] = tokens_ref[...].astype(F32).T.astype(BF16)
    _, rank = route_slots(routes_ref)
    expert_index = lax.broadcasted_iota(jnp.int32, (E, tok_count), 0)
    scale = jnp.zeros((E, tok_count), F32)
    for k in range(routes_ref.shape[0]):
        scale += jnp.where(routes_ref[k : k + 1, :] == expert_index, scale_ref[k : k + 1, :], 0.0)
    slot = lax.broadcasted_iota(jnp.int32, (CAP, tok_count), 0).astype(F32)
    rows = []
    for expert in range(E):
        hit = slot == rank[expert : expert + 1, :]
        rows.append(jnp.where(hit, scale[expert : expert + 1, :], 0.0))
    weighted = jnp.concatenate(rows, axis=0).T
    coarse = weighted.astype(BF16)
    coarse_ref[...] = coarse
    fine_ref[...] = (weighted - coarse.astype(F32)).astype(BF16)


def returns(tokens_t, routes_t, scale_t):
    width, tok_count = tokens_t.shape
    return pl.pallas_call(
        returns_kernel,
        out_shape=(
            jax.ShapeDtypeStruct((tok_count, width), BF16),
            jax.ShapeDtypeStruct((tok_count, E * CAP), BF16),
            jax.ShapeDtypeStruct((tok_count, E * CAP), BF16),
        ),
        in_specs=[VMEM] * 3,
        out_specs=(VMEM,) * 3,
        name="returns",
    )(tokens_t, routes_t, scale_t)


def experts_kernel(rows_ref, gate_up_ref, down_ref, out_ref, total_ref):
    slab = pl.program_id(1)
    blocks, cap, width = rows_ref.shape
    rows = rows_ref[...].reshape(blocks * cap, width)
    projected = jnp.dot(rows, gate_up_ref[...], preferred_element_type=F32)
    gate_part = projected[:, :HALF]
    up_part = projected[:, HALF:]
    hidden = (gate_part * jax.nn.sigmoid(1.702 * gate_part) * (up_part + 1.0)).astype(BF16)
    value = jnp.dot(hidden, down_ref[...], preferred_element_type=F32)

    @pl.when(slab == 0)
    def _():
        total_ref[...] = value

    @pl.when(slab > 0)
    def _():
        total_ref[...] += value

    @pl.when(slab == pl.num_programs(1) - 1)
    def _():
        out_ref[...] = total_ref[...].astype(BF16).reshape(blocks, cap, width)


def run_experts(received, gate_up, down_proj):
    seq_count, experts, cap, width = received.shape
    slabs = gate_up.shape[0] // experts
    rows_spec = pl.BlockSpec((seq_count, None, cap, width), lambda e, k: (0, e, 0, 0))
    return pl.pallas_call(
        experts_kernel,
        out_shape=jax.ShapeDtypeStruct(received.shape, BF16),
        grid=(experts, slabs),
        in_specs=[
            rows_spec,
            pl.BlockSpec((None, width, gate_up.shape[2]), lambda e, k: (e * slabs + k, 0, 0)),
            pl.BlockSpec((None, down_proj.shape[1], width), lambda e, k: (e * slabs + k, 0, 0)),
        ],
        out_specs=rows_spec,
        scratch_shapes=[pltpu.VMEM((seq_count * cap, width), F32)],
        compiler_params=pltpu.CompilerParams(vmem_limit_bytes=48 << 20),
        name="experts",
    )(received, gate_up, down_proj)


def shard_of(place_ref, step, flip, lines):
    line = lax.rem(place_ref[0] - step + lines, lines)
    return line * 2 + (place_ref[1] + flip) % 2


def quarter_of(place_ref, group_flip, pipe_flip):
    return (place_ref[2] + group_flip) % 2 * 2 + (place_ref[3] + pipe_flip) % 2


def qkv_kernel(
    rows, place_ref, tables_ref, residual_ref, coarse_ref, fine_ref, gain_ref, *rest
):
    parts, (packed_ref, hidden_ref, held, slices, sems) = rest[:8], rest[8:]
    lines, padded, columns = held.shape[1:]
    copies = []
    for i, part in enumerate(parts):
        copy = pltpu.make_async_copy(part.at[:, :, pl.ds(0, columns)], held.at[i], sems.at[i])
        copy.start()
        copies.append(copy)
    table = tables_ref[...]
    mixed = jnp.dot(coarse_ref[...], table, preferred_element_type=F32)
    mixed += jnp.dot(fine_ref[...], table, preferred_element_type=F32)
    hidden = (residual_ref[...].astype(F32) + mixed).astype(BF16)
    value = hidden.astype(F32)
    hidden_ref[...] = value.T.astype(BF16)
    mean_square = jnp.mean(value * value, axis=-1, keepdims=True)
    normed = value * lax.rsqrt(mean_square + eps) * gain_ref[...]
    slices[...] = jnp.zeros_like(slices)
    for s in range(2 * lines):
        slices[s, :, :rows] = normed[:, s * rows : (s + 1) * rows].astype(BF16)
    for pair in range(4):
        total = jnp.zeros((value.shape[0], columns), F32)
        for flip in range(2):
            copies[pair * 2 + flip].wait()
            for step in range(lines):
                total += jnp.dot(
                    slices[shard_of(place_ref, step, flip, lines)],
                    held[pair * 2 + flip, step],
                    preferred_element_type=F32,
                )
        start = quarter_of(place_ref, pair % 2, pair // 2) * columns
        packed_ref[:, pl.ds(pl.multiple_of(start, 128), columns)] = total.astype(BF16)


def project_qkv(place, tables, residual, coarse, fine, gain, parts, rows, columns):
    tok_count, width = residual.shape
    lines, padded = parts[0].shape[:2]
    return pl.pallas_call(
        functools.partial(qkv_kernel, rows),
        out_shape=(
            jax.ShapeDtypeStruct((tok_count, 4 * columns), BF16),
            jax.ShapeDtypeStruct((width, tok_count), BF16),
        ),
        in_specs=[SMEM] + [VMEM] * 5 + [ANY] * 8,
        out_specs=(VMEM, VMEM),
        scratch_shapes=[
            pltpu.VMEM((8, lines, padded, columns), BF16),
            pltpu.VMEM((2 * lines, tok_count, padded), BF16),
            pltpu.SemaphoreType.DMA((8,)),
        ],
        compiler_params=pltpu.CompilerParams(vmem_limit_bytes=40 << 20),
        name="qkv",
    )(place, tables, residual, coarse, fine, gain, *parts)


def attention_kernel(
    place_ref, sink_ref, packed_ref, halo_ref, hidden_ref, *rest
):
    parts, (out_ref, held, mixed, total_ref, sems) = rest[:8], rest[8:]
    lines, padded, columns = held.shape[1:]
    depth = mixed.shape[2]
    fold = columns // depth
    quarter_rows = out_ref.shape[0] // 4
    first_column = parts[0].shape[2] - columns
    copies = []
    for i, part in enumerate(parts):
        copy = pltpu.make_async_copy(
            part.at[:, :, pl.ds(first_column, columns)], held.at[i], sems.at[i]
        )
        copy.start()
        copies.append(copy)
    tok_count = packed_ref.shape[0]
    pair_width = 2 * HEAD_SIZE
    query_width = QUERY_HEADS * HEAD_SIZE
    kv_width = KEY_VALUE_HEADS * HEAD_SIZE
    query_groups = QUERY_HEADS // KEY_VALUE_HEADS
    span = halo_ref.shape[0]
    extent = span + tok_count
    query_pos = lax.broadcasted_iota(jnp.int32, (tok_count, extent), 0) + span
    key_pos = lax.broadcasted_iota(jnp.int32, (tok_count, extent), 1)
    distance = query_pos - key_pos
    halo_valid = place_ref[0] + place_ref[1] + place_ref[3] > 0
    first_key = jnp.where(halo_valid, 0, span)
    allowed = (distance >= 0) & (distance < WINDOW_SPAN) & (key_pos >= first_key)
    left = lax.broadcasted_iota(jnp.int32, (extent, pair_width), 1) < HEAD_SIZE
    scale = float(HEAD_SIZE) ** (-0.5)

    def sides(start, head):
        lanes = pl.ds(start + head // 2 * pair_width, pair_width)
        own = packed_ref[:, query_width + start + head // 2 * pair_width :][:, :pair_width]
        both = jnp.concatenate([halo_ref[:, lanes], own], axis=0).astype(F32)
        turned = pltpu.roll(both, HEAD_SIZE, 1)
        low, high = (both, turned) if head % 2 == 0 else (turned, both)
        low = jnp.where(left, low, 0.0).astype(BF16)
        high = jnp.where(left, 0.0, high).astype(BF16)
        return low, high

    pairs = query_groups // 2
    for head in range(KEY_VALUE_HEADS):
        keys, values = sides(0, head), sides(kv_width, head)
        base = head * pairs * pair_width
        stacked = jnp.concatenate(
            [packed_ref[:, base + j * pair_width : base + (j + 1) * pair_width] for j in range(pairs)],
            axis=0,
        )
        outcome = None
        for side in range(2):
            scores = lax.dot_general(
                stacked, keys[side], (((1,), (1,)), ((), ())), preferred_element_type=F32
            )
            probs = []
            for j in range(pairs):
                piece = scores[j * tok_count : (j + 1) * tok_count] * scale
                weights = jnp.where(allowed, jnp.exp(piece), 0.0)
                sink = sink_ref[head * query_groups + 2 * j + side]
                sums = jnp.sum(weights, axis=-1, keepdims=True) + sink
                probs.append((weights / sums).astype(BF16))
            part = jnp.dot(
                jnp.concatenate(probs, axis=0), values[side], preferred_element_type=F32
            )
            outcome = part if outcome is None else outcome + part
        for j in range(pairs):
            column = base + j * pair_width
            mixed[column // depth, :, column % depth : column % depth + pair_width] = outcome[
                j * tok_count : (j + 1) * tok_count
            ].astype(BF16)

    for pair in range(4):
        totals = [jnp.zeros((padded, tok_count), F32) for _ in range(fold)]
        for flip in range(2):
            copies[pair * 2 + flip].wait()
            for step in range(lines):
                against = mixed[shard_of(place_ref, step, flip, lines)]
                for i in range(fold):
                    totals[i] += lax.dot_general(
                        held[pair * 2 + flip, step, :, i * depth : (i + 1) * depth],
                        against,
                        (((1,), (1,)), ((), ())),
                        preferred_element_type=F32,
                    )
        start = quarter_of(place_ref, pair % 2, pair // 2) * quarter_rows
        for i in range(fold):
            count = min(padded, quarter_rows - i * padded)
            total_ref[pl.ds(pl.multiple_of(start + i * padded, 8), count), :] = totals[i][:count]
    out_ref[...] = (hidden_ref[...].astype(F32) + total_ref[...]).astype(BF16)


def attend_and_project(place, sinks, packed, halo, hidden_t, parts, columns, depth):
    width, tok_count = hidden_t.shape
    lines, padded = parts[0].shape[:2]
    return pl.pallas_call(
        attention_kernel,
        out_shape=jax.ShapeDtypeStruct((width, tok_count), BF16),
        in_specs=[SMEM] * 2 + [VMEM] * 3 + [ANY] * 8,
        out_specs=VMEM,
        scratch_shapes=[
            pltpu.VMEM((8, lines, padded, columns), BF16),
            pltpu.VMEM((2 * lines, tok_count, depth), BF16),
            pltpu.VMEM((width, tok_count), F32),
            pltpu.SemaphoreType.DMA((8,)),
        ],
        compiler_params=pltpu.CompilerParams(vmem_limit_bytes=40 << 20),
        name="attention",
    )(place, sinks, packed, halo, hidden_t, *parts)


def place_of():
    seq_index = lax.axis_index("seq")
    return jnp.stack(
        [seq_index // 2, seq_index % 2, lax.axis_index("groups") % 2, lax.axis_index("pipe")]
    ).astype(jnp.int32)


def shard_block(qkv_proj, out_proj):
    rows, qkv_width = qkv_proj.shape
    depth, width = out_proj.shape
    quarter = lax.axis_index("groups") % 2 * 2 + lax.axis_index("pipe")
    qw, ow = qkv_width // 4, width // 4
    padded = rows + -rows % 8
    mine_qkv = lax.dynamic_slice_in_dim(qkv_proj, quarter * qw, qw, 1)
    mine_out = lax.dynamic_slice_in_dim(out_proj.T, quarter * ow, ow, 0)
    pieces = [jnp.pad(mine_qkv, ((0, padded - rows), (0, 0)))]
    for first in range(0, ow, padded):
        piece = mine_out[first : first + padded]
        pieces.append(jnp.pad(piece, ((0, padded - piece.shape[0]), (0, 0))))
    return jnp.concatenate(pieces, axis=1)


def fused_body(
    tokens, routes, route_weights, moe_gain, gate_up, down_proj, attn_gain, qkv_proj, sinks, out_proj
):
    seq_count = lax.axis_size("seq")
    tok_count, width = tokens.shape[1:]
    per_device = gate_up.shape[0]
    rows, qkv_width = qkv_proj.shape
    depth = out_proj.shape[0]
    tokens_t, routes_t, scale_t = tokens[0].T, routes[0].T, route_weights[0].T
    block = shard_block(qkv_proj, out_proj)
    column = jnp.stack(neighbour_relay(block, seq_count))
    other = swapped(column, "seq")
    parts = [column, other, swapped(column, "groups"), swapped(other, "groups")]
    parts += [swapped(part, "pipe") for part in parts]

    table = dispatch(tokens_t, routes_t, moe_gain.reshape(1, width))
    outgoing = table.reshape(seq_count, per_device // 2, CAP, width)
    received = lax.all_to_all(outgoing, "seq", split_axis=0, concat_axis=0, tiled=True)
    finished = run_experts(received, gate_up, down_proj)
    summed = lax.all_to_all(finished, "seq", split_axis=0, concat_axis=0, tiled=True)
    summed = summed.reshape(E * CAP, width)
    residual, coarse, fine = returns(tokens_t, routes_t, scale_t)
    place = place_of()
    packed, hidden_t = project_qkv(
        place, summed, residual, coarse, fine, attn_gain.reshape(1, width), parts, rows, qkv_width // 4
    )
    query_width = QUERY_HEADS * HEAD_SIZE
    halo = halo_exchange(packed[tok_count - WINDOW_SPAN :, query_width:])
    columns = block.shape[1] - qkv_width // 4
    out_t = attend_and_project(place, jnp.exp(sinks), packed, halo, hidden_t, parts, columns, depth)
    return out_t.T[None]


def swapped(value, axis):
    return lax.ppermute(value, axis, [(i, i ^ 1) for i in range(lax.axis_size(axis))])


def rms_scale(value_matrix, gain):
    widened = value_matrix.astype(jnp.float32)
    mean_square = jnp.mean(widened * widened, axis=-1, keepdims=True)
    return (widened * lax.rsqrt(mean_square + eps) * gain).astype(jnp.bfloat16)


def routing_tables(route_rows, route_scale):
    tok_count = route_rows.shape[0]
    experts = jnp.arange(E, dtype=jnp.int32)
    named = route_rows[None, :, :] == experts[:, None, None]
    member = jnp.any(named, axis=2)
    scale = jnp.sum(jnp.where(named, route_scale[None, :, :], 0.0), axis=2)
    token = jnp.arange(tok_count, dtype=jnp.int32)
    before = (token[:, None] < token[None, :]).astype(jnp.bfloat16)
    rank = jnp.dot(member.astype(jnp.bfloat16), before, preferred_element_type=jnp.float32)
    slot = jnp.arange(CAP, dtype=jnp.float32)
    chosen = member[:, None, :] & (rank[:, None, :] == slot[None, :, None])
    select = chosen.reshape(E * CAP, tok_count).astype(jnp.bfloat16)
    weighted = jnp.where(chosen, scale[:, None, :], 0.0).reshape(E * CAP, tok_count)
    return select, weighted


def neighbour_relay(block, seq_count):
    rounds = seq_count // 2
    up = [(i, i + 2) for i in range(seq_count - 2)]
    down = [(i + 2, i) for i in range(seq_count - 2)]
    rising, falling = [block], [block]
    for _ in range(rounds - 1):
        rising.append(lax.ppermute(rising[-1], "seq", up))
        falling.append(lax.ppermute(falling[-1], "seq", down))
    line = lax.axis_index("seq") // 2
    blocks = [block]
    for k in range(1, rounds):
        blocks.append(jnp.where(line >= k, rising[k], falling[rounds - k]))
    return blocks


def gather_weights(qkv_proj, out_proj):
    seq_count = lax.axis_size("seq")
    rows, qkv_width = qkv_proj.shape
    depth, width = out_proj.shape
    group_bit = lax.axis_index("groups") % 2
    pipe_bit = lax.axis_index("pipe")
    quarter = group_bit * 2 + pipe_bit
    qw, ow = qkv_width // 4, width // 4
    fold = ow // rows
    mine_qkv = lax.dynamic_slice_in_dim(qkv_proj, quarter * qw, qw, 1)
    mine_out = lax.dynamic_slice_in_dim(out_proj.T, quarter * ow, ow, 0)
    block = jnp.concatenate(
        [mine_qkv] + [mine_out[i * rows : (i + 1) * rows] for i in range(fold)], axis=1
    )
    blocks = neighbour_relay(block, seq_count)
    lines = seq_count // 2
    line = lax.axis_index("seq") // 2
    stacked = jnp.stack(blocks)
    column = jnp.stack(
        [lax.dynamic_index_in_dim(stacked, (line - j) % lines, 0, keepdims=False) for j in range(lines)]
    )
    other = swapped(column, "seq")
    odd = lax.axis_index("seq") % 2 == 1
    both = jnp.stack([jnp.where(odd, other, column), jnp.where(odd, column, other)], axis=1)
    both = both.reshape(seq_count, rows, block.shape[1])
    across = swapped(both, "groups")
    high = group_bit == 1
    halves = jnp.stack([jnp.where(high, across, both), jnp.where(high, both, across)])
    beside = swapped(halves, "pipe")
    second = pipe_bit == 1
    whole = jnp.stack([jnp.where(second, beside, halves), jnp.where(second, halves, beside)], axis=1)
    whole = whole.reshape(4, seq_count, rows, block.shape[1])
    qkv_full = whole[..., :qw].transpose(1, 2, 0, 3).reshape(seq_count * rows, qkv_width)
    out_full = whole[..., qw:].reshape(4, seq_count, rows, fold, depth)
    out_full = out_full.transpose(1, 4, 0, 3, 2).reshape(seq_count * depth, width)
    return qkv_full, out_full


def expert_layer(local, route_rows, route_scale, moe_gain, gate_up, down_proj):
    tok_count, width = local.shape
    seq_count = lax.axis_size("seq")
    per_device = gate_up.shape[0]
    normed = rms_scale(local, moe_gain)
    select, weighted = routing_tables(route_rows, route_scale)
    table = jnp.dot(select, normed, preferred_element_type=jnp.float32).astype(jnp.bfloat16)
    by_expert = table.reshape(E, CAP, width)
    experts = max(1, per_device // 2)
    slabs = per_device // experts
    if slabs == 1:
        by_expert = jnp.repeat(by_expert, 2, axis=0)
    outgoing = by_expert.reshape(seq_count, experts, CAP, width)
    received = lax.all_to_all(outgoing, "seq", split_axis=0, concat_axis=0, tiled=True)
    rows = received.transpose(1, 0, 2, 3).reshape(experts, seq_count * CAP, width)
    gate_up = gate_up.reshape(experts, slabs, width, 2 * HALF)
    down_proj = down_proj.reshape(experts, slabs, HALF, width)
    projected = jnp.einsum("erd,ekdh->ekrh", rows, gate_up, preferred_element_type=jnp.float32)
    gate_part = projected[..., :HALF]
    up_part = projected[..., HALF:]
    hidden = (gate_part * jax.nn.sigmoid(1.702 * gate_part) * (up_part + 1.0)).astype(jnp.bfloat16)
    partial_value = jnp.einsum(
        "ekrh,ekhd->erd", hidden, down_proj, preferred_element_type=jnp.float32
    ).reshape(experts, seq_count, CAP, width)
    partial_value = partial_value.transpose(1, 0, 2, 3)
    if slabs == 2:
        finished = partial_value.astype(jnp.bfloat16)
    else:
        first = lax.axis_index("seq") % 2 == 0
        lower_rows = partial_value[:, :, : CAP // 2]
        upper_rows = partial_value[:, :, CAP // 2 :]
        kept = jnp.where(first, lower_rows, upper_rows)
        given = jnp.where(first, upper_rows, lower_rows)
        partner_part = swapped(given.astype(jnp.bfloat16), "seq").astype(given.dtype)
        finished = (kept + partner_part).astype(jnp.bfloat16)
    summed = lax.all_to_all(finished, "seq", split_axis=0, concat_axis=0, tiled=True).reshape(
        E * CAP, width
    )
    coarse = weighted.astype(jnp.bfloat16)
    fine = (weighted - coarse.astype(jnp.float32)).astype(jnp.bfloat16)
    dims = (((0,), (0,)), ((), ()))
    mixed = lax.dot_general(coarse, summed, dims, preferred_element_type=jnp.float32)
    mixed += lax.dot_general(fine, summed, dims, preferred_element_type=jnp.float32)
    return (local.astype(jnp.float32) + mixed).astype(jnp.bfloat16)


def attend(query_matrix, keys_extended, values_extended, head_sink_logits, halo_valid):
    tok_count = query_matrix.shape[0]
    query_groups = QUERY_HEADS // KEY_VALUE_HEADS
    scale = float(HEAD_SIZE) ** (-0.5)
    sink_mass_total = jnp.exp(head_sink_logits).reshape(KEY_VALUE_HEADS, query_groups, 1, 1)
    block_queries = query_matrix.reshape(tok_count, KEY_VALUE_HEADS, query_groups, HEAD_SIZE)
    block_keys = keys_extended.reshape(tok_count + WINDOW_SPAN, KEY_VALUE_HEADS, HEAD_SIZE)
    block_values = values_extended.reshape(tok_count + WINDOW_SPAN, KEY_VALUE_HEADS, HEAD_SIZE)
    scores = (
        jnp.einsum("qhgd,khd->hgqk", block_queries, block_keys, preferred_element_type=jnp.float32)
        * scale
    )
    query_pos = jnp.arange(tok_count, dtype=jnp.int32)[:, None] + WINDOW_SPAN
    key_pos = jnp.arange(tok_count + WINDOW_SPAN, dtype=jnp.int32)[None, :]
    distance = query_pos - key_pos
    allowed = (distance >= 0) & (distance < WINDOW_SPAN) & ((key_pos >= WINDOW_SPAN) | halo_valid)
    weights = jnp.where(allowed, jnp.exp(scores), 0.0)
    probs = (weights / (jnp.sum(weights, axis=-1, keepdims=True) + sink_mass_total)).astype(
        jnp.bfloat16
    )
    mixed = jnp.einsum("hgqk,khd->qhgd", probs, block_values, preferred_element_type=jnp.float32)
    return mixed.reshape(tok_count, QUERY_HEADS * HEAD_SIZE).astype(jnp.bfloat16)


def halo_exchange(pairs):
    seq_count, pipe_count = lax.axis_size("seq"), lax.axis_size("pipe")
    order = [s * pipe_count + p for p in range(pipe_count) for s in range(seq_count)]
    return lax.ppermute(pairs, ("seq", "pipe"), list(zip(order[:-1], order[1:])))


def body(
    tokens,
    routes,
    route_weights,
    moe_gain,
    gate_up,
    down_proj,
    attn_gain,
    qkv_proj,
    head_sink_logits,
    out_proj,
):
    if gate_up.shape[0] % 2 == 0 and out_proj.shape[0] % 128 == 0 and tokens.shape[1] == WINDOW_SPAN:
        return fused_body(
            tokens,
            routes,
            route_weights,
            moe_gain,
            gate_up,
            down_proj,
            attn_gain,
            qkv_proj,
            head_sink_logits,
            out_proj,
        )
    qkv_full, out_full = gather_weights(qkv_proj, out_proj)
    hidden = expert_layer(tokens[0], routes[0], route_weights[0], moe_gain, gate_up, down_proj)
    tok_count, width = hidden.shape
    normed = rms_scale(hidden, attn_gain)
    seq_index = lax.axis_index("seq")
    pipe_index = lax.axis_index("pipe")
    halo_valid = (seq_index > 0) | (pipe_index > 0)
    query_width = QUERY_HEADS * HEAD_SIZE
    width_of_pair = KEY_VALUE_HEADS * HEAD_SIZE
    packed_heads = jnp.dot(normed, qkv_full, preferred_element_type=jnp.float32).astype(
        jnp.bfloat16
    )
    own_pairs = packed_heads[:, query_width:]
    halo_pairs = halo_exchange(own_pairs[tok_count - WINDOW_SPAN :])
    query_matrix = packed_heads[:, :query_width]
    pairs_ext = jnp.concatenate([halo_pairs, own_pairs], axis=0)
    keys_extended = pairs_ext[:, :width_of_pair]
    values_extended = pairs_ext[:, width_of_pair:]
    attended = attend(query_matrix, keys_extended, values_extended, head_sink_logits, halo_valid)
    projected = jnp.dot(attended, out_full, preferred_element_type=jnp.float32)
    return (hidden.astype(jnp.float32) + projected).astype(jnp.bfloat16)[None]


def solution(mesh):
    in_specs = (
        P("pipe", ("groups", "seq"), None),
        P("pipe", ("groups", "seq"), None),
        P("pipe", ("groups", "seq"), None),
        P(),
        P("seq", None, None),
        P("seq", None, None),
        P(),
        P("seq", None),
        P(),
        P("seq", None),
    )
    out_specs = P("pipe", ("groups", "seq"), None)
    return jax.shard_map(body, mesh=mesh, in_specs=in_specs, out_specs=out_specs, check_vma=False)
```

```python
import functools

import jax
import jax.numpy as jnp
from jax import lax
from jax.experimental import pallas as pl
from jax.experimental.pallas import tpu as pltpu
from jax.sharding import PartitionSpec as P


E = 16
QUERY_HEADS = 32
KEY_VALUE_HEADS = 4
HEAD_SIZE = 64
WINDOW_SPAN = 128
HALF = 720
CAP = 48


eps = 1e-05


F32 = jnp.float32
BF16 = jnp.bfloat16
VMEM = pl.BlockSpec(memory_space=pltpu.VMEM)
SMEM = pl.BlockSpec(memory_space=pltpu.SMEM)
HBM = pl.BlockSpec(memory_space=pltpu.HBM)


def route_slots(routes_ref):
    tok_count = routes_ref.shape[1]
    expert = lax.broadcasted_iota(jnp.int32, (E, tok_count), 0)
    member = jnp.zeros((E, tok_count), jnp.bool_)
    for k in range(routes_ref.shape[0]):
        member = member | (routes_ref[k : k + 1, :] == expert)
    first = lax.broadcasted_iota(jnp.int32, (tok_count, tok_count), 0)
    second = lax.broadcasted_iota(jnp.int32, (tok_count, tok_count), 1)
    before = jnp.where(first < second, 1.0, 0.0).astype(BF16)
    flags = jnp.where(member, 1.0, 0.0)
    rank = jnp.dot(flags.astype(BF16), before, preferred_element_type=F32)
    return flags, jnp.where(flags > 0.0, rank, -1.0)


def dispatch_kernel(tokens_ref, routes_ref, gain_ref, table_ref):
    tok_count = tokens_ref.shape[1]
    value = tokens_ref[...].astype(F32).T
    mean_square = jnp.mean(value * value, axis=-1, keepdims=True)
    normed = (value * lax.rsqrt(mean_square + eps) * gain_ref[...]).astype(BF16)
    _, rank = route_slots(routes_ref)
    slot = lax.broadcasted_iota(jnp.int32, (CAP, tok_count), 0).astype(F32)
    for expert in range(E):
        select = jnp.where(slot == rank[expert : expert + 1, :], 1.0, 0.0).astype(BF16)
        table_ref[expert] = jnp.dot(select, normed, preferred_element_type=F32).astype(BF16)


def dispatch(tokens_t, routes_t, gain):
    width = tokens_t.shape[0]
    return pl.pallas_call(
        dispatch_kernel,
        out_shape=jax.ShapeDtypeStruct((E, CAP, width), BF16),
        in_specs=[VMEM] * 3,
        out_specs=VMEM,
        name="dispatch",
    )(tokens_t, routes_t, gain)


def returns_kernel(tokens_ref, routes_ref, scale_ref, residual_ref, coarse_ref, fine_ref):
    tok_count = tokens_ref.shape[1]
    residual_ref[...] = tokens_ref[...].astype(F32).T.astype(BF16)
    _, rank = route_slots(routes_ref)
    expert_index = lax.broadcasted_iota(jnp.int32, (E, tok_count), 0)
    scale = jnp.zeros((E, tok_count), F32)
    for k in range(routes_ref.shape[0]):
        scale += jnp.where(routes_ref[k : k + 1, :] == expert_index, scale_ref[k : k + 1, :], 0.0)
    slot = lax.broadcasted_iota(jnp.int32, (CAP, tok_count), 0).astype(F32)
    rows = []
    for expert in range(E):
        hit = slot == rank[expert : expert + 1, :]
        rows.append(jnp.where(hit, scale[expert : expert + 1, :], 0.0))
    weighted = jnp.concatenate(rows, axis=0).T
    coarse = weighted.astype(BF16)
    coarse_ref[...] = coarse
    fine_ref[...] = (weighted - coarse.astype(F32)).astype(BF16)


def returns(tokens_t, routes_t, scale_t):
    width, tok_count = tokens_t.shape
    return pl.pallas_call(
        returns_kernel,
        out_shape=(
            jax.ShapeDtypeStruct((tok_count, width), BF16),
            jax.ShapeDtypeStruct((tok_count, E * CAP), BF16),
            jax.ShapeDtypeStruct((tok_count, E * CAP), BF16),
        ),
        in_specs=[VMEM] * 3,
        out_specs=(VMEM,) * 3,
        name="returns",
    )(tokens_t, routes_t, scale_t)


def experts_kernel(rows_ref, gate_up_ref, down_ref, out_ref, total_ref):
    slab = pl.program_id(1)
    blocks, cap, width = rows_ref.shape
    rows = rows_ref[...].reshape(blocks * cap, width)
    projected = jnp.dot(rows, gate_up_ref[...], preferred_element_type=F32)
    gate_part = projected[:, :HALF]
    up_part = projected[:, HALF:]
    hidden = (gate_part * jax.nn.sigmoid(1.702 * gate_part) * (up_part + 1.0)).astype(BF16)
    value = jnp.dot(hidden, down_ref[...], preferred_element_type=F32)

    @pl.when(slab == 0)
    def _():
        total_ref[...] = value

    @pl.when(slab > 0)
    def _():
        total_ref[...] += value

    @pl.when(slab == pl.num_programs(1) - 1)
    def _():
        out_ref[...] = total_ref[...].astype(BF16).reshape(blocks, cap, width)


def run_experts(received, gate_up, down_proj):
    seq_count, experts, cap, width = received.shape
    slabs = gate_up.shape[0] // experts
    rows_spec = pl.BlockSpec((seq_count, None, cap, width), lambda e, k: (0, e, 0, 0))
    return pl.pallas_call(
        experts_kernel,
        out_shape=pltpu.HBM(received.shape, BF16),
        grid=(experts, slabs),
        in_specs=[
            rows_spec,
            pl.BlockSpec((None, width, gate_up.shape[2]), lambda e, k: (e * slabs + k, 0, 0)),
            pl.BlockSpec((None, down_proj.shape[1], width), lambda e, k: (e * slabs + k, 0, 0)),
        ],
        out_specs=rows_spec,
        scratch_shapes=[pltpu.VMEM((seq_count * cap, width), F32)],
        compiler_params=pltpu.CompilerParams(vmem_limit_bytes=48 << 20),
        name="experts",
    )(received, gate_up, down_proj)


def in_hbm(parts):
    return [pltpu.with_memory_space_constraint(part, pltpu.HBM) for part in parts]


def shard_of(place_ref, step, flip, lines):
    line = lax.rem(place_ref[0] - step + lines, lines)
    return line * 2 + (place_ref[1] + flip) % 2


def quarter_of(place_ref, group_flip, pipe_flip):
    return (place_ref[2] + group_flip) % 2 * 2 + (place_ref[3] + pipe_flip) % 2


def qkv_kernel(
    rows, place_ref, tables_ref, residual_ref, coarse_ref, fine_ref, gain_ref, *rest
):
    parts, (packed_ref, hidden_ref, held, slices, sems) = rest[:8], rest[8:]
    lines, _, columns = held.shape[1:]
    copies = []
    for i, part in enumerate(parts):
        copy = pltpu.make_async_copy(part, held.at[i], sems.at[i])
        copy.start()
        copies.append(copy)
    table = tables_ref[...]
    mixed = jnp.dot(coarse_ref[...], table, preferred_element_type=F32)
    mixed += jnp.dot(fine_ref[...], table, preferred_element_type=F32)
    hidden = (residual_ref[...].astype(F32) + mixed).astype(BF16)
    value = hidden.astype(F32)
    hidden_ref[...] = value.T.astype(BF16)
    mean_square = jnp.mean(value * value, axis=-1, keepdims=True)
    normed = value * lax.rsqrt(mean_square + eps) * gain_ref[...]
    slices[...] = jnp.zeros_like(slices)
    for s in range(2 * lines):
        slices[s, :, :rows] = normed[:, s * rows : (s + 1) * rows].astype(BF16)
    for pair in range(4):
        total = jnp.zeros((value.shape[0], columns), F32)
        for flip in range(2):
            copies[pair * 2 + flip].wait()
            for step in range(lines):
                total += jnp.dot(
                    slices[shard_of(place_ref, step, flip, lines)],
                    held[pair * 2 + flip, step],
                    preferred_element_type=F32,
                )
        start = quarter_of(place_ref, pair % 2, pair // 2) * columns
        packed_ref[:, pl.ds(pl.multiple_of(start, 128), columns)] = total.astype(BF16)


def project_qkv(place, tables, residual, coarse, fine, gain, parts, rows, columns):
    tok_count, width = residual.shape
    lines, padded = parts[0].shape[:2]
    return pl.pallas_call(
        functools.partial(qkv_kernel, rows),
        out_shape=(
            jax.ShapeDtypeStruct((tok_count, 4 * columns), BF16),
            jax.ShapeDtypeStruct((width, tok_count), BF16),
        ),
        in_specs=[SMEM] + [VMEM] * 5 + [HBM] * 8,
        out_specs=(VMEM, VMEM),
        scratch_shapes=[
            pltpu.VMEM((8, lines, padded, columns), BF16),
            pltpu.VMEM((2 * lines, tok_count, padded), BF16),
            pltpu.SemaphoreType.DMA((8,)),
        ],
        compiler_params=pltpu.CompilerParams(vmem_limit_bytes=40 << 20),
        name="qkv",
    )(place, tables, residual, coarse, fine, gain, *in_hbm(parts))


def attention_kernel(
    place_ref, sink_ref, packed_ref, halo_ref, hidden_ref, *rest
):
    parts, (out_ref, held, mixed, total_ref, sems) = rest[:8], rest[8:]
    lines, quarter_rows, depth = held.shape[1:]
    copies = []
    for i, part in enumerate(parts):
        copy = pltpu.make_async_copy(part, held.at[i], sems.at[i])
        copy.start()
        copies.append(copy)
    tok_count = packed_ref.shape[0]
    pair_width = 2 * HEAD_SIZE
    query_width = QUERY_HEADS * HEAD_SIZE
    kv_width = KEY_VALUE_HEADS * HEAD_SIZE
    query_groups = QUERY_HEADS // KEY_VALUE_HEADS
    span = halo_ref.shape[0]
    extent = span + tok_count
    query_pos = lax.broadcasted_iota(jnp.int32, (tok_count, extent), 0) + span
    key_pos = lax.broadcasted_iota(jnp.int32, (tok_count, extent), 1)
    distance = query_pos - key_pos
    halo_valid = place_ref[0] + place_ref[1] + place_ref[3] > 0
    first_key = jnp.where(halo_valid, 0, span)
    allowed = (distance >= 0) & (distance < WINDOW_SPAN) & (key_pos >= first_key)
    left = lax.broadcasted_iota(jnp.int32, (extent, pair_width), 1) < HEAD_SIZE
    scale = float(HEAD_SIZE) ** (-0.5)

    def sides(start, head):
        lanes = pl.ds(start + head // 2 * pair_width, pair_width)
        own = packed_ref[:, query_width + start + head // 2 * pair_width :][:, :pair_width]
        both = jnp.concatenate([halo_ref[:, lanes], own], axis=0).astype(F32)
        turned = pltpu.roll(both, HEAD_SIZE, 1)
        low, high = (both, turned) if head % 2 == 0 else (turned, both)
        low = jnp.where(left, low, 0.0).astype(BF16)
        high = jnp.where(left, 0.0, high).astype(BF16)
        return low, high

    pairs = query_groups // 2
    for head in range(KEY_VALUE_HEADS):
        keys, values = sides(0, head), sides(kv_width, head)
        base = head * pairs * pair_width
        stacked = jnp.concatenate(
            [packed_ref[:, base + j * pair_width : base + (j + 1) * pair_width] for j in range(pairs)],
            axis=0,
        )
        outcome = None
        for side in range(2):
            scores = lax.dot_general(
                stacked, keys[side], (((1,), (1,)), ((), ())), preferred_element_type=F32
            )
            probs = []
            for j in range(pairs):
                piece = scores[j * tok_count : (j + 1) * tok_count] * scale
                weights = jnp.where(allowed, jnp.exp(piece), 0.0)
                sink = sink_ref[head * query_groups + 2 * j + side]
                sums = jnp.sum(weights, axis=-1, keepdims=True) + sink
                probs.append((weights / sums).astype(BF16))
            part = jnp.dot(
                jnp.concatenate(probs, axis=0), values[side], preferred_element_type=F32
            )
            outcome = part if outcome is None else outcome + part
        for j in range(pairs):
            column = base + j * pair_width
            mixed[column // depth, :, column % depth : column % depth + pair_width] = outcome[
                j * tok_count : (j + 1) * tok_count
            ].astype(BF16)

    for pair in range(4):
        total = jnp.zeros((quarter_rows, tok_count), F32)
        for flip in range(2):
            copies[pair * 2 + flip].wait()
            for step in range(lines):
                total += lax.dot_general(
                    held[pair * 2 + flip, step],
                    mixed[shard_of(place_ref, step, flip, lines)],
                    (((1,), (1,)), ((), ())),
                    preferred_element_type=F32,
                )
        start = quarter_of(place_ref, pair % 2, pair // 2) * quarter_rows
        total_ref[pl.ds(pl.multiple_of(start, 8), quarter_rows), :] = total
    out_ref[...] = (hidden_ref[...].astype(F32) + total_ref[...]).astype(BF16)


def attend_and_project(place, sinks, packed, halo, hidden_t, parts):
    width, tok_count = hidden_t.shape
    lines, quarter_rows, depth = parts[0].shape
    return pl.pallas_call(
        attention_kernel,
        out_shape=jax.ShapeDtypeStruct((width, tok_count), BF16),
        in_specs=[SMEM] * 2 + [VMEM] * 3 + [HBM] * 8,
        out_specs=VMEM,
        scratch_shapes=[
            pltpu.VMEM((8, lines, quarter_rows, depth), BF16),
            pltpu.VMEM((2 * lines, tok_count, depth), BF16),
            pltpu.VMEM((width, tok_count), F32),
            pltpu.SemaphoreType.DMA((8,)),
        ],
        compiler_params=pltpu.CompilerParams(vmem_limit_bytes=40 << 20),
        name="attention",
    )(place, sinks, packed, halo, hidden_t, *in_hbm(parts))


def place_of():
    seq_index = lax.axis_index("seq")
    return jnp.stack(
        [seq_index // 2, seq_index % 2, lax.axis_index("groups") % 2, lax.axis_index("pipe")]
    ).astype(jnp.int32)


def own_quarters(qkv_proj, out_proj):
    rows, qkv_width = qkv_proj.shape
    quarter = lax.axis_index("groups") % 2 * 2 + lax.axis_index("pipe")
    qw, ow = qkv_width // 4, out_proj.shape[1] // 4
    mine_qkv = lax.dynamic_slice_in_dim(qkv_proj, quarter * qw, qw, 1)
    mine_out = lax.dynamic_slice_in_dim(out_proj.T, quarter * ow, ow, 0)
    return jnp.pad(mine_qkv, ((0, -rows % 8), (0, 0))), mine_out


def along_lines(block, seq_count):
    blocks = [block]
    for k in range(1, seq_count // 2):
        pairs = [(i, (i + 2 * k) % seq_count) for i in range(seq_count)]
        blocks.append(lax.ppermute(block, "seq", pairs))
    return blocks


def fused_body(
    tokens, routes, route_weights, moe_gain, gate_up, down_proj, attn_gain, qkv_proj, sinks, out_proj
):
    seq_count = lax.axis_size("seq")
    tok_count, width = tokens.shape[1:]
    per_device = gate_up.shape[0]
    rows, qkv_width = qkv_proj.shape
    tokens_t, routes_t, scale_t = tokens[0].T, routes[0].T, route_weights[0].T
    mine_qkv, mine_out = own_quarters(qkv_proj, out_proj)
    qkv_lines = along_lines(mine_qkv, seq_count)

    table = dispatch(tokens_t, routes_t, moe_gain.reshape(1, width))
    outgoing = table.reshape(seq_count, per_device // 2, CAP, width)
    received = lax.all_to_all(outgoing, "seq", split_axis=0, concat_axis=0, tiled=True)

    qkv_lines, mine_out = lax.optimization_barrier((qkv_lines, mine_out))
    qkv_own = jnp.stack(qkv_lines)
    qkv_mate = swapped(qkv_own, "seq")
    out_lines = along_lines(mine_out, seq_count)
    qkv_parts = [qkv_own, qkv_mate, swapped(qkv_own, "groups"), swapped(qkv_mate, "groups")]
    residual, coarse, fine = returns(tokens_t, routes_t, scale_t)
    received, residual, coarse, fine = lax.optimization_barrier((received, residual, coarse, fine))

    finished = run_experts(received, gate_up, down_proj)
    out_own = jnp.stack(out_lines)
    out_mate = swapped(out_own, "seq")
    summed = lax.all_to_all(finished, "seq", split_axis=0, concat_axis=0, tiled=True)
    qkv_parts += [swapped(part, "pipe") for part in qkv_parts]
    out_parts = [out_own, out_mate, swapped(out_own, "groups"), swapped(out_mate, "groups")]
    out_parts += [swapped(part, "pipe") for part in out_parts]

    summed = summed.reshape(E * CAP, width)
    place = place_of()
    packed, hidden_t = project_qkv(
        place, summed, residual, coarse, fine, attn_gain.reshape(1, width), qkv_parts, rows, qkv_width // 4
    )
    query_width = QUERY_HEADS * HEAD_SIZE
    halo = halo_exchange(packed[tok_count - WINDOW_SPAN :, query_width:])
    out_t = attend_and_project(place, jnp.exp(sinks), packed, halo, hidden_t, out_parts)
    return out_t.T[None]


def swapped(value, axis):
    return lax.ppermute(value, axis, [(i, i ^ 1) for i in range(lax.axis_size(axis))])


def rms_scale(value_matrix, gain):
    widened = value_matrix.astype(jnp.float32)
    mean_square = jnp.mean(widened * widened, axis=-1, keepdims=True)
    return (widened * lax.rsqrt(mean_square + eps) * gain).astype(jnp.bfloat16)


def routing_tables(route_rows, route_scale):
    tok_count = route_rows.shape[0]
    experts = jnp.arange(E, dtype=jnp.int32)
    named = route_rows[None, :, :] == experts[:, None, None]
    member = jnp.any(named, axis=2)
    scale = jnp.sum(jnp.where(named, route_scale[None, :, :], 0.0), axis=2)
    token = jnp.arange(tok_count, dtype=jnp.int32)
    before = (token[:, None] < token[None, :]).astype(jnp.bfloat16)
    rank = jnp.dot(member.astype(jnp.bfloat16), before, preferred_element_type=jnp.float32)
    slot = jnp.arange(CAP, dtype=jnp.float32)
    chosen = member[:, None, :] & (rank[:, None, :] == slot[None, :, None])
    select = chosen.reshape(E * CAP, tok_count).astype(jnp.bfloat16)
    weighted = jnp.where(chosen, scale[:, None, :], 0.0).reshape(E * CAP, tok_count)
    return select, weighted


def neighbour_relay(block, seq_count):
    rounds = seq_count // 2
    up = [(i, i + 2) for i in range(seq_count - 2)]
    down = [(i + 2, i) for i in range(seq_count - 2)]
    rising, falling = [block], [block]
    for _ in range(rounds - 1):
        rising.append(lax.ppermute(rising[-1], "seq", up))
        falling.append(lax.ppermute(falling[-1], "seq", down))
    line = lax.axis_index("seq") // 2
    blocks = [block]
    for k in range(1, rounds):
        blocks.append(jnp.where(line >= k, rising[k], falling[rounds - k]))
    return blocks


def gather_weights(qkv_proj, out_proj):
    seq_count = lax.axis_size("seq")
    rows, qkv_width = qkv_proj.shape
    depth, width = out_proj.shape
    group_bit = lax.axis_index("groups") % 2
    pipe_bit = lax.axis_index("pipe")
    quarter = group_bit * 2 + pipe_bit
    qw, ow = qkv_width // 4, width // 4
    fold = ow // rows
    mine_qkv = lax.dynamic_slice_in_dim(qkv_proj, quarter * qw, qw, 1)
    mine_out = lax.dynamic_slice_in_dim(out_proj.T, quarter * ow, ow, 0)
    block = jnp.concatenate(
        [mine_qkv] + [mine_out[i * rows : (i + 1) * rows] for i in range(fold)], axis=1
    )
    blocks = neighbour_relay(block, seq_count)
    lines = seq_count // 2
    line = lax.axis_index("seq") // 2
    stacked = jnp.stack(blocks)
    column = jnp.stack(
        [lax.dynamic_index_in_dim(stacked, (line - j) % lines, 0, keepdims=False) for j in range(lines)]
    )
    other = swapped(column, "seq")
    odd = lax.axis_index("seq") % 2 == 1
    both = jnp.stack([jnp.where(odd, other, column), jnp.where(odd, column, other)], axis=1)
    both = both.reshape(seq_count, rows, block.shape[1])
    across = swapped(both, "groups")
    high = group_bit == 1
    halves = jnp.stack([jnp.where(high, across, both), jnp.where(high, both, across)])
    beside = swapped(halves, "pipe")
    second = pipe_bit == 1
    whole = jnp.stack([jnp.where(second, beside, halves), jnp.where(second, halves, beside)], axis=1)
    whole = whole.reshape(4, seq_count, rows, block.shape[1])
    qkv_full = whole[..., :qw].transpose(1, 2, 0, 3).reshape(seq_count * rows, qkv_width)
    out_full = whole[..., qw:].reshape(4, seq_count, rows, fold, depth)
    out_full = out_full.transpose(1, 4, 0, 3, 2).reshape(seq_count * depth, width)
    return qkv_full, out_full


def expert_layer(local, route_rows, route_scale, moe_gain, gate_up, down_proj):
    _, width = local.shape
    seq_count = lax.axis_size("seq")
    per_device = gate_up.shape[0]
    normed = rms_scale(local, moe_gain)
    select, weighted = routing_tables(route_rows, route_scale)
    table = jnp.dot(select, normed, preferred_element_type=jnp.float32).astype(jnp.bfloat16)
    by_expert = table.reshape(E, CAP, width)
    experts = max(1, per_device // 2)
    slabs = per_device // experts
    if slabs == 1:
        by_expert = jnp.repeat(by_expert, 2, axis=0)
    outgoing = by_expert.reshape(seq_count, experts, CAP, width)
    received = lax.all_to_all(outgoing, "seq", split_axis=0, concat_axis=0, tiled=True)
    rows = received.transpose(1, 0, 2, 3).reshape(experts, seq_count * CAP, width)
    gate_up = gate_up.reshape(experts, slabs, width, 2 * HALF)
    down_proj = down_proj.reshape(experts, slabs, HALF, width)
    projected = jnp.einsum("erd,ekdh->ekrh", rows, gate_up, preferred_element_type=jnp.float32)
    gate_part = projected[..., :HALF]
    up_part = projected[..., HALF:]
    hidden = (gate_part * jax.nn.sigmoid(1.702 * gate_part) * (up_part + 1.0)).astype(jnp.bfloat16)
    partial_value = jnp.einsum(
        "ekrh,ekhd->erd", hidden, down_proj, preferred_element_type=jnp.float32
    ).reshape(experts, seq_count, CAP, width)
    partial_value = partial_value.transpose(1, 0, 2, 3)
    if slabs == 2:
        finished = partial_value.astype(jnp.bfloat16)
    else:
        first = lax.axis_index("seq") % 2 == 0
        lower_rows = partial_value[:, :, : CAP // 2]
        upper_rows = partial_value[:, :, CAP // 2 :]
        kept = jnp.where(first, lower_rows, upper_rows)
        given = jnp.where(first, upper_rows, lower_rows)
        partner_part = swapped(given.astype(jnp.bfloat16), "seq").astype(given.dtype)
        finished = (kept + partner_part).astype(jnp.bfloat16)
    summed = lax.all_to_all(finished, "seq", split_axis=0, concat_axis=0, tiled=True).reshape(
        E * CAP, width
    )
    coarse = weighted.astype(jnp.bfloat16)
    fine = (weighted - coarse.astype(jnp.float32)).astype(jnp.bfloat16)
    dims = (((0,), (0,)), ((), ()))
    mixed = lax.dot_general(coarse, summed, dims, preferred_element_type=jnp.float32)
    mixed += lax.dot_general(fine, summed, dims, preferred_element_type=jnp.float32)
    return (local.astype(jnp.float32) + mixed).astype(jnp.bfloat16)


def attend(query_matrix, keys_extended, values_extended, head_sink_logits, halo_valid):
    tok_count = query_matrix.shape[0]
    query_groups = QUERY_HEADS // KEY_VALUE_HEADS
    scale = float(HEAD_SIZE) ** (-0.5)
    sink_mass_total = jnp.exp(head_sink_logits).reshape(KEY_VALUE_HEADS, query_groups, 1, 1)
    block_queries = query_matrix.reshape(tok_count, KEY_VALUE_HEADS, query_groups, HEAD_SIZE)
    block_keys = keys_extended.reshape(tok_count + WINDOW_SPAN, KEY_VALUE_HEADS, HEAD_SIZE)
    block_values = values_extended.reshape(tok_count + WINDOW_SPAN, KEY_VALUE_HEADS, HEAD_SIZE)
    scores = (
        jnp.einsum("qhgd,khd->hgqk", block_queries, block_keys, preferred_element_type=jnp.float32)
        * scale
    )
    query_pos = jnp.arange(tok_count, dtype=jnp.int32)[:, None] + WINDOW_SPAN
    key_pos = jnp.arange(tok_count + WINDOW_SPAN, dtype=jnp.int32)[None, :]
    distance = query_pos - key_pos
    allowed = (distance >= 0) & (distance < WINDOW_SPAN) & ((key_pos >= WINDOW_SPAN) | halo_valid)
    weights = jnp.where(allowed, jnp.exp(scores), 0.0)
    probs = (weights / (jnp.sum(weights, axis=-1, keepdims=True) + sink_mass_total)).astype(
        jnp.bfloat16
    )
    mixed = jnp.einsum("hgqk,khd->qhgd", probs, block_values, preferred_element_type=jnp.float32)
    return mixed.reshape(tok_count, QUERY_HEADS * HEAD_SIZE).astype(jnp.bfloat16)


def halo_exchange(pairs):
    seq_count, pipe_count = lax.axis_size("seq"), lax.axis_size("pipe")
    order = [s * pipe_count + p for p in range(pipe_count) for s in range(seq_count)]
    return lax.ppermute(pairs, ("seq", "pipe"), list(zip(order[:-1], order[1:])))


def body(
    tokens,
    routes,
    route_weights,
    moe_gain,
    gate_up,
    down_proj,
    attn_gain,
    qkv_proj,
    head_sink_logits,
    out_proj,
):
    if gate_up.shape[0] % 2 == 0 and out_proj.shape[0] % 128 == 0 and tokens.shape[1] == WINDOW_SPAN:
        return fused_body(
            tokens,
            routes,
            route_weights,
            moe_gain,
            gate_up,
            down_proj,
            attn_gain,
            qkv_proj,
            head_sink_logits,
            out_proj,
        )
    qkv_full, out_full = gather_weights(qkv_proj, out_proj)
    hidden = expert_layer(tokens[0], routes[0], route_weights[0], moe_gain, gate_up, down_proj)
    tok_count, _ = hidden.shape
    normed = rms_scale(hidden, attn_gain)
    seq_index = lax.axis_index("seq")
    pipe_index = lax.axis_index("pipe")
    halo_valid = (seq_index > 0) | (pipe_index > 0)
    query_width = QUERY_HEADS * HEAD_SIZE
    width_of_pair = KEY_VALUE_HEADS * HEAD_SIZE
    packed_heads = jnp.dot(normed, qkv_full, preferred_element_type=jnp.float32).astype(
        jnp.bfloat16
    )
    own_pairs = packed_heads[:, query_width:]
    halo_pairs = halo_exchange(own_pairs[tok_count - WINDOW_SPAN :])
    query_matrix = packed_heads[:, :query_width]
    pairs_ext = jnp.concatenate([halo_pairs, own_pairs], axis=0)
    keys_extended = pairs_ext[:, :width_of_pair]
    values_extended = pairs_ext[:, width_of_pair:]
    attended = attend(query_matrix, keys_extended, values_extended, head_sink_logits, halo_valid)
    projected = jnp.dot(attended, out_full, preferred_element_type=jnp.float32)
    return (hidden.astype(jnp.float32) + projected).astype(jnp.bfloat16)[None]


def solution(mesh):
    in_specs = (
        P("pipe", ("groups", "seq"), None),
        P("pipe", ("groups", "seq"), None),
        P("pipe", ("groups", "seq"), None),
        P(),
        P("seq", None, None),
        P("seq", None, None),
        P(),
        P("seq", None),
        P(),
        P("seq", None),
    )
    out_specs = P("pipe", ("groups", "seq"), None)
    return jax.shard_map(body, mesh=mesh, in_specs=in_specs, out_specs=out_specs, check_vma=False)
```

```python
import functools

import jax
import jax.numpy as jnp
from jax import lax
from jax.experimental import pallas as pl
from jax.experimental.pallas import tpu as pltpu
from jax.sharding import PartitionSpec as P


E = 16
QUERY_HEADS = 32
KEY_VALUE_HEADS = 4
HEAD_SIZE = 64
WINDOW_SPAN = 128
HALF = 720
CAP = 48


eps = 1e-05


F32 = jnp.float32
BF16 = jnp.bfloat16
VMEM = pl.BlockSpec(memory_space=pltpu.VMEM)
SMEM = pl.BlockSpec(memory_space=pltpu.SMEM)
HBM = pl.BlockSpec(memory_space=pltpu.HBM)


def route_slots(routes_ref):
    tok_count = routes_ref.shape[1]
    expert = lax.broadcasted_iota(jnp.int32, (E, tok_count), 0)
    member = jnp.zeros((E, tok_count), jnp.bool_)
    for k in range(routes_ref.shape[0]):
        member = member | (routes_ref[k : k + 1, :] == expert)
    first = lax.broadcasted_iota(jnp.int32, (tok_count, tok_count), 0)
    second = lax.broadcasted_iota(jnp.int32, (tok_count, tok_count), 1)
    before = jnp.where(first < second, 1.0, 0.0).astype(BF16)
    flags = jnp.where(member, 1.0, 0.0)
    rank = jnp.dot(flags.astype(BF16), before, preferred_element_type=F32)
    return flags, jnp.where(flags > 0.0, rank, -1.0)


def slot_lanes(width):
    spare = -width % 128
    return spare if spare >= E else spare + 128


def prepare_kernel(tokens_ref, routes_ref, gain_ref, block_ref):
    width, tok_count = tokens_ref.shape
    value = tokens_ref[...].astype(F32).T
    mean_square = jnp.mean(value * value, axis=-1, keepdims=True)
    normed = value * lax.rsqrt(mean_square + eps) * gain_ref[...][None, :]
    block_ref[:, :width] = normed.astype(BF16)
    _, rank = route_slots(routes_ref)
    spare = block_ref.shape[1] - width
    unused = jnp.full((spare - E, tok_count), -1.0, F32)
    block_ref[:, width:] = jnp.concatenate([rank, unused], axis=0).T.astype(BF16)


def prepare(tokens_t, routes_t, gain):
    width, tok_count = tokens_t.shape
    return pl.pallas_call(
        prepare_kernel,
        out_shape=jax.ShapeDtypeStruct((tok_count, width + slot_lanes(width)), BF16),
        in_specs=[VMEM] * 3,
        out_specs=VMEM,
        name="prepare",
    )(tokens_t, routes_t, gain)


def returns_kernel(tokens_ref, routes_ref, scale_ref, residual_ref, coarse_ref, fine_ref):
    tok_count = tokens_ref.shape[1]
    residual_ref[...] = tokens_ref[...].astype(F32).T.astype(BF16)
    _, rank = route_slots(routes_ref)
    expert_index = lax.broadcasted_iota(jnp.int32, (E, tok_count), 0)
    scale = jnp.zeros((E, tok_count), F32)
    for k in range(routes_ref.shape[0]):
        scale += jnp.where(routes_ref[k : k + 1, :] == expert_index, scale_ref[k : k + 1, :], 0.0)
    slot = lax.broadcasted_iota(jnp.int32, (CAP, tok_count), 0).astype(F32)
    rows = []
    for expert in range(E):
        hit = slot == rank[expert : expert + 1, :]
        rows.append(jnp.where(hit, scale[expert : expert + 1, :], 0.0))
    weighted = jnp.concatenate(rows, axis=0).T
    coarse = weighted.astype(BF16)
    coarse_ref[...] = coarse
    fine_ref[...] = (weighted - coarse.astype(F32)).astype(BF16)


def returns(tokens_t, routes_t, scale_t):
    width, tok_count = tokens_t.shape
    return pl.pallas_call(
        returns_kernel,
        out_shape=(
            jax.ShapeDtypeStruct((tok_count, width), BF16),
            jax.ShapeDtypeStruct((tok_count, E * CAP), BF16),
            jax.ShapeDtypeStruct((tok_count, E * CAP), BF16),
        ),
        in_specs=[VMEM] * 3,
        out_specs=(VMEM,) * 3,
        name="returns",
    )(tokens_t, routes_t, scale_t)


def experts_kernel(lines, place_ref, *refs):
    blocks = refs[: 2 * lines]
    gate_up_ref, down_ref, out_ref, picked, slots, total_ref = refs[2 * lines :]
    expert, slab = pl.program_id(0), pl.program_id(1)
    experts, _, width = picked.shape
    tok_count, _ = blocks[0].shape

    @pl.when((expert == 0) & (slab == 0))
    def _():
        place = shard_of(place_ref, 0, 0, lines) * experts
        slot = lax.broadcasted_iota(jnp.int32, (CAP, tok_count), 0).astype(F32)
        for i, block in enumerate(blocks):
            slots[i] = block[:, width:].astype(F32).T
            select = [slot == slots[i, pl.ds(place + e, 1), :] for e in range(experts)]
            select = jnp.where(jnp.concatenate(select, axis=0), 1.0, 0.0).astype(BF16)
            rows = jnp.dot(select, block[:, :width], preferred_element_type=F32).astype(BF16)
            for e in range(experts):
                picked[e, i * CAP : (i + 1) * CAP, :] = rows[e * CAP : (e + 1) * CAP]

    projected = jnp.dot(picked[expert], gate_up_ref[...], preferred_element_type=F32)
    gate_part = projected[:, :HALF]
    up_part = projected[:, HALF:]
    hidden = (gate_part * jax.nn.sigmoid(1.702 * gate_part) * (up_part + 1.0)).astype(BF16)
    value = jnp.dot(hidden, down_ref[...], preferred_element_type=F32)

    @pl.when(slab == 0)
    def _():
        total_ref[...] = value

    @pl.when(slab > 0)
    def _():
        total_ref[...] += value

    @pl.when(slab == pl.num_programs(1) - 1)
    def _():
        for i in range(2 * lines):
            owner = shard_of(place_ref, i // 2, i % 2, lines)
            out_ref[owner] = total_ref[i * CAP : (i + 1) * CAP].astype(BF16)


def run_experts(place, blocks, gate_up, down_proj):
    seq_count = len(blocks)
    tok_count, sent = blocks[0].shape
    per_device, width, gate_width = gate_up.shape
    slabs = 2
    experts = per_device // slabs
    return pl.pallas_call(
        functools.partial(experts_kernel, seq_count // 2),
        out_shape=pltpu.HBM((seq_count, experts, CAP, width), BF16),
        grid=(experts, slabs),
        in_specs=[SMEM]
        + [pl.BlockSpec((tok_count, sent), lambda e, k: (0, 0))] * seq_count
        + [
            pl.BlockSpec((None, width, gate_width), lambda e, k: (e * slabs + k, 0, 0)),
            pl.BlockSpec((None, down_proj.shape[1], width), lambda e, k: (e * slabs + k, 0, 0)),
        ],
        out_specs=pl.BlockSpec((seq_count, None, CAP, width), lambda e, k: (0, e, 0, 0)),
        scratch_shapes=[
            pltpu.VMEM((experts, seq_count * CAP, width), BF16),
            pltpu.VMEM((seq_count, sent - width, tok_count), F32),
            pltpu.VMEM((seq_count * CAP, width), F32),
        ],
        compiler_params=pltpu.CompilerParams(vmem_limit_bytes=48 << 20),
        name="experts",
    )(place, *blocks, gate_up, down_proj)


def in_hbm(parts):
    return [pltpu.with_memory_space_constraint(part, pltpu.HBM) for part in parts]


def start_copies(parts, held, sems):
    half = held.shape[1] // 2
    copies = []
    for i, part in enumerate(parts):
        target = held.at[i // 2, pl.ds(i % 2 * half, half)]
        copy = pltpu.make_async_copy(part, target, sems.at[i])
        copy.start()
        copies.append(copy)
    return [copies[i : i + 2] for i in range(0, len(copies), 2)]


def block_step(slot, lines):
    half = lines // 2
    return slot % half * 2 + slot // half


def shard_of(place_ref, step, flip, lines):
    line, bit = 0, 1
    while bit < lines:
        line += (place_ref[0] // bit + step // bit) % 2 * bit
        bit *= 2
    return line * 2 + (place_ref[1] + flip) % 2


def quarter_of(place_ref, group_flip, pipe_flip):
    return (place_ref[2] + group_flip) % 2 * 2 + (place_ref[3] + pipe_flip) % 2


def qkv_kernel(
    rows, place_ref, tables_ref, residual_ref, coarse_ref, fine_ref, gain_ref, *rest
):
    parts, (packed_ref, hidden_ref, held, slices, sems) = rest[:16], rest[16:]
    lines, _, columns = held.shape[1:]
    copies = start_copies(parts, held, sems)
    table = tables_ref[...]
    mixed = jnp.dot(coarse_ref[...], table, preferred_element_type=F32)
    mixed += jnp.dot(fine_ref[...], table, preferred_element_type=F32)
    hidden = (residual_ref[...].astype(F32) + mixed).astype(BF16)
    value = hidden.astype(F32)
    hidden_ref[...] = value.T.astype(BF16)
    mean_square = jnp.mean(value * value, axis=-1, keepdims=True)
    normed = value * lax.rsqrt(mean_square + eps) * gain_ref[...][None, :]
    slices[...] = jnp.zeros_like(slices)
    for s in range(2 * lines):
        slices[s, :, :rows] = normed[:, s * rows : (s + 1) * rows].astype(BF16)
    for pair in range(4):
        total = jnp.zeros((value.shape[0], columns), F32)
        for flip in range(2):
            for copy in copies[pair * 2 + flip]:
                copy.wait()
            for step in range(lines):
                total += jnp.dot(
                    slices[shard_of(place_ref, block_step(step, lines), flip, lines)],
                    held[pair * 2 + flip, step],
                    preferred_element_type=F32,
                )
        start = quarter_of(place_ref, pair % 2, pair // 2) * columns
        packed_ref[:, pl.ds(pl.multiple_of(start, 128), columns)] = total.astype(BF16)


def project_qkv(place, tables, residual, coarse, fine, gain, parts, rows, columns):
    tok_count, width = residual.shape
    lines, padded = 2 * parts[0].shape[0], parts[0].shape[1]
    return pl.pallas_call(
        functools.partial(qkv_kernel, rows),
        out_shape=(
            jax.ShapeDtypeStruct((tok_count, 4 * columns), BF16),
            jax.ShapeDtypeStruct((width, tok_count), BF16),
        ),
        in_specs=[SMEM] + [VMEM] * 5 + [HBM] * 16,
        out_specs=(VMEM, VMEM),
        scratch_shapes=[
            pltpu.VMEM((8, lines, padded, columns), BF16),
            pltpu.VMEM((2 * lines, tok_count, padded), BF16),
            pltpu.SemaphoreType.DMA((16,)),
        ],
        compiler_params=pltpu.CompilerParams(vmem_limit_bytes=40 << 20),
        name="qkv",
    )(place, tables, residual, coarse, fine, gain, *in_hbm(parts))


def attention_kernel(
    place_ref, sink_ref, packed_ref, halo_ref, hidden_ref, *rest
):
    parts, (out_ref, held, mixed, total_ref, sems) = rest[:16], rest[16:]
    lines, quarter_rows, depth = held.shape[1:]
    copies = start_copies(parts, held, sems)
    tok_count = packed_ref.shape[0]
    pair_width = 2 * HEAD_SIZE
    query_width = QUERY_HEADS * HEAD_SIZE
    kv_width = KEY_VALUE_HEADS * HEAD_SIZE
    query_groups = QUERY_HEADS // KEY_VALUE_HEADS
    span = halo_ref.shape[0]
    extent = span + tok_count
    query_pos = lax.broadcasted_iota(jnp.int32, (tok_count, extent), 0) + span
    key_pos = lax.broadcasted_iota(jnp.int32, (tok_count, extent), 1)
    distance = query_pos - key_pos
    halo_valid = place_ref[0] + place_ref[1] + place_ref[3] > 0
    first_key = jnp.where(halo_valid, 0, span)
    allowed = (distance >= 0) & (distance < WINDOW_SPAN) & (key_pos >= first_key)
    left = lax.broadcasted_iota(jnp.int32, (extent, pair_width), 1) < HEAD_SIZE
    scale = float(HEAD_SIZE) ** (-0.5)

    def sides(start, head):
        lanes = pl.ds(start + head // 2 * pair_width, pair_width)
        own = packed_ref[:, query_width + start + head // 2 * pair_width :][:, :pair_width]
        both = jnp.concatenate([halo_ref[:, lanes], own], axis=0).astype(F32)
        turned = pltpu.roll(both, HEAD_SIZE, 1)
        low, high = (both, turned) if head % 2 == 0 else (turned, both)
        low = jnp.where(left, low, 0.0).astype(BF16)
        high = jnp.where(left, 0.0, high).astype(BF16)
        return low, high

    pairs = query_groups // 2
    for head in range(KEY_VALUE_HEADS):
        keys, values = sides(0, head), sides(kv_width, head)
        base = head * pairs * pair_width
        stacked = jnp.concatenate(
            [packed_ref[:, base + j * pair_width : base + (j + 1) * pair_width] for j in range(pairs)],
            axis=0,
        )
        outcome = None
        for side in range(2):
            scores = lax.dot_general(
                stacked, keys[side], (((1,), (1,)), ((), ())), preferred_element_type=F32
            )
            probs = []
            for j in range(pairs):
                piece = scores[j * tok_count : (j + 1) * tok_count] * scale
                weights = jnp.where(allowed, jnp.exp(piece), 0.0)
                sink = sink_ref[head * query_groups + 2 * j + side]
                sums = jnp.sum(weights, axis=-1, keepdims=True) + sink
                probs.append((weights / sums).astype(BF16))
            part = jnp.dot(
                jnp.concatenate(probs, axis=0), values[side], preferred_element_type=F32
            )
            outcome = part if outcome is None else outcome + part
        for j in range(pairs):
            column = base + j * pair_width
            mixed[column // depth, :, column % depth : column % depth + pair_width] = outcome[
                j * tok_count : (j + 1) * tok_count
            ].astype(BF16)

    for pair in range(4):
        total = jnp.zeros((quarter_rows, tok_count), F32)
        for flip in range(2):
            for copy in copies[pair * 2 + flip]:
                copy.wait()
            for step in range(lines):
                total += lax.dot_general(
                    held[pair * 2 + flip, step],
                    mixed[shard_of(place_ref, block_step(step, lines), flip, lines)],
                    (((1,), (1,)), ((), ())),
                    preferred_element_type=F32,
                )
        start = quarter_of(place_ref, pair % 2, pair // 2) * quarter_rows
        total_ref[pl.ds(pl.multiple_of(start, 8), quarter_rows), :] = total
    out_ref[...] = (hidden_ref[...].astype(F32) + total_ref[...]).astype(BF16)


def attend_and_project(place, sinks, packed, halo, hidden_t, parts):
    width, tok_count = hidden_t.shape
    half, quarter_rows, depth = parts[0].shape
    lines = 2 * half
    return pl.pallas_call(
        attention_kernel,
        out_shape=jax.ShapeDtypeStruct((width, tok_count), BF16),
        in_specs=[SMEM] * 2 + [VMEM] * 3 + [HBM] * 16,
        out_specs=VMEM,
        scratch_shapes=[
            pltpu.VMEM((8, lines, quarter_rows, depth), BF16),
            pltpu.VMEM((2 * lines, tok_count, depth), BF16),
            pltpu.VMEM((width, tok_count), F32),
            pltpu.SemaphoreType.DMA((16,)),
        ],
        compiler_params=pltpu.CompilerParams(vmem_limit_bytes=40 << 20),
        name="attention",
    )(place, sinks, packed, halo, hidden_t, *in_hbm(parts))


def place_of():
    seq_index = lax.axis_index("seq")
    return jnp.stack(
        [seq_index // 2, seq_index % 2, lax.axis_index("groups") % 2, lax.axis_index("pipe")]
    ).astype(jnp.int32)


def own_quarters(qkv_proj, out_proj):
    rows, qkv_width = qkv_proj.shape
    quarter = lax.axis_index("groups") % 2 * 2 + lax.axis_index("pipe")
    qw, ow = qkv_width // 4, out_proj.shape[1] // 4
    mine_qkv = lax.dynamic_slice_in_dim(qkv_proj, quarter * qw, qw, 1)
    mine_out = lax.dynamic_slice_in_dim(out_proj.T, quarter * ow, ow, 0)
    return jnp.pad(mine_qkv, ((0, -rows % 8), (0, 0))), mine_out


def flipped(value, bit):
    count = lax.axis_size("seq")
    return lax.ppermute(value, "seq", [(i, i ^ bit * 2) for i in range(count)])


def far_blocks(block, lines):
    bit = lines // 2
    found = {0: block}
    while bit > 1:
        for step in list(found):
            found[step + bit] = flipped(found[step], bit)
        bit //= 2
    return [found[step] for step in range(0, lines, 2)]


def gather_quarters(mine, lines):
    even = jnp.stack(far_blocks(mine, lines))
    odd = flipped(even, 1)
    parts = []
    even_mate, even_across = swapped(even, "seq"), swapped(even, "groups")
    odd_mate, odd_across = swapped(odd, "seq"), swapped(odd, "groups")
    even_last = swapped(even_mate, "groups")
    odd_last = swapped(odd_mate, "groups")
    parts = [even, odd, even_mate, odd_mate, even_across, odd_across, even_last, odd_last]
    beside = []
    for part in parts:
        beside.append(swapped(part, "pipe"))
    return parts + beside


def fused_body(
    tokens, routes, route_weights, moe_gain, gate_up, down_proj, attn_gain, qkv_proj, sinks, out_proj
):
    seq_count = lax.axis_size("seq")
    tok_count, width = tokens.shape[1:]
    rows, qkv_width = qkv_proj.shape
    tokens_t, routes_t, scale_t = tokens[0].T, routes[0].T, route_weights[0].T
    place = place_of()

    block = prepare(tokens_t, routes_t, moe_gain)
    lines = seq_count // 2
    evens = far_blocks(block, lines)
    blocks = []
    for even in evens:
        odd = flipped(even, 1)
        for value in (even, odd):
            blocks += [value, swapped(value, "seq")]
    mine_qkv, mine_out = own_quarters(qkv_proj, out_proj)
    qkv_parts = gather_quarters(mine_qkv, lines)
    out_parts = gather_quarters(mine_out, lines)

    finished = run_experts(place, blocks, gate_up, down_proj)
    summed = lax.all_to_all(finished, "seq", split_axis=0, concat_axis=0, tiled=True)
    residual, coarse, fine = returns(tokens_t, routes_t, scale_t)

    summed = summed.reshape(E * CAP, width)
    packed, hidden_t = project_qkv(
        place, summed, residual, coarse, fine, attn_gain, qkv_parts, rows, qkv_width // 4
    )
    query_width = QUERY_HEADS * HEAD_SIZE
    halo = halo_exchange(packed[tok_count - WINDOW_SPAN :, query_width:])
    out_t = attend_and_project(place, jnp.exp(sinks), packed, halo, hidden_t, out_parts)
    return out_t.T[None]


def swapped(value, axis):
    return lax.ppermute(value, axis, [(i, i ^ 1) for i in range(lax.axis_size(axis))])


def rms_scale(value_matrix, gain):
    widened = value_matrix.astype(jnp.float32)
    mean_square = jnp.mean(widened * widened, axis=-1, keepdims=True)
    return (widened * lax.rsqrt(mean_square + eps) * gain).astype(jnp.bfloat16)


def routing_tables(route_rows, route_scale):
    tok_count = route_rows.shape[0]
    experts = jnp.arange(E, dtype=jnp.int32)
    named = route_rows[None, :, :] == experts[:, None, None]
    member = jnp.any(named, axis=2)
    scale = jnp.sum(jnp.where(named, route_scale[None, :, :], 0.0), axis=2)
    token = jnp.arange(tok_count, dtype=jnp.int32)
    before = (token[:, None] < token[None, :]).astype(jnp.bfloat16)
    rank = jnp.dot(member.astype(jnp.bfloat16), before, preferred_element_type=jnp.float32)
    slot = jnp.arange(CAP, dtype=jnp.float32)
    chosen = member[:, None, :] & (rank[:, None, :] == slot[None, :, None])
    select = chosen.reshape(E * CAP, tok_count).astype(jnp.bfloat16)
    weighted = jnp.where(chosen, scale[:, None, :], 0.0).reshape(E * CAP, tok_count)
    return select, weighted


def neighbour_relay(block, seq_count):
    rounds = seq_count // 2
    up = [(i, i + 2) for i in range(seq_count - 2)]
    down = [(i + 2, i) for i in range(seq_count - 2)]
    rising, falling = [block], [block]
    for _ in range(rounds - 1):
        rising.append(lax.ppermute(rising[-1], "seq", up))
        falling.append(lax.ppermute(falling[-1], "seq", down))
    line = lax.axis_index("seq") // 2
    blocks = [block]
    for k in range(1, rounds):
        blocks.append(jnp.where(line >= k, rising[k], falling[rounds - k]))
    return blocks


def gather_weights(qkv_proj, out_proj):
    seq_count = lax.axis_size("seq")
    rows, qkv_width = qkv_proj.shape
    depth, width = out_proj.shape
    group_bit = lax.axis_index("groups") % 2
    pipe_bit = lax.axis_index("pipe")
    quarter = group_bit * 2 + pipe_bit
    qw, ow = qkv_width // 4, width // 4
    fold = ow // rows
    mine_qkv = lax.dynamic_slice_in_dim(qkv_proj, quarter * qw, qw, 1)
    mine_out = lax.dynamic_slice_in_dim(out_proj.T, quarter * ow, ow, 0)
    block = jnp.concatenate(
        [mine_qkv] + [mine_out[i * rows : (i + 1) * rows] for i in range(fold)], axis=1
    )
    blocks = neighbour_relay(block, seq_count)
    lines = seq_count // 2
    line = lax.axis_index("seq") // 2
    stacked = jnp.stack(blocks)
    column = jnp.stack(
        [lax.dynamic_index_in_dim(stacked, (line - j) % lines, 0, keepdims=False) for j in range(lines)]
    )
    other = swapped(column, "seq")
    odd = lax.axis_index("seq") % 2 == 1
    both = jnp.stack([jnp.where(odd, other, column), jnp.where(odd, column, other)], axis=1)
    both = both.reshape(seq_count, rows, block.shape[1])
    across = swapped(both, "groups")
    high = group_bit == 1
    halves = jnp.stack([jnp.where(high, across, both), jnp.where(high, both, across)])
    beside = swapped(halves, "pipe")
    second = pipe_bit == 1
    whole = jnp.stack([jnp.where(second, beside, halves), jnp.where(second, halves, beside)], axis=1)
    whole = whole.reshape(4, seq_count, rows, block.shape[1])
    qkv_full = whole[..., :qw].transpose(1, 2, 0, 3).reshape(seq_count * rows, qkv_width)
    out_full = whole[..., qw:].reshape(4, seq_count, rows, fold, depth)
    out_full = out_full.transpose(1, 4, 0, 3, 2).reshape(seq_count * depth, width)
    return qkv_full, out_full


def expert_layer(local, route_rows, route_scale, moe_gain, gate_up, down_proj):
    _, width = local.shape
    seq_count = lax.axis_size("seq")
    per_device = gate_up.shape[0]
    normed = rms_scale(local, moe_gain)
    select, weighted = routing_tables(route_rows, route_scale)
    table = jnp.dot(select, normed, preferred_element_type=jnp.float32).astype(jnp.bfloat16)
    by_expert = table.reshape(E, CAP, width)
    experts = max(1, per_device // 2)
    slabs = per_device // experts
    if slabs == 1:
        by_expert = jnp.repeat(by_expert, 2, axis=0)
    outgoing = by_expert.reshape(seq_count, experts, CAP, width)
    received = lax.all_to_all(outgoing, "seq", split_axis=0, concat_axis=0, tiled=True)
    rows = received.transpose(1, 0, 2, 3).reshape(experts, seq_count * CAP, width)
    gate_up = gate_up.reshape(experts, slabs, width, 2 * HALF)
    down_proj = down_proj.reshape(experts, slabs, HALF, width)
    projected = jnp.einsum("erd,ekdh->ekrh", rows, gate_up, preferred_element_type=jnp.float32)
    gate_part = projected[..., :HALF]
    up_part = projected[..., HALF:]
    hidden = (gate_part * jax.nn.sigmoid(1.702 * gate_part) * (up_part + 1.0)).astype(jnp.bfloat16)
    partial_value = jnp.einsum(
        "ekrh,ekhd->erd", hidden, down_proj, preferred_element_type=jnp.float32
    ).reshape(experts, seq_count, CAP, width)
    partial_value = partial_value.transpose(1, 0, 2, 3)
    if slabs == 2:
        finished = partial_value.astype(jnp.bfloat16)
    else:
        first = lax.axis_index("seq") % 2 == 0
        lower_rows = partial_value[:, :, : CAP // 2]
        upper_rows = partial_value[:, :, CAP // 2 :]
        kept = jnp.where(first, lower_rows, upper_rows)
        given = jnp.where(first, upper_rows, lower_rows)
        partner_part = swapped(given.astype(jnp.bfloat16), "seq").astype(given.dtype)
        finished = (kept + partner_part).astype(jnp.bfloat16)
    summed = lax.all_to_all(finished, "seq", split_axis=0, concat_axis=0, tiled=True).reshape(
        E * CAP, width
    )
    coarse = weighted.astype(jnp.bfloat16)
    fine = (weighted - coarse.astype(jnp.float32)).astype(jnp.bfloat16)
    dims = (((0,), (0,)), ((), ()))
    mixed = lax.dot_general(coarse, summed, dims, preferred_element_type=jnp.float32)
    mixed += lax.dot_general(fine, summed, dims, preferred_element_type=jnp.float32)
    return (local.astype(jnp.float32) + mixed).astype(jnp.bfloat16)


def attend(query_matrix, keys_extended, values_extended, head_sink_logits, halo_valid):
    tok_count = query_matrix.shape[0]
    query_groups = QUERY_HEADS // KEY_VALUE_HEADS
    scale = float(HEAD_SIZE) ** (-0.5)
    sink_mass_total = jnp.exp(head_sink_logits).reshape(KEY_VALUE_HEADS, query_groups, 1, 1)
    block_queries = query_matrix.reshape(tok_count, KEY_VALUE_HEADS, query_groups, HEAD_SIZE)
    block_keys = keys_extended.reshape(tok_count + WINDOW_SPAN, KEY_VALUE_HEADS, HEAD_SIZE)
    block_values = values_extended.reshape(tok_count + WINDOW_SPAN, KEY_VALUE_HEADS, HEAD_SIZE)
    scores = (
        jnp.einsum("qhgd,khd->hgqk", block_queries, block_keys, preferred_element_type=jnp.float32)
        * scale
    )
    query_pos = jnp.arange(tok_count, dtype=jnp.int32)[:, None] + WINDOW_SPAN
    key_pos = jnp.arange(tok_count + WINDOW_SPAN, dtype=jnp.int32)[None, :]
    distance = query_pos - key_pos
    allowed = (distance >= 0) & (distance < WINDOW_SPAN) & ((key_pos >= WINDOW_SPAN) | halo_valid)
    weights = jnp.where(allowed, jnp.exp(scores), 0.0)
    probs = (weights / (jnp.sum(weights, axis=-1, keepdims=True) + sink_mass_total)).astype(
        jnp.bfloat16
    )
    mixed = jnp.einsum("hgqk,khd->qhgd", probs, block_values, preferred_element_type=jnp.float32)
    return mixed.reshape(tok_count, QUERY_HEADS * HEAD_SIZE).astype(jnp.bfloat16)


def halo_exchange(pairs):
    seq_count, pipe_count = lax.axis_size("seq"), lax.axis_size("pipe")
    order = [s * pipe_count + p for p in range(pipe_count) for s in range(seq_count)]
    return lax.ppermute(pairs, ("seq", "pipe"), list(zip(order[:-1], order[1:])))


def body(
    tokens,
    routes,
    route_weights,
    moe_gain,
    gate_up,
    down_proj,
    attn_gain,
    qkv_proj,
    head_sink_logits,
    out_proj,
):
    if gate_up.shape[0] % 2 == 0 and out_proj.shape[0] % 128 == 0 and tokens.shape[1] == WINDOW_SPAN:
        return fused_body(
            tokens,
            routes,
            route_weights,
            moe_gain,
            gate_up,
            down_proj,
            attn_gain,
            qkv_proj,
            head_sink_logits,
            out_proj,
        )
    qkv_full, out_full = gather_weights(qkv_proj, out_proj)
    hidden = expert_layer(tokens[0], routes[0], route_weights[0], moe_gain, gate_up, down_proj)
    tok_count, _ = hidden.shape
    normed = rms_scale(hidden, attn_gain)
    seq_index = lax.axis_index("seq")
    pipe_index = lax.axis_index("pipe")
    halo_valid = (seq_index > 0) | (pipe_index > 0)
    query_width = QUERY_HEADS * HEAD_SIZE
    width_of_pair = KEY_VALUE_HEADS * HEAD_SIZE
    packed_heads = jnp.dot(normed, qkv_full, preferred_element_type=jnp.float32).astype(
        jnp.bfloat16
    )
    own_pairs = packed_heads[:, query_width:]
    halo_pairs = halo_exchange(own_pairs[tok_count - WINDOW_SPAN :])
    query_matrix = packed_heads[:, :query_width]
    pairs_ext = jnp.concatenate([halo_pairs, own_pairs], axis=0)
    keys_extended = pairs_ext[:, :width_of_pair]
    values_extended = pairs_ext[:, width_of_pair:]
    attended = attend(query_matrix, keys_extended, values_extended, head_sink_logits, halo_valid)
    projected = jnp.dot(attended, out_full, preferred_element_type=jnp.float32)
    return (hidden.astype(jnp.float32) + projected).astype(jnp.bfloat16)[None]


def solution(mesh):
    in_specs = (
        P("pipe", ("groups", "seq"), None),
        P("pipe", ("groups", "seq"), None),
        P("pipe", ("groups", "seq"), None),
        P(),
        P("seq", None, None),
        P("seq", None, None),
        P(),
        P("seq", None),
        P(),
        P("seq", None),
    )
    out_specs = P("pipe", ("groups", "seq"), None)
    return jax.shard_map(body, mesh=mesh, in_specs=in_specs, out_specs=out_specs, check_vma=False)
```

```python
import functools

import jax
import jax.numpy as jnp
from jax import lax
from jax.experimental import pallas as pl
from jax.experimental.pallas import tpu as pltpu
from jax.sharding import PartitionSpec as P


E = 16
QUERY_HEADS = 32
KEY_VALUE_HEADS = 4
HEAD_SIZE = 64
WINDOW_SPAN = 128
HALF = 720
CAP = 48


eps = 1e-05


F32 = jnp.float32
BF16 = jnp.bfloat16
VMEM = pl.BlockSpec(memory_space=pltpu.VMEM)
SMEM = pl.BlockSpec(memory_space=pltpu.SMEM)
HBM = pl.BlockSpec(memory_space=pltpu.HBM)


def route_slots(routes_ref):
    tok_count = routes_ref.shape[1]
    expert = lax.broadcasted_iota(jnp.int32, (E, tok_count), 0)
    member = jnp.zeros((E, tok_count), jnp.bool_)
    for k in range(routes_ref.shape[0]):
        member = member | (routes_ref[k : k + 1, :] == expert)
    first = lax.broadcasted_iota(jnp.int32, (tok_count, tok_count), 0)
    second = lax.broadcasted_iota(jnp.int32, (tok_count, tok_count), 1)
    before = jnp.where(first < second, 1.0, 0.0).astype(BF16)
    flags = jnp.where(member, 1.0, 0.0)
    rank = jnp.dot(flags.astype(BF16), before, preferred_element_type=F32)
    return flags, jnp.where(flags > 0.0, rank, -1.0)


def slot_lanes(width):
    spare = -width % 128
    return spare if spare >= E else spare + 128


def prepare_kernel(tokens_ref, routes_ref, gain_ref, block_ref):
    width, tok_count = tokens_ref.shape
    value = tokens_ref[...].astype(F32).T
    mean_square = jnp.mean(value * value, axis=-1, keepdims=True)
    normed = value * lax.rsqrt(mean_square + eps) * gain_ref[...][None, :]
    block_ref[:, :width] = normed.astype(BF16)
    _, rank = route_slots(routes_ref)
    spare = block_ref.shape[1] - width
    unused = jnp.full((spare - E, tok_count), -1.0, F32)
    block_ref[:, width:] = jnp.concatenate([rank, unused], axis=0).T.astype(BF16)


def prepare(tokens_t, routes_t, gain):
    width, tok_count = tokens_t.shape
    return pl.pallas_call(
        prepare_kernel,
        out_shape=pltpu.HBM((tok_count, width + slot_lanes(width)), BF16),
        in_specs=[VMEM] * 3,
        out_specs=VMEM,
        name="prepare",
    )(tokens_t, routes_t, gain)


def returns_kernel(tokens_ref, routes_ref, scale_ref, residual_ref, coarse_ref, fine_ref):
    tok_count = tokens_ref.shape[1]
    residual_ref[...] = tokens_ref[...].astype(F32).T.astype(BF16)
    _, rank = route_slots(routes_ref)
    expert_index = lax.broadcasted_iota(jnp.int32, (E, tok_count), 0)
    scale = jnp.zeros((E, tok_count), F32)
    for k in range(routes_ref.shape[0]):
        scale += jnp.where(routes_ref[k : k + 1, :] == expert_index, scale_ref[k : k + 1, :], 0.0)
    slot = lax.broadcasted_iota(jnp.int32, (CAP, tok_count), 0).astype(F32)
    rows = []
    for expert in range(E):
        hit = slot == rank[expert : expert + 1, :]
        rows.append(jnp.where(hit, scale[expert : expert + 1, :], 0.0))
    weighted = jnp.concatenate(rows, axis=0).T
    coarse = weighted.astype(BF16)
    coarse_ref[...] = coarse
    fine_ref[...] = (weighted - coarse.astype(F32)).astype(BF16)


def returns(tokens_t, routes_t, scale_t):
    width, tok_count = tokens_t.shape
    return pl.pallas_call(
        returns_kernel,
        out_shape=(
            pltpu.VMEM((tok_count, width), BF16),
            pltpu.VMEM((tok_count, E * CAP), BF16),
            pltpu.VMEM((tok_count, E * CAP), BF16),
        ),
        in_specs=[VMEM] * 3,
        out_specs=(VMEM,) * 3,
        name="returns",
    )(tokens_t, routes_t, scale_t)


def experts_kernel(lines, place_ref, *refs):
    blocks = refs[: 2 * lines]
    gate_up_ref, down_ref, out_ref, picked, slots, total_ref = refs[2 * lines :]
    expert, slab = pl.program_id(0), pl.program_id(1)
    experts, _, width = picked.shape
    tok_count, _ = blocks[0].shape

    @pl.when((expert == 0) & (slab == 0))
    def _():
        place = shard_of(place_ref, 0, 0, lines) * experts
        slot = lax.broadcasted_iota(jnp.int32, (CAP, tok_count), 0).astype(F32)
        for i, block in enumerate(blocks):
            slots[i] = block[:, width:].astype(F32).T
            select = [slot == slots[i, pl.ds(place + e, 1), :] for e in range(experts)]
            select = jnp.where(jnp.concatenate(select, axis=0), 1.0, 0.0).astype(BF16)
            rows = jnp.dot(select, block[:, :width], preferred_element_type=F32).astype(BF16)
            for e in range(experts):
                picked[e, i * CAP : (i + 1) * CAP, :] = rows[e * CAP : (e + 1) * CAP]

    projected = jnp.dot(picked[expert], gate_up_ref[...], preferred_element_type=F32)
    gate_part = projected[:, :HALF]
    up_part = projected[:, HALF:]
    hidden = (gate_part * jax.nn.sigmoid(1.702 * gate_part) * (up_part + 1.0)).astype(BF16)
    value = jnp.dot(hidden, down_ref[...], preferred_element_type=F32)

    @pl.when(slab == 0)
    def _():
        total_ref[...] = value

    @pl.when(slab > 0)
    def _():
        total_ref[...] += value

    @pl.when(slab == pl.num_programs(1) - 1)
    def _():
        for i in range(2 * lines):
            owner = shard_of(place_ref, i // 2, i % 2, lines)
            out_ref[owner] = total_ref[i * CAP : (i + 1) * CAP].astype(BF16)


def run_experts(place, blocks, gate_up, down_proj):
    seq_count = len(blocks)
    tok_count, sent = blocks[0].shape
    per_device, width, gate_width = gate_up.shape
    slabs = 2
    experts = per_device // slabs
    return pl.pallas_call(
        functools.partial(experts_kernel, seq_count // 2),
        out_shape=pltpu.HBM((seq_count, experts, CAP, width), BF16),
        grid=(experts, slabs),
        in_specs=[SMEM]
        + [pl.BlockSpec((tok_count, sent), lambda e, k: (0, 0))] * seq_count
        + [
            pl.BlockSpec((None, width, gate_width), lambda e, k: (e * slabs + k, 0, 0)),
            pl.BlockSpec((None, down_proj.shape[1], width), lambda e, k: (e * slabs + k, 0, 0)),
        ],
        out_specs=pl.BlockSpec((seq_count, None, CAP, width), lambda e, k: (0, e, 0, 0)),
        scratch_shapes=[
            pltpu.VMEM((experts, seq_count * CAP, width), BF16),
            pltpu.VMEM((seq_count, sent - width, tok_count), F32),
            pltpu.VMEM((seq_count * CAP, width), F32),
        ],
        compiler_params=pltpu.CompilerParams(vmem_limit_bytes=40 << 20),
        name="experts",
    )(place, *blocks, *in_hbm([gate_up, down_proj]))


def in_hbm(parts):
    return [pltpu.with_memory_space_constraint(part, pltpu.HBM) for part in parts]


def start_copies(parts, held, sems, first):
    half = held.shape[1] // 2
    copies = []
    for i, part in enumerate(parts):
        target = held.at[i // 2, pl.ds(i % 2 * half, half)]
        source = part.at[:, :, pl.ds(first, held.shape[3])]
        copy = pltpu.make_async_copy(source, target, sems.at[i])
        copy.start()
        copies.append(copy)
    return [copies[i : i + 2] for i in range(0, len(copies), 2)]


def block_step(slot, lines):
    half = lines // 2
    return slot % half * 2 + slot // half


def shard_of(place_ref, step, flip, lines):
    line, bit = 0, 1
    while bit < lines:
        line += (place_ref[0] // bit + step // bit) % 2 * bit
        bit *= 2
    return line * 2 + (place_ref[1] + flip) % 2


def quarter_of(place_ref, group_flip, pipe_flip):
    return (place_ref[2] + group_flip) % 2 * 2 + (place_ref[3] + pipe_flip) % 2


def columns_of(held, slices, place_ref, copies, lines, columns, out_ref):
    tok_count = slices.shape[1]
    for pair in range(4):
        total = jnp.zeros((tok_count, columns), F32)
        for flip in range(2):
            for copy in copies[pair * 2 + flip]:
                copy.wait()
            for step in range(lines):
                total += jnp.dot(
                    slices[shard_of(place_ref, block_step(step, lines), flip, lines)],
                    held[pair * 2 + flip, step],
                    preferred_element_type=F32,
                )
        start = quarter_of(place_ref, pair % 2, pair // 2) * columns
        out_ref[:, pl.ds(pl.multiple_of(start, 128), columns)] = total.astype(BF16)


def pairs_kernel(
    rows, place_ref, tables_ref, residual_ref, coarse_ref, fine_ref, gain_ref, *rest
):
    parts, (pairs_ref, slices, hidden_ref, held, sems) = rest[:16], rest[16:]
    lines, _, columns = held.shape[1:]
    copies = start_copies(parts, held, sems, parts[0].shape[2] - columns)
    table = tables_ref[...]
    mixed = jnp.dot(coarse_ref[...], table, preferred_element_type=F32)
    mixed += jnp.dot(fine_ref[...], table, preferred_element_type=F32)
    hidden = (residual_ref[...].astype(F32) + mixed).astype(BF16)
    value = hidden.astype(F32)
    mean_square = jnp.mean(value * value, axis=-1, keepdims=True)
    normed = (value * lax.rsqrt(mean_square + eps) * gain_ref[...][None, :]).astype(BF16)
    slices[...] = jnp.zeros_like(slices)
    for s in range(2 * lines):
        slices[s, :, :rows] = normed[:, s * rows : (s + 1) * rows]
    columns_of(held, slices, place_ref, copies, lines, columns, pairs_ref)
    hidden_ref[...] = value.T.astype(BF16)


def project_pairs(place, tables, residual, coarse, fine, gain, parts, rows, columns):
    tok_count, width = residual.shape
    lines, padded = 2 * parts[0].shape[0], parts[0].shape[1]
    return pl.pallas_call(
        functools.partial(pairs_kernel, rows),
        out_shape=(
            jax.ShapeDtypeStruct((tok_count, 4 * columns), BF16),
            jax.ShapeDtypeStruct((2 * lines, tok_count, padded), BF16),
            jax.ShapeDtypeStruct((width, tok_count), BF16),
        ),
        in_specs=[SMEM] + [VMEM] * 5 + [HBM] * 16,
        out_specs=(VMEM,) * 3,
        scratch_shapes=[
            pltpu.VMEM((8, lines, padded, columns), BF16),
            pltpu.SemaphoreType.DMA((16,)),
        ],
        compiler_params=pltpu.CompilerParams(vmem_limit_bytes=20 << 20),
        name="pairs",
    )(place, tables, residual, coarse, fine, gain, *in_hbm(parts))


def queries_kernel(place_ref, slices, *rest):
    parts, (queries_ref, held, sems) = rest[:16], rest[16:]
    lines, _, columns = held.shape[1:]
    copies = start_copies(parts, held, sems, 0)
    columns_of(held, slices, place_ref, copies, lines, columns, queries_ref)


def project_queries(place, slices, parts, columns):
    count, tok_count, padded = slices.shape
    return pl.pallas_call(
        queries_kernel,
        out_shape=jax.ShapeDtypeStruct((tok_count, 4 * columns), BF16),
        in_specs=[SMEM, VMEM] + [HBM] * 16,
        out_specs=VMEM,
        scratch_shapes=[
            pltpu.VMEM((8, count // 2, padded, columns), BF16),
            pltpu.SemaphoreType.DMA((16,)),
        ],
        compiler_params=pltpu.CompilerParams(vmem_limit_bytes=20 << 20),
        name="queries",
    )(place, slices, *in_hbm(parts))


def attention_kernel(
    place_ref, sink_ref, packed_ref, pairs_ref, halo_ref, hidden_ref, *rest
):
    parts, (out_ref, held, mixed, total_ref, sems) = rest[:16], rest[16:]
    lines, quarter_rows, depth = held.shape[1:]
    copies = start_copies(parts, held, sems, 0)
    tok_count = packed_ref.shape[0]
    pair_width = 2 * HEAD_SIZE
    kv_width = KEY_VALUE_HEADS * HEAD_SIZE
    query_groups = QUERY_HEADS // KEY_VALUE_HEADS
    span = halo_ref.shape[0]
    extent = span + tok_count
    query_pos = lax.broadcasted_iota(jnp.int32, (tok_count, extent), 0) + span
    key_pos = lax.broadcasted_iota(jnp.int32, (tok_count, extent), 1)
    distance = query_pos - key_pos
    halo_valid = place_ref[0] + place_ref[1] + place_ref[3] > 0
    first_key = jnp.where(halo_valid, 0, span)
    allowed = (distance >= 0) & (distance < WINDOW_SPAN) & (key_pos >= first_key)
    left = lax.broadcasted_iota(jnp.int32, (extent, pair_width), 1) < HEAD_SIZE
    scale = float(HEAD_SIZE) ** (-0.5)

    def sides(start, head, factor):
        lanes = pl.ds(start + head // 2 * pair_width, pair_width)
        both = jnp.concatenate([halo_ref[:, lanes], pairs_ref[:, lanes]], axis=0)
        both = both.astype(F32) * factor
        turned = pltpu.roll(both, HEAD_SIZE, 1)
        low, high = (both, turned) if head % 2 == 0 else (turned, both)
        low = jnp.where(left, low, 0.0).astype(BF16)
        high = jnp.where(left, 0.0, high).astype(BF16)
        return low, high

    pairs = query_groups // 2
    for head in range(KEY_VALUE_HEADS):
        keys, values = sides(0, head, scale), sides(kv_width, head, 1.0)
        base = head * pairs * pair_width
        stacked = jnp.concatenate(
            [packed_ref[:, base + j * pair_width : base + (j + 1) * pair_width] for j in range(pairs)],
            axis=0,
        )
        outcome = None
        for side in range(2):
            scores = lax.dot_general(
                stacked, keys[side], (((1,), (1,)), ((), ())), preferred_element_type=F32
            )
            probs = []
            for j in range(pairs):
                piece = scores[j * tok_count : (j + 1) * tok_count]
                weights = jnp.where(allowed, jnp.exp(piece), 0.0)
                sink = sink_ref[head * query_groups + 2 * j + side]
                sums = jnp.sum(weights, axis=-1, keepdims=True) + sink
                probs.append((weights * (1.0 / sums)).astype(BF16))
            part = jnp.dot(
                jnp.concatenate(probs, axis=0), values[side], preferred_element_type=F32
            )
            outcome = part if outcome is None else outcome + part
        for j in range(pairs):
            column = base + j * pair_width
            mixed[column // depth, :, column % depth : column % depth + pair_width] = outcome[
                j * tok_count : (j + 1) * tok_count
            ].astype(BF16)

    for pair in range(4):
        total = jnp.zeros((quarter_rows, tok_count), F32)
        for flip in range(2):
            for copy in copies[pair * 2 + flip]:
                copy.wait()
            for step in range(lines):
                total += lax.dot_general(
                    held[pair * 2 + flip, step],
                    mixed[shard_of(place_ref, block_step(step, lines), flip, lines)],
                    (((1,), (1,)), ((), ())),
                    preferred_element_type=F32,
                )
        start = quarter_of(place_ref, pair % 2, pair // 2) * quarter_rows
        total_ref[pl.ds(pl.multiple_of(start, 8), quarter_rows), :] = total
    out_ref[...] = (hidden_ref[...].astype(F32) + total_ref[...]).astype(BF16)


def attend_and_project(place, sinks, queries, pairs, halo, hidden_t, parts):
    width, tok_count = hidden_t.shape
    half, quarter_rows, depth = parts[0].shape
    lines = 2 * half
    return pl.pallas_call(
        attention_kernel,
        out_shape=jax.ShapeDtypeStruct((width, tok_count), BF16),
        in_specs=[SMEM] * 2 + [VMEM] * 4 + [HBM] * 16,
        out_specs=VMEM,
        scratch_shapes=[
            pltpu.VMEM((8, lines, quarter_rows, depth), BF16),
            pltpu.VMEM((2 * lines, tok_count, depth), BF16),
            pltpu.VMEM((width, tok_count), F32),
            pltpu.SemaphoreType.DMA((16,)),
        ],
        compiler_params=pltpu.CompilerParams(vmem_limit_bytes=24 << 20),
        name="attention",
    )(place, sinks, queries, pairs, halo, hidden_t, *in_hbm(parts))


def place_of():
    seq_index = lax.axis_index("seq")
    return jnp.stack(
        [seq_index // 2, seq_index % 2, lax.axis_index("groups") % 2, lax.axis_index("pipe")]
    ).astype(jnp.int32)


def own_quarters(qkv_proj, out_proj):
    rows, qkv_width = qkv_proj.shape
    quarter = lax.axis_index("groups") % 2 * 2 + lax.axis_index("pipe")
    query_width = QUERY_HEADS * HEAD_SIZE
    qw, pw, ow = query_width // 4, (qkv_width - query_width) // 4, out_proj.shape[1] // 4
    mine_queries = lax.dynamic_slice_in_dim(qkv_proj, quarter * qw, qw, 1)
    mine_pairs = lax.dynamic_slice_in_dim(qkv_proj, query_width + quarter * pw, pw, 1)
    mine_qkv = jnp.concatenate([mine_queries, mine_pairs], axis=1)
    mine_out = lax.dynamic_slice_in_dim(out_proj.T, quarter * ow, ow, 0)
    return jnp.pad(mine_qkv, ((0, -rows % 8), (0, 0))), mine_out


def flipped(value, bit):
    count = lax.axis_size("seq")
    return lax.ppermute(value, "seq", [(i, i ^ bit * 2) for i in range(count)])


def far_blocks(block, lines):
    bit = lines // 2
    found = {0: block}
    while bit > 1:
        for step in list(found):
            found[step + bit] = flipped(found[step], bit)
        bit //= 2
    return [found[step] for step in range(0, lines, 2)]


def gather_quarters(mine, lines, last_axis):
    far = far_blocks(mine, lines)
    even = jnp.stack(far)
    odd = flipped(even, 1)
    even_mate, even_across = swapped(even, "seq"), swapped(even, "groups")
    odd_mate, odd_across = swapped(odd, "seq"), swapped(odd, "groups")
    even_last = swapped(even_mate, "groups")
    odd_last = swapped(odd_across if last_axis == "seq" else odd_mate, last_axis)
    parts = [even, odd, even_mate, odd_mate, even_across, odd_across, even_last, odd_last]
    return parts + [swapped(part, "pipe") for part in parts]


def fused_body(
    tokens, routes, route_weights, moe_gain, gate_up, down_proj, attn_gain, qkv_proj, sinks, out_proj
):
    seq_count = lax.axis_size("seq")
    tok_count, width = tokens.shape[1:]
    rows, qkv_width = qkv_proj.shape
    tokens_t, routes_t, scale_t = tokens[0].T, routes[0].T, route_weights[0].T
    place = place_of()

    block = prepare(tokens_t, routes_t, moe_gain)
    lines = seq_count // 2
    evens = far_blocks(block, lines)
    blocks = []
    for even in evens:
        odd = flipped(even, 1)
        for value in (even, odd):
            blocks += [value, swapped(value, "seq")]
    mine_qkv, mine_out = own_quarters(qkv_proj, out_proj)
    qkv_parts = gather_quarters(mine_qkv, lines, "groups")
    out_parts = gather_quarters(mine_out, lines, "seq")

    finished = run_experts(place, in_hbm(blocks[:1]) + blocks[1:], gate_up, down_proj)
    summed = lax.all_to_all(finished, "seq", split_axis=0, concat_axis=0, tiled=True)
    residual, coarse, fine = returns(tokens_t, routes_t, scale_t)

    summed = summed.reshape(E * CAP, width)
    query_width = QUERY_HEADS * HEAD_SIZE
    pairs, slices, hidden_t = project_pairs(
        place, summed, residual, coarse, fine, attn_gain, qkv_parts, rows, (qkv_width - query_width) // 4
    )
    halo = halo_exchange(pairs[tok_count - WINDOW_SPAN :])
    queries = project_queries(place, slices, qkv_parts, query_width // 4)
    out_t = attend_and_project(place, jnp.exp(sinks), queries, pairs, halo, hidden_t, out_parts)
    return out_t.T[None]


def swapped(value, axis):
    return lax.ppermute(value, axis, [(i, i ^ 1) for i in range(lax.axis_size(axis))])


def rms_scale(value_matrix, gain):
    widened = value_matrix.astype(jnp.float32)
    mean_square = jnp.mean(widened * widened, axis=-1, keepdims=True)
    return (widened * lax.rsqrt(mean_square + eps) * gain).astype(jnp.bfloat16)


def routing_tables(route_rows, route_scale):
    tok_count = route_rows.shape[0]
    experts = jnp.arange(E, dtype=jnp.int32)
    named = route_rows[None, :, :] == experts[:, None, None]
    member = jnp.any(named, axis=2)
    scale = jnp.sum(jnp.where(named, route_scale[None, :, :], 0.0), axis=2)
    token = jnp.arange(tok_count, dtype=jnp.int32)
    before = (token[:, None] < token[None, :]).astype(jnp.bfloat16)
    rank = jnp.dot(member.astype(jnp.bfloat16), before, preferred_element_type=jnp.float32)
    slot = jnp.arange(CAP, dtype=jnp.float32)
    chosen = member[:, None, :] & (rank[:, None, :] == slot[None, :, None])
    select = chosen.reshape(E * CAP, tok_count).astype(jnp.bfloat16)
    weighted = jnp.where(chosen, scale[:, None, :], 0.0).reshape(E * CAP, tok_count)
    return select, weighted


def neighbour_relay(block, seq_count):
    rounds = seq_count // 2
    up = [(i, i + 2) for i in range(seq_count - 2)]
    down = [(i + 2, i) for i in range(seq_count - 2)]
    rising, falling = [block], [block]
    for _ in range(rounds - 1):
        rising.append(lax.ppermute(rising[-1], "seq", up))
        falling.append(lax.ppermute(falling[-1], "seq", down))
    line = lax.axis_index("seq") // 2
    blocks = [block]
    for k in range(1, rounds):
        blocks.append(jnp.where(line >= k, rising[k], falling[rounds - k]))
    return blocks


def gather_weights(qkv_proj, out_proj):
    seq_count = lax.axis_size("seq")
    rows, qkv_width = qkv_proj.shape
    depth, width = out_proj.shape
    group_bit = lax.axis_index("groups") % 2
    pipe_bit = lax.axis_index("pipe")
    quarter = group_bit * 2 + pipe_bit
    qw, ow = qkv_width // 4, width // 4
    fold = ow // rows
    mine_qkv = lax.dynamic_slice_in_dim(qkv_proj, quarter * qw, qw, 1)
    mine_out = lax.dynamic_slice_in_dim(out_proj.T, quarter * ow, ow, 0)
    block = jnp.concatenate(
        [mine_qkv] + [mine_out[i * rows : (i + 1) * rows] for i in range(fold)], axis=1
    )
    blocks = neighbour_relay(block, seq_count)
    lines = seq_count // 2
    line = lax.axis_index("seq") // 2
    stacked = jnp.stack(blocks)
    column = jnp.stack(
        [lax.dynamic_index_in_dim(stacked, (line - j) % lines, 0, keepdims=False) for j in range(lines)]
    )
    other = swapped(column, "seq")
    odd = lax.axis_index("seq") % 2 == 1
    both = jnp.stack([jnp.where(odd, other, column), jnp.where(odd, column, other)], axis=1)
    both = both.reshape(seq_count, rows, block.shape[1])
    across = swapped(both, "groups")
    high = group_bit == 1
    halves = jnp.stack([jnp.where(high, across, both), jnp.where(high, both, across)])
    beside = swapped(halves, "pipe")
    second = pipe_bit == 1
    whole = jnp.stack([jnp.where(second, beside, halves), jnp.where(second, halves, beside)], axis=1)
    whole = whole.reshape(4, seq_count, rows, block.shape[1])
    qkv_full = whole[..., :qw].transpose(1, 2, 0, 3).reshape(seq_count * rows, qkv_width)
    out_full = whole[..., qw:].reshape(4, seq_count, rows, fold, depth)
    out_full = out_full.transpose(1, 4, 0, 3, 2).reshape(seq_count * depth, width)
    return qkv_full, out_full


def expert_layer(local, route_rows, route_scale, moe_gain, gate_up, down_proj):
    _, width = local.shape
    seq_count = lax.axis_size("seq")
    per_device = gate_up.shape[0]
    normed = rms_scale(local, moe_gain)
    select, weighted = routing_tables(route_rows, route_scale)
    table = jnp.dot(select, normed, preferred_element_type=jnp.float32).astype(jnp.bfloat16)
    by_expert = table.reshape(E, CAP, width)
    experts = max(1, per_device // 2)
    slabs = per_device // experts
    if slabs == 1:
        by_expert = jnp.repeat(by_expert, 2, axis=0)
    outgoing = by_expert.reshape(seq_count, experts, CAP, width)
    received = lax.all_to_all(outgoing, "seq", split_axis=0, concat_axis=0, tiled=True)
    rows = received.transpose(1, 0, 2, 3).reshape(experts, seq_count * CAP, width)
    gate_up = gate_up.reshape(experts, slabs, width, 2 * HALF)
    down_proj = down_proj.reshape(experts, slabs, HALF, width)
    projected = jnp.einsum("erd,ekdh->ekrh", rows, gate_up, preferred_element_type=jnp.float32)
    gate_part = projected[..., :HALF]
    up_part = projected[..., HALF:]
    hidden = (gate_part * jax.nn.sigmoid(1.702 * gate_part) * (up_part + 1.0)).astype(jnp.bfloat16)
    partial_value = jnp.einsum(
        "ekrh,ekhd->erd", hidden, down_proj, preferred_element_type=jnp.float32
    ).reshape(experts, seq_count, CAP, width)
    partial_value = partial_value.transpose(1, 0, 2, 3)
    if slabs == 2:
        finished = partial_value.astype(jnp.bfloat16)
    else:
        first = lax.axis_index("seq") % 2 == 0
        lower_rows = partial_value[:, :, : CAP // 2]
        upper_rows = partial_value[:, :, CAP // 2 :]
        kept = jnp.where(first, lower_rows, upper_rows)
        given = jnp.where(first, upper_rows, lower_rows)
        partner_part = swapped(given.astype(jnp.bfloat16), "seq").astype(given.dtype)
        finished = (kept + partner_part).astype(jnp.bfloat16)
    summed = lax.all_to_all(finished, "seq", split_axis=0, concat_axis=0, tiled=True).reshape(
        E * CAP, width
    )
    coarse = weighted.astype(jnp.bfloat16)
    fine = (weighted - coarse.astype(jnp.float32)).astype(jnp.bfloat16)
    dims = (((0,), (0,)), ((), ()))
    mixed = lax.dot_general(coarse, summed, dims, preferred_element_type=jnp.float32)
    mixed += lax.dot_general(fine, summed, dims, preferred_element_type=jnp.float32)
    return (local.astype(jnp.float32) + mixed).astype(jnp.bfloat16)


def attend(query_matrix, keys_extended, values_extended, head_sink_logits, halo_valid):
    tok_count = query_matrix.shape[0]
    query_groups = QUERY_HEADS // KEY_VALUE_HEADS
    scale = float(HEAD_SIZE) ** (-0.5)
    sink_mass_total = jnp.exp(head_sink_logits).reshape(KEY_VALUE_HEADS, query_groups, 1, 1)
    block_queries = query_matrix.reshape(tok_count, KEY_VALUE_HEADS, query_groups, HEAD_SIZE)
    block_keys = keys_extended.reshape(tok_count + WINDOW_SPAN, KEY_VALUE_HEADS, HEAD_SIZE)
    block_values = values_extended.reshape(tok_count + WINDOW_SPAN, KEY_VALUE_HEADS, HEAD_SIZE)
    scores = (
        jnp.einsum("qhgd,khd->hgqk", block_queries, block_keys, preferred_element_type=jnp.float32)
        * scale
    )
    query_pos = jnp.arange(tok_count, dtype=jnp.int32)[:, None] + WINDOW_SPAN
    key_pos = jnp.arange(tok_count + WINDOW_SPAN, dtype=jnp.int32)[None, :]
    distance = query_pos - key_pos
    allowed = (distance >= 0) & (distance < WINDOW_SPAN) & ((key_pos >= WINDOW_SPAN) | halo_valid)
    weights = jnp.where(allowed, jnp.exp(scores), 0.0)
    probs = (weights / (jnp.sum(weights, axis=-1, keepdims=True) + sink_mass_total)).astype(
        jnp.bfloat16
    )
    mixed = jnp.einsum("hgqk,khd->qhgd", probs, block_values, preferred_element_type=jnp.float32)
    return mixed.reshape(tok_count, QUERY_HEADS * HEAD_SIZE).astype(jnp.bfloat16)


def halo_exchange(pairs):
    seq_count, pipe_count = lax.axis_size("seq"), lax.axis_size("pipe")
    order = [s * pipe_count + p for p in range(pipe_count) for s in range(seq_count)]
    return lax.ppermute(pairs, ("seq", "pipe"), list(zip(order[:-1], order[1:])))


def body(
    tokens,
    routes,
    route_weights,
    moe_gain,
    gate_up,
    down_proj,
    attn_gain,
    qkv_proj,
    head_sink_logits,
    out_proj,
):
    if gate_up.shape[0] % 2 == 0 and out_proj.shape[0] % 128 == 0 and tokens.shape[1] == WINDOW_SPAN:
        return fused_body(
            tokens,
            routes,
            route_weights,
            moe_gain,
            gate_up,
            down_proj,
            attn_gain,
            qkv_proj,
            head_sink_logits,
            out_proj,
        )
    qkv_full, out_full = gather_weights(qkv_proj, out_proj)
    hidden = expert_layer(tokens[0], routes[0], route_weights[0], moe_gain, gate_up, down_proj)
    tok_count, _ = hidden.shape
    normed = rms_scale(hidden, attn_gain)
    seq_index = lax.axis_index("seq")
    pipe_index = lax.axis_index("pipe")
    halo_valid = (seq_index > 0) | (pipe_index > 0)
    query_width = QUERY_HEADS * HEAD_SIZE
    width_of_pair = KEY_VALUE_HEADS * HEAD_SIZE
    packed_heads = jnp.dot(normed, qkv_full, preferred_element_type=jnp.float32).astype(
        jnp.bfloat16
    )
    own_pairs = packed_heads[:, query_width:]
    halo_pairs = halo_exchange(own_pairs[tok_count - WINDOW_SPAN :])
    query_matrix = packed_heads[:, :query_width]
    pairs_ext = jnp.concatenate([halo_pairs, own_pairs], axis=0)
    keys_extended = pairs_ext[:, :width_of_pair]
    values_extended = pairs_ext[:, width_of_pair:]
    attended = attend(query_matrix, keys_extended, values_extended, head_sink_logits, halo_valid)
    projected = jnp.dot(attended, out_full, preferred_element_type=jnp.float32)
    return (hidden.astype(jnp.float32) + projected).astype(jnp.bfloat16)[None]


def solution(mesh):
    in_specs = (
        P("pipe", ("groups", "seq"), None),
        P("pipe", ("groups", "seq"), None),
        P("pipe", ("groups", "seq"), None),
        P(),
        P("seq", None, None),
        P("seq", None, None),
        P(),
        P("seq", None),
        P(),
        P("seq", None),
    )
    out_specs = P("pipe", ("groups", "seq"), None)
    return jax.shard_map(body, mesh=mesh, in_specs=in_specs, out_specs=out_specs, check_vma=False)
```

```python
import functools

import jax
import jax.numpy as jnp
from jax import lax
from jax.experimental import pallas as pl
from jax.experimental.pallas import tpu as pltpu
from jax.sharding import PartitionSpec as P


E = 16
QUERY_HEADS = 32
KEY_VALUE_HEADS = 4
HEAD_SIZE = 64
WINDOW_SPAN = 128
HALF = 720
CAP = 48


eps = 1e-05


F32 = jnp.float32
BF16 = jnp.bfloat16
VMEM = pl.BlockSpec(memory_space=pltpu.VMEM)
SMEM = pl.BlockSpec(memory_space=pltpu.SMEM)
HBM = pl.BlockSpec(memory_space=pltpu.HBM)


def route_slots(routes_ref):
    tok_count = routes_ref.shape[1]
    expert = lax.broadcasted_iota(jnp.int32, (E, tok_count), 0)
    member = jnp.zeros((E, tok_count), jnp.bool_)
    for k in range(routes_ref.shape[0]):
        member = member | (routes_ref[k : k + 1, :] == expert)
    first = lax.broadcasted_iota(jnp.int32, (tok_count, tok_count), 0)
    second = lax.broadcasted_iota(jnp.int32, (tok_count, tok_count), 1)
    before = jnp.where(first < second, 1.0, 0.0).astype(BF16)
    flags = jnp.where(member, 1.0, 0.0)
    rank = jnp.dot(flags.astype(BF16), before, preferred_element_type=F32)
    return flags, jnp.where(flags > 0.0, rank, -1.0)


def slot_lanes(width):
    spare = -width % 128
    return spare if spare >= E else spare + 128


def prepare_kernel(tokens_ref, routes_ref, gain_ref, block_ref):
    width, tok_count = tokens_ref.shape
    value = tokens_ref[...].astype(F32).T
    mean_square = jnp.mean(value * value, axis=-1, keepdims=True)
    normed = value * lax.rsqrt(mean_square + eps) * gain_ref[...][None, :]
    block_ref[:, :width] = normed.astype(BF16)
    _, rank = route_slots(routes_ref)
    spare = block_ref.shape[1] - width
    unused = jnp.full((spare - E, tok_count), -1.0, F32)
    block_ref[:, width:] = jnp.concatenate([rank, unused], axis=0).T.astype(BF16)


def prepare(tokens_t, routes_t, gain):
    width, tok_count = tokens_t.shape
    return pl.pallas_call(
        prepare_kernel,
        out_shape=jax.ShapeDtypeStruct((tok_count, width + slot_lanes(width)), BF16),
        in_specs=[VMEM] * 3,
        out_specs=VMEM,
        name="prepare",
    )(tokens_t, routes_t, gain)


def returns_kernel(tokens_ref, routes_ref, scale_ref, residual_ref, coarse_ref, fine_ref):
    tok_count = tokens_ref.shape[1]
    residual_ref[...] = tokens_ref[...].astype(F32).T.astype(BF16)
    _, rank = route_slots(routes_ref)
    expert_index = lax.broadcasted_iota(jnp.int32, (E, tok_count), 0)
    scale = jnp.zeros((E, tok_count), F32)
    for k in range(routes_ref.shape[0]):
        scale += jnp.where(routes_ref[k : k + 1, :] == expert_index, scale_ref[k : k + 1, :], 0.0)
    slot = lax.broadcasted_iota(jnp.int32, (CAP, tok_count), 0).astype(F32)
    rows = []
    for expert in range(E):
        hit = slot == rank[expert : expert + 1, :]
        rows.append(jnp.where(hit, scale[expert : expert + 1, :], 0.0))
    weighted = jnp.concatenate(rows, axis=0).T
    coarse = weighted.astype(BF16)
    coarse_ref[...] = coarse
    fine_ref[...] = (weighted - coarse.astype(F32)).astype(BF16)


def returns(tokens_t, routes_t, scale_t):
    width, tok_count = tokens_t.shape
    return pl.pallas_call(
        returns_kernel,
        out_shape=(
            pltpu.VMEM((tok_count, width), BF16),
            pltpu.VMEM((tok_count, E * CAP), BF16),
            pltpu.VMEM((tok_count, E * CAP), BF16),
        ),
        in_specs=[VMEM] * 3,
        out_specs=(VMEM,) * 3,
        name="returns",
    )(tokens_t, routes_t, scale_t)


def fetch_kernel(gate_up_ref, down_ref, gate_up_out, down_out, sems):
    copies = [
        pltpu.make_async_copy(gate_up_ref.at[0], gate_up_out, sems.at[0]),
        pltpu.make_async_copy(down_ref.at[0], down_out, sems.at[1]),
    ]
    for copy in copies:
        copy.start()
    for copy in copies:
        copy.wait()


def fetch_first(gate_up, down_proj):
    return pl.pallas_call(
        fetch_kernel,
        out_shape=(pltpu.VMEM(gate_up.shape[1:], BF16), pltpu.VMEM(down_proj.shape[1:], BF16)),
        in_specs=[HBM] * 2,
        out_specs=(VMEM, VMEM),
        scratch_shapes=[pltpu.SemaphoreType.DMA((2,))],
        compiler_params=pltpu.CompilerParams(vmem_limit_bytes=4 << 20),
        name="fetch",
    )(gate_up, down_proj)


def experts_kernel(lines, place_ref, *refs):
    blocks = refs[: 2 * lines]
    first_up, first_down, gate_up_ref, down_ref, out_ref = refs[2 * lines : 2 * lines + 5]
    picked, slots, total_ref, ups, downs, results, sems = refs[2 * lines + 5 :]
    experts, _, width = picked.shape
    per_device = gate_up_ref.shape[0]
    slabs = per_device // experts
    tok_count, _ = blocks[0].shape

    def weights(slab):
        spot = slab % 2
        return [
            pltpu.make_async_copy(gate_up_ref.at[slab], ups.at[spot], sems.at[spot]),
            pltpu.make_async_copy(down_ref.at[slab], downs.at[spot], sems.at[2 + spot]),
        ]

    def begin(slab):
        if slab < per_device:
            for copy in weights(slab):
                copy.start()

    begin(1)
    begin(2)
    place = shard_of(place_ref, 0, 0, lines) * experts
    slot = lax.broadcasted_iota(jnp.int32, (CAP, tok_count), 0).astype(F32)
    for i, block in enumerate(blocks):
        slots[i] = block[:, width:].astype(F32).T
        select = [slot == slots[i, pl.ds(place + e, 1), :] for e in range(experts)]
        select = jnp.where(jnp.concatenate(select, axis=0), 1.0, 0.0).astype(BF16)
        rows = jnp.dot(select, block[:, :width], preferred_element_type=F32).astype(BF16)
        for e in range(experts):
            picked[e, i * CAP : (i + 1) * CAP, :] = rows[e * CAP : (e + 1) * CAP]

    sent_back = []
    for slab in range(per_device):
        expert, part = slab // slabs, slab % slabs
        if slab == 0:
            gate_up, down = first_up, first_down
        else:
            for copy in weights(slab):
                copy.wait()
            gate_up, down = ups.at[slab % 2], downs.at[slab % 2]
        projected = jnp.dot(picked[expert], gate_up[...], preferred_element_type=F32)
        gate_part = projected[:, :HALF]
        up_part = projected[:, HALF:]
        hidden = (gate_part * jax.nn.sigmoid(1.702 * gate_part) * (up_part + 1.0)).astype(BF16)
        value = jnp.dot(hidden, down[...], preferred_element_type=F32)
        if slab >= 1:
            begin(slab + 2)
        if part < slabs - 1:
            total_ref[...] = value if part == 0 else total_ref[...] + value
            continue
        if part > 0:
            value += total_ref[...]
        for i in range(2 * lines):
            owner = shard_of(place_ref, i // 2, i % 2, lines)
            results[expert, owner] = value[i * CAP : (i + 1) * CAP].astype(BF16)
        copy = pltpu.make_async_copy(results.at[expert], out_ref.at[:, expert], sems.at[4 + expert])
        copy.start()
        sent_back.append(copy)
    for copy in sent_back:
        copy.wait()


def run_experts(place, blocks, first, gate_up, down_proj):
    seq_count = len(blocks)
    tok_count, sent = blocks[0].shape
    per_device, width, gate_width = gate_up.shape
    experts = per_device // 2
    return pl.pallas_call(
        functools.partial(experts_kernel, seq_count // 2),
        out_shape=pltpu.HBM((seq_count, experts, CAP, width), BF16),
        in_specs=[SMEM] + [VMEM] * (seq_count + 2) + [HBM] * 2,
        out_specs=HBM,
        scratch_shapes=[
            pltpu.VMEM((experts, seq_count * CAP, width), BF16),
            pltpu.VMEM((seq_count, sent - width, tok_count), F32),
            pltpu.VMEM((seq_count * CAP, width), F32),
            pltpu.VMEM((2, width, gate_width), BF16),
            pltpu.VMEM((2, down_proj.shape[1], width), BF16),
            pltpu.VMEM((experts, seq_count, CAP, width), BF16),
            pltpu.SemaphoreType.DMA((4 + experts,)),
        ],
        compiler_params=pltpu.CompilerParams(vmem_limit_bytes=36 << 20),
        name="experts",
    )(place, *blocks, *first, gate_up, down_proj)


def stack_kernel(*refs):
    *parts, out_ref, sems = refs
    copies = []
    for i, part in enumerate(parts):
        copy = pltpu.make_async_copy(part, out_ref.at[i], sems.at[i])
        copy.start()
        copies.append(copy)
    for copy in copies:
        copy.wait()


def stacked(parts):
    return pl.pallas_call(
        stack_kernel,
        out_shape=pltpu.HBM((len(parts),) + parts[0].shape, parts[0].dtype),
        in_specs=[pl.BlockSpec(memory_space=pl.ANY)] * len(parts),
        out_specs=HBM,
        scratch_shapes=[pltpu.SemaphoreType.DMA((len(parts),))],
        compiler_params=pltpu.CompilerParams(vmem_limit_bytes=1 << 20),
    )(*parts)


def in_hbm(parts):
    return [pltpu.with_memory_space_constraint(part, pltpu.HBM) for part in parts]


def start_copies(parts, held, sems, first):
    half = held.shape[1] // 2
    copies = []
    for i, part in enumerate(parts):
        target = held.at[i // 2, pl.ds(i % 2 * half, half)]
        source = part.at[:, :, pl.ds(first, held.shape[3])]
        copy = pltpu.make_async_copy(source, target, sems.at[i])
        copy.start()
        copies.append(copy)
    return [copies[i : i + 2] for i in range(0, len(copies), 2)]


def block_step(slot, lines):
    half = lines // 2
    return slot % half * 2 + slot // half


def shard_of(place_ref, step, flip, lines):
    line, bit = 0, 1
    while bit < lines:
        line += (place_ref[0] // bit + step // bit) % 2 * bit
        bit *= 2
    return line * 2 + (place_ref[1] + flip) % 2


def quarter_of(place_ref, group_flip, pipe_flip):
    return (place_ref[2] + group_flip) % 2 * 2 + (place_ref[3] + pipe_flip) % 2


def columns_of(held, slices, place_ref, copies, lines, columns, out_ref):
    tok_count = slices.shape[1]
    for pair in range(4):
        total = jnp.zeros((tok_count, columns), F32)
        for flip in range(2):
            for copy in copies[pair * 2 + flip]:
                copy.wait()
            for step in range(lines):
                total += jnp.dot(
                    slices[shard_of(place_ref, block_step(step, lines), flip, lines)],
                    held[pair * 2 + flip, step],
                    preferred_element_type=F32,
                )
        start = quarter_of(place_ref, pair % 2, pair // 2) * columns
        out_ref[:, pl.ds(pl.multiple_of(start, 128), columns)] = total.astype(BF16)


def pairs_kernel(
    rows, place_ref, tables_ref, residual_ref, coarse_ref, fine_ref, gain_ref, *rest
):
    parts, (pairs_ref, slices, hidden_ref, held, sems) = rest[:16], rest[16:]
    lines, _, columns = held.shape[1:]
    copies = start_copies(parts, held, sems, parts[0].shape[2] - columns)
    table = tables_ref[...]
    mixed = jnp.dot(coarse_ref[...], table, preferred_element_type=F32)
    mixed += jnp.dot(fine_ref[...], table, preferred_element_type=F32)
    hidden = (residual_ref[...].astype(F32) + mixed).astype(BF16)
    value = hidden.astype(F32)
    mean_square = jnp.mean(value * value, axis=-1, keepdims=True)
    normed = (value * lax.rsqrt(mean_square + eps) * gain_ref[...][None, :]).astype(BF16)
    slices[...] = jnp.zeros_like(slices)
    for s in range(2 * lines):
        slices[s, :, :rows] = normed[:, s * rows : (s + 1) * rows]
    columns_of(held, slices, place_ref, copies, lines, columns, pairs_ref)
    hidden_ref[...] = value.T.astype(BF16)


def project_pairs(place, tables, residual, coarse, fine, gain, parts, rows, columns):
    tok_count, width = residual.shape
    lines, padded = 2 * parts[0].shape[0], parts[0].shape[1]
    return pl.pallas_call(
        functools.partial(pairs_kernel, rows),
        out_shape=(
            jax.ShapeDtypeStruct((tok_count, 4 * columns), BF16),
            jax.ShapeDtypeStruct((2 * lines, tok_count, padded), BF16),
            jax.ShapeDtypeStruct((width, tok_count), BF16),
        ),
        in_specs=[SMEM] + [VMEM] * 5 + [HBM] * 16,
        out_specs=(VMEM,) * 3,
        scratch_shapes=[
            pltpu.VMEM((8, lines, padded, columns), BF16),
            pltpu.SemaphoreType.DMA((16,)),
        ],
        compiler_params=pltpu.CompilerParams(vmem_limit_bytes=20 << 20),
        name="pairs",
    )(place, tables, residual, coarse, fine, gain, *in_hbm(parts))


def queries_kernel(place_ref, slices, *rest):
    parts, (queries_ref, held, sems) = rest[:16], rest[16:]
    lines, _, columns = held.shape[1:]
    copies = start_copies(parts, held, sems, 0)
    columns_of(held, slices, place_ref, copies, lines, columns, queries_ref)


def project_queries(place, slices, parts, columns):
    count, tok_count, padded = slices.shape
    return pl.pallas_call(
        queries_kernel,
        out_shape=jax.ShapeDtypeStruct((tok_count, 4 * columns), BF16),
        in_specs=[SMEM, VMEM] + [HBM] * 16,
        out_specs=VMEM,
        scratch_shapes=[
            pltpu.VMEM((8, count // 2, padded, columns), BF16),
            pltpu.SemaphoreType.DMA((16,)),
        ],
        compiler_params=pltpu.CompilerParams(vmem_limit_bytes=20 << 20),
        name="queries",
    )(place, slices, *in_hbm(parts))


def attention_kernel(
    place_ref, sink_ref, packed_ref, pairs_ref, halo_ref, hidden_ref, *rest
):
    parts, (out_ref, held, mixed, total_ref, sems) = rest[:16], rest[16:]
    lines, quarter_rows, depth = held.shape[1:]
    copies = start_copies(parts, held, sems, 0)
    tok_count = packed_ref.shape[0]
    pair_width = 2 * HEAD_SIZE
    kv_width = KEY_VALUE_HEADS * HEAD_SIZE
    query_groups = QUERY_HEADS // KEY_VALUE_HEADS
    span = halo_ref.shape[0]
    query_pos = lax.broadcasted_iota(jnp.int32, (tok_count, span), 0)
    key_pos = lax.broadcasted_iota(jnp.int32, (tok_count, span), 1)
    inside = key_pos <= query_pos
    halo_valid = place_ref[0] + place_ref[1] + place_ref[3] > 0
    usable = key_pos < jnp.where(halo_valid, span, 0)
    left = lax.broadcasted_iota(jnp.int32, (span + tok_count, pair_width), 1) < HEAD_SIZE
    scale = float(HEAD_SIZE) ** (-0.5)

    def sides(start, head, factor):
        lanes = pl.ds(start + head // 2 * pair_width, pair_width)
        both = jnp.concatenate([halo_ref[:, lanes], pairs_ref[:, lanes]], axis=0)
        both = both.astype(F32) * factor
        turned = pltpu.roll(both, HEAD_SIZE, 1)
        low, high = (both, turned) if head % 2 == 0 else (turned, both)
        low = jnp.where(left, low, 0.0).astype(BF16)
        high = jnp.where(left, 0.0, high).astype(BF16)
        return low, high

    pairs = query_groups // 2
    for head in range(KEY_VALUE_HEADS):
        keys, values = sides(0, head, scale), sides(kv_width, head, 1.0)
        base = head * pairs * pair_width
        stacked = jnp.concatenate(
            [packed_ref[:, base + j * pair_width : base + (j + 1) * pair_width] for j in range(pairs)],
            axis=0,
        )
        outcome = None
        for side in range(2):
            scores = lax.dot_general(
                stacked, keys[side], (((1,), (1,)), ((), ())), preferred_element_type=F32
            )
            probs = []
            for j in range(pairs):
                piece = scores[j * tok_count : (j + 1) * tok_count]
                weights = jnp.exp(jnp.where(inside, piece[:, span:], piece[:, :span]))
                weights = jnp.where(inside | usable, weights, 0.0)
                sink = sink_ref[head * query_groups + 2 * j + side]
                sums = jnp.sum(weights, axis=-1, keepdims=True) + sink
                share = weights * (1.0 / sums)
                ahead = jnp.where(inside, 0.0, share).astype(BF16)
                own = jnp.where(inside, share, 0.0).astype(BF16)
                probs.append(jnp.concatenate([ahead, own], axis=1))
            part = jnp.dot(
                jnp.concatenate(probs, axis=0), values[side], preferred_element_type=F32
            )
            outcome = part if outcome is None else outcome + part
        for j in range(pairs):
            column = base + j * pair_width
            mixed[column // depth, :, column % depth : column % depth + pair_width] = outcome[
                j * tok_count : (j + 1) * tok_count
            ].astype(BF16)

    for pair in range(4):
        total = jnp.zeros((quarter_rows, tok_count), F32)
        for flip in range(2):
            for copy in copies[pair * 2 + flip]:
                copy.wait()
            for step in range(lines):
                total += lax.dot_general(
                    held[pair * 2 + flip, step],
                    mixed[shard_of(place_ref, block_step(step, lines), flip, lines)],
                    (((1,), (1,)), ((), ())),
                    preferred_element_type=F32,
                )
        start = quarter_of(place_ref, pair % 2, pair // 2) * quarter_rows
        total_ref[pl.ds(pl.multiple_of(start, 8), quarter_rows), :] = total
    out_ref[...] = (hidden_ref[...].astype(F32) + total_ref[...]).astype(BF16)


def attend_and_project(place, sinks, queries, pairs, halo, hidden_t, parts):
    width, tok_count = hidden_t.shape
    half, quarter_rows, depth = parts[0].shape
    lines = 2 * half
    return pl.pallas_call(
        attention_kernel,
        out_shape=jax.ShapeDtypeStruct((width, tok_count), BF16),
        in_specs=[SMEM] * 2 + [VMEM] * 4 + [HBM] * 16,
        out_specs=VMEM,
        scratch_shapes=[
            pltpu.VMEM((8, lines, quarter_rows, depth), BF16),
            pltpu.VMEM((2 * lines, tok_count, depth), BF16),
            pltpu.VMEM((width, tok_count), F32),
            pltpu.SemaphoreType.DMA((16,)),
        ],
        compiler_params=pltpu.CompilerParams(vmem_limit_bytes=24 << 20),
        name="attention",
    )(place, sinks, queries, pairs, halo, hidden_t, *in_hbm(parts))


def place_of():
    seq_index = lax.axis_index("seq")
    return jnp.stack(
        [seq_index // 2, seq_index % 2, lax.axis_index("groups") % 2, lax.axis_index("pipe")]
    ).astype(jnp.int32)


def own_quarters(qkv_proj, out_proj):
    rows, qkv_width = qkv_proj.shape
    quarter = lax.axis_index("groups") % 2 * 2 + lax.axis_index("pipe")
    query_width = QUERY_HEADS * HEAD_SIZE
    qw, pw, ow = query_width // 4, (qkv_width - query_width) // 4, out_proj.shape[1] // 4
    mine_queries = lax.dynamic_slice_in_dim(qkv_proj, quarter * qw, qw, 1)
    mine_pairs = lax.dynamic_slice_in_dim(qkv_proj, query_width + quarter * pw, pw, 1)
    mine_qkv = jnp.concatenate([mine_queries, mine_pairs], axis=1)
    mine_out = lax.dynamic_slice_in_dim(out_proj.T, quarter * ow, ow, 0)
    return jnp.pad(mine_qkv, ((0, -rows % 8), (0, 0))), mine_out


def flipped(value, bit):
    count = lax.axis_size("seq")
    return lax.ppermute(value, "seq", [(i, i ^ bit * 2) for i in range(count)])


def far_blocks(block, lines):
    bit = lines // 2
    found = {0: block}
    while bit > 1:
        for step in list(found):
            found[step + bit] = flipped(found[step], bit)
        bit //= 2
    return [found[step] for step in range(0, lines, 2)]


def gather_quarters(mine, lines, last_axis):
    far = far_blocks(mine, lines)
    even = stacked(far)
    odd = flipped(even, 1)
    even_mate, even_across = swapped(even, "seq"), swapped(even, "groups")
    odd_mate, odd_across = swapped(odd, "seq"), swapped(odd, "groups")
    even_last = swapped(even_mate, "groups")
    odd_last = swapped(odd_across if last_axis == "seq" else odd_mate, last_axis)
    parts = [even, odd, even_mate, odd_mate, even_across, odd_across, even_last, odd_last]
    return parts + [swapped(part, "pipe") for part in parts]


def fused_body(
    tokens, routes, route_weights, moe_gain, gate_up, down_proj, attn_gain, qkv_proj, sinks, out_proj
):
    seq_count = lax.axis_size("seq")
    tok_count, width = tokens.shape[1:]
    rows, qkv_width = qkv_proj.shape
    tokens_t, routes_t, scale_t = tokens[0].T, routes[0].T, route_weights[0].T
    place = place_of()

    block = prepare(tokens_t, routes_t, moe_gain)
    lines = seq_count // 2
    evens = far_blocks(block, lines)
    blocks = []
    for even in evens:
        odd = flipped(even, 1)
        for value in (even, odd):
            blocks += [value, swapped(value, "seq")]
    mine_qkv, mine_out = own_quarters(qkv_proj, out_proj)
    gate_up, down_proj, place, mine_qkv, mine_out = lax.optimization_barrier(
        (gate_up, down_proj, place, mine_qkv, mine_out)
    )
    qkv_parts = gather_quarters(mine_qkv, lines, "groups")
    out_parts = gather_quarters(mine_out, lines, "seq")

    gate_up, down_proj = in_hbm([gate_up, down_proj])
    first = [pltpu.with_memory_space_constraint(w, pltpu.VMEM) for w in fetch_first(gate_up, down_proj)]
    finished = run_experts(place, blocks, first, gate_up, down_proj)
    summed = lax.all_to_all(finished, "seq", split_axis=0, concat_axis=0, tiled=True)
    residual, coarse, fine = returns(tokens_t, routes_t, scale_t)

    summed = summed.reshape(E * CAP, width)
    query_width = QUERY_HEADS * HEAD_SIZE
    pairs, slices, hidden_t = project_pairs(
        place, summed, residual, coarse, fine, attn_gain, qkv_parts, rows, (qkv_width - query_width) // 4
    )
    halo = halo_exchange(pairs[tok_count - WINDOW_SPAN :])
    queries = project_queries(place, slices, qkv_parts, query_width // 4)
    out_t = attend_and_project(place, jnp.exp(sinks), queries, pairs, halo, hidden_t, out_parts)
    return out_t.T[None]


def swapped(value, axis):
    return lax.ppermute(value, axis, [(i, i ^ 1) for i in range(lax.axis_size(axis))])


def rms_scale(value_matrix, gain):
    widened = value_matrix.astype(jnp.float32)
    mean_square = jnp.mean(widened * widened, axis=-1, keepdims=True)
    return (widened * lax.rsqrt(mean_square + eps) * gain).astype(jnp.bfloat16)


def routing_tables(route_rows, route_scale):
    tok_count = route_rows.shape[0]
    experts = jnp.arange(E, dtype=jnp.int32)
    named = route_rows[None, :, :] == experts[:, None, None]
    member = jnp.any(named, axis=2)
    scale = jnp.sum(jnp.where(named, route_scale[None, :, :], 0.0), axis=2)
    token = jnp.arange(tok_count, dtype=jnp.int32)
    before = (token[:, None] < token[None, :]).astype(jnp.bfloat16)
    rank = jnp.dot(member.astype(jnp.bfloat16), before, preferred_element_type=jnp.float32)
    slot = jnp.arange(CAP, dtype=jnp.float32)
    chosen = member[:, None, :] & (rank[:, None, :] == slot[None, :, None])
    select = chosen.reshape(E * CAP, tok_count).astype(jnp.bfloat16)
    weighted = jnp.where(chosen, scale[:, None, :], 0.0).reshape(E * CAP, tok_count)
    return select, weighted


def neighbour_relay(block, seq_count):
    rounds = seq_count // 2
    up = [(i, i + 2) for i in range(seq_count - 2)]
    down = [(i + 2, i) for i in range(seq_count - 2)]
    rising, falling = [block], [block]
    for _ in range(rounds - 1):
        rising.append(lax.ppermute(rising[-1], "seq", up))
        falling.append(lax.ppermute(falling[-1], "seq", down))
    line = lax.axis_index("seq") // 2
    blocks = [block]
    for k in range(1, rounds):
        blocks.append(jnp.where(line >= k, rising[k], falling[rounds - k]))
    return blocks


def gather_weights(qkv_proj, out_proj):
    seq_count = lax.axis_size("seq")
    rows, qkv_width = qkv_proj.shape
    depth, width = out_proj.shape
    group_bit = lax.axis_index("groups") % 2
    pipe_bit = lax.axis_index("pipe")
    quarter = group_bit * 2 + pipe_bit
    qw, ow = qkv_width // 4, width // 4
    fold = ow // rows
    mine_qkv = lax.dynamic_slice_in_dim(qkv_proj, quarter * qw, qw, 1)
    mine_out = lax.dynamic_slice_in_dim(out_proj.T, quarter * ow, ow, 0)
    block = jnp.concatenate(
        [mine_qkv] + [mine_out[i * rows : (i + 1) * rows] for i in range(fold)], axis=1
    )
    blocks = neighbour_relay(block, seq_count)
    lines = seq_count // 2
    line = lax.axis_index("seq") // 2
    stacked = jnp.stack(blocks)
    column = jnp.stack(
        [lax.dynamic_index_in_dim(stacked, (line - j) % lines, 0, keepdims=False) for j in range(lines)]
    )
    other = swapped(column, "seq")
    odd = lax.axis_index("seq") % 2 == 1
    both = jnp.stack([jnp.where(odd, other, column), jnp.where(odd, column, other)], axis=1)
    both = both.reshape(seq_count, rows, block.shape[1])
    across = swapped(both, "groups")
    high = group_bit == 1
    halves = jnp.stack([jnp.where(high, across, both), jnp.where(high, both, across)])
    beside = swapped(halves, "pipe")
    second = pipe_bit == 1
    whole = jnp.stack([jnp.where(second, beside, halves), jnp.where(second, halves, beside)], axis=1)
    whole = whole.reshape(4, seq_count, rows, block.shape[1])
    qkv_full = whole[..., :qw].transpose(1, 2, 0, 3).reshape(seq_count * rows, qkv_width)
    out_full = whole[..., qw:].reshape(4, seq_count, rows, fold, depth)
    out_full = out_full.transpose(1, 4, 0, 3, 2).reshape(seq_count * depth, width)
    return qkv_full, out_full


def expert_layer(local, route_rows, route_scale, moe_gain, gate_up, down_proj):
    _, width = local.shape
    seq_count = lax.axis_size("seq")
    per_device = gate_up.shape[0]
    normed = rms_scale(local, moe_gain)
    select, weighted = routing_tables(route_rows, route_scale)
    table = jnp.dot(select, normed, preferred_element_type=jnp.float32).astype(jnp.bfloat16)
    by_expert = table.reshape(E, CAP, width)
    experts = max(1, per_device // 2)
    slabs = per_device // experts
    if slabs == 1:
        by_expert = jnp.repeat(by_expert, 2, axis=0)
    outgoing = by_expert.reshape(seq_count, experts, CAP, width)
    received = lax.all_to_all(outgoing, "seq", split_axis=0, concat_axis=0, tiled=True)
    rows = received.transpose(1, 0, 2, 3).reshape(experts, seq_count * CAP, width)
    gate_up = gate_up.reshape(experts, slabs, width, 2 * HALF)
    down_proj = down_proj.reshape(experts, slabs, HALF, width)
    projected = jnp.einsum("erd,ekdh->ekrh", rows, gate_up, preferred_element_type=jnp.float32)
    gate_part = projected[..., :HALF]
    up_part = projected[..., HALF:]
    hidden = (gate_part * jax.nn.sigmoid(1.702 * gate_part) * (up_part + 1.0)).astype(jnp.bfloat16)
    partial_value = jnp.einsum(
        "ekrh,ekhd->erd", hidden, down_proj, preferred_element_type=jnp.float32
    ).reshape(experts, seq_count, CAP, width)
    partial_value = partial_value.transpose(1, 0, 2, 3)
    if slabs == 2:
        finished = partial_value.astype(jnp.bfloat16)
    else:
        first = lax.axis_index("seq") % 2 == 0
        lower_rows = partial_value[:, :, : CAP // 2]
        upper_rows = partial_value[:, :, CAP // 2 :]
        kept = jnp.where(first, lower_rows, upper_rows)
        given = jnp.where(first, upper_rows, lower_rows)
        partner_part = swapped(given.astype(jnp.bfloat16), "seq").astype(given.dtype)
        finished = (kept + partner_part).astype(jnp.bfloat16)
    summed = lax.all_to_all(finished, "seq", split_axis=0, concat_axis=0, tiled=True).reshape(
        E * CAP, width
    )
    coarse = weighted.astype(jnp.bfloat16)
    fine = (weighted - coarse.astype(jnp.float32)).astype(jnp.bfloat16)
    dims = (((0,), (0,)), ((), ()))
    mixed = lax.dot_general(coarse, summed, dims, preferred_element_type=jnp.float32)
    mixed += lax.dot_general(fine, summed, dims, preferred_element_type=jnp.float32)
    return (local.astype(jnp.float32) + mixed).astype(jnp.bfloat16)


def attend(query_matrix, keys_extended, values_extended, head_sink_logits, halo_valid):
    tok_count = query_matrix.shape[0]
    query_groups = QUERY_HEADS // KEY_VALUE_HEADS
    scale = float(HEAD_SIZE) ** (-0.5)
    sink_mass_total = jnp.exp(head_sink_logits).reshape(KEY_VALUE_HEADS, query_groups, 1, 1)
    block_queries = query_matrix.reshape(tok_count, KEY_VALUE_HEADS, query_groups, HEAD_SIZE)
    block_keys = keys_extended.reshape(tok_count + WINDOW_SPAN, KEY_VALUE_HEADS, HEAD_SIZE)
    block_values = values_extended.reshape(tok_count + WINDOW_SPAN, KEY_VALUE_HEADS, HEAD_SIZE)
    scores = (
        jnp.einsum("qhgd,khd->hgqk", block_queries, block_keys, preferred_element_type=jnp.float32)
        * scale
    )
    query_pos = jnp.arange(tok_count, dtype=jnp.int32)[:, None] + WINDOW_SPAN
    key_pos = jnp.arange(tok_count + WINDOW_SPAN, dtype=jnp.int32)[None, :]
    distance = query_pos - key_pos
    allowed = (distance >= 0) & (distance < WINDOW_SPAN) & ((key_pos >= WINDOW_SPAN) | halo_valid)
    weights = jnp.where(allowed, jnp.exp(scores), 0.0)
    probs = (weights / (jnp.sum(weights, axis=-1, keepdims=True) + sink_mass_total)).astype(
        jnp.bfloat16
    )
    mixed = jnp.einsum("hgqk,khd->qhgd", probs, block_values, preferred_element_type=jnp.float32)
    return mixed.reshape(tok_count, QUERY_HEADS * HEAD_SIZE).astype(jnp.bfloat16)


def halo_exchange(pairs):
    seq_count, pipe_count = lax.axis_size("seq"), lax.axis_size("pipe")
    order = [s * pipe_count + p for p in range(pipe_count) for s in range(seq_count)]
    return lax.ppermute(pairs, ("seq", "pipe"), list(zip(order[:-1], order[1:])))


def body(
    tokens,
    routes,
    route_weights,
    moe_gain,
    gate_up,
    down_proj,
    attn_gain,
    qkv_proj,
    head_sink_logits,
    out_proj,
):
    if gate_up.shape[0] % 2 == 0 and out_proj.shape[0] % 128 == 0 and tokens.shape[1] == WINDOW_SPAN:
        return fused_body(
            tokens,
            routes,
            route_weights,
            moe_gain,
            gate_up,
            down_proj,
            attn_gain,
            qkv_proj,
            head_sink_logits,
            out_proj,
        )
    qkv_full, out_full = gather_weights(qkv_proj, out_proj)
    hidden = expert_layer(tokens[0], routes[0], route_weights[0], moe_gain, gate_up, down_proj)
    tok_count, _ = hidden.shape
    normed = rms_scale(hidden, attn_gain)
    seq_index = lax.axis_index("seq")
    pipe_index = lax.axis_index("pipe")
    halo_valid = (seq_index > 0) | (pipe_index > 0)
    query_width = QUERY_HEADS * HEAD_SIZE
    width_of_pair = KEY_VALUE_HEADS * HEAD_SIZE
    packed_heads = jnp.dot(normed, qkv_full, preferred_element_type=jnp.float32).astype(
        jnp.bfloat16
    )
    own_pairs = packed_heads[:, query_width:]
    halo_pairs = halo_exchange(own_pairs[tok_count - WINDOW_SPAN :])
    query_matrix = packed_heads[:, :query_width]
    pairs_ext = jnp.concatenate([halo_pairs, own_pairs], axis=0)
    keys_extended = pairs_ext[:, :width_of_pair]
    values_extended = pairs_ext[:, width_of_pair:]
    attended = attend(query_matrix, keys_extended, values_extended, head_sink_logits, halo_valid)
    projected = jnp.dot(attended, out_full, preferred_element_type=jnp.float32)
    return (hidden.astype(jnp.float32) + projected).astype(jnp.bfloat16)[None]


def solution(mesh):
    in_specs = (
        P("pipe", ("groups", "seq"), None),
        P("pipe", ("groups", "seq"), None),
        P("pipe", ("groups", "seq"), None),
        P(),
        P("seq", None, None),
        P("seq", None, None),
        P(),
        P("seq", None),
        P(),
        P("seq", None),
    )
    out_specs = P("pipe", ("groups", "seq"), None)
    return jax.shard_map(body, mesh=mesh, in_specs=in_specs, out_specs=out_specs, check_vma=False)
```

```python
import functools

import jax
import jax.numpy as jnp
from jax import lax
from jax.experimental import pallas as pl
from jax.experimental.pallas import tpu as pltpu
from jax.sharding import PartitionSpec as P


E = 16
QUERY_HEADS = 32
KEY_VALUE_HEADS = 4
HEAD_SIZE = 64
WINDOW_SPAN = 128
HALF = 720
CAP = 48


eps = 1e-05


F32 = jnp.float32
BF16 = jnp.bfloat16
VMEM = pl.BlockSpec(memory_space=pltpu.VMEM)
SMEM = pl.BlockSpec(memory_space=pltpu.SMEM)
HBM = pl.BlockSpec(memory_space=pltpu.HBM)


def route_slots(routes_ref):
    tok_count = routes_ref.shape[1]
    expert = lax.broadcasted_iota(jnp.int32, (E, tok_count), 0)
    member = jnp.zeros((E, tok_count), jnp.bool_)
    for k in range(routes_ref.shape[0]):
        member = member | (routes_ref[k : k + 1, :] == expert)
    first = lax.broadcasted_iota(jnp.int32, (tok_count, tok_count), 0)
    second = lax.broadcasted_iota(jnp.int32, (tok_count, tok_count), 1)
    before = jnp.where(first < second, 1.0, 0.0).astype(BF16)
    flags = jnp.where(member, 1.0, 0.0)
    rank = jnp.dot(flags.astype(BF16), before, preferred_element_type=F32)
    return flags, jnp.where(flags > 0.0, rank, -1.0)


def slot_lanes(width):
    spare = -width % 128
    return spare if spare >= E else spare + 128


def prepare_kernel(tokens_ref, routes_ref, gain_ref, block_ref):
    width, tok_count = tokens_ref.shape
    value = tokens_ref[...].astype(F32).T
    mean_square = jnp.mean(value * value, axis=-1, keepdims=True)
    normed = value * lax.rsqrt(mean_square + eps) * gain_ref[...][None, :]
    block_ref[:, :width] = normed.astype(BF16)
    _, rank = route_slots(routes_ref)
    spare = block_ref.shape[1] - width
    unused = jnp.full((spare - E, tok_count), -1.0, F32)
    block_ref[:, width:] = jnp.concatenate([rank, unused], axis=0).T.astype(BF16)


def prepare(tokens_t, routes_t, gain):
    width, tok_count = tokens_t.shape
    return pl.pallas_call(
        prepare_kernel,
        out_shape=jax.ShapeDtypeStruct((tok_count, width + slot_lanes(width)), BF16),
        in_specs=[VMEM] * 3,
        out_specs=VMEM,
        name="prepare",
    )(tokens_t, routes_t, gain)


def returns_kernel(tokens_ref, routes_ref, scale_ref, residual_ref, coarse_ref, fine_ref):
    tok_count = tokens_ref.shape[1]
    residual_ref[...] = tokens_ref[...].astype(F32).T.astype(BF16)
    _, rank = route_slots(routes_ref)
    expert_index = lax.broadcasted_iota(jnp.int32, (E, tok_count), 0)
    scale = jnp.zeros((E, tok_count), F32)
    for k in range(routes_ref.shape[0]):
        scale += jnp.where(routes_ref[k : k + 1, :] == expert_index, scale_ref[k : k + 1, :], 0.0)
    slot = lax.broadcasted_iota(jnp.int32, (CAP, tok_count), 0).astype(F32)
    rows = []
    for expert in range(E):
        hit = slot == rank[expert : expert + 1, :]
        rows.append(jnp.where(hit, scale[expert : expert + 1, :], 0.0))
    weighted = jnp.concatenate(rows, axis=0).T
    coarse = weighted.astype(BF16)
    coarse_ref[...] = coarse
    fine_ref[...] = (weighted - coarse.astype(F32)).astype(BF16)


def returns(tokens_t, routes_t, scale_t):
    width, tok_count = tokens_t.shape
    return pl.pallas_call(
        returns_kernel,
        out_shape=(
            pltpu.VMEM((tok_count, width), BF16),
            pltpu.VMEM((tok_count, E * CAP), BF16),
            pltpu.VMEM((tok_count, E * CAP), BF16),
        ),
        in_specs=[VMEM] * 3,
        out_specs=(VMEM,) * 3,
        name="returns",
    )(tokens_t, routes_t, scale_t)


def fetch_kernel(gate_up_ref, down_ref, gate_up_out, down_out, sems):
    copies = [
        pltpu.make_async_copy(gate_up_ref.at[0], gate_up_out, sems.at[0]),
        pltpu.make_async_copy(down_ref.at[0], down_out, sems.at[1]),
    ]
    for copy in copies:
        copy.start()
    for copy in copies:
        copy.wait()


def fetch_first(gate_up, down_proj):
    return pl.pallas_call(
        fetch_kernel,
        out_shape=(pltpu.VMEM(gate_up.shape[1:], BF16), pltpu.VMEM(down_proj.shape[1:], BF16)),
        in_specs=[HBM] * 2,
        out_specs=(VMEM, VMEM),
        scratch_shapes=[pltpu.SemaphoreType.DMA((2,))],
        compiler_params=pltpu.CompilerParams(vmem_limit_bytes=4 << 20),
        name="fetch",
    )(gate_up, down_proj)


def experts_kernel(lines, place_ref, *refs):
    blocks = refs[: 2 * lines]
    first_up, first_down, gate_up_ref, down_ref, out_ref = refs[2 * lines : 2 * lines + 5]
    picked, slots, total_ref, ups, downs, results, sems = refs[2 * lines + 5 :]
    experts, _, width = picked.shape
    per_device = gate_up_ref.shape[0]
    slabs = per_device // experts
    tok_count, _ = blocks[0].shape

    def weights(slab):
        spot = slab % 2
        return [
            pltpu.make_async_copy(gate_up_ref.at[slab], ups.at[spot], sems.at[spot]),
            pltpu.make_async_copy(down_ref.at[slab], downs.at[spot], sems.at[2 + spot]),
        ]

    def begin(slab):
        if slab < per_device:
            for copy in weights(slab):
                copy.start()

    begin(1)
    begin(2)
    place = shard_of(place_ref, 0, 0, lines) * experts
    slot = lax.broadcasted_iota(jnp.int32, (CAP, tok_count), 0).astype(F32)
    for i, block in enumerate(blocks):
        slots[i] = block[:, width:].astype(F32).T
        select = [slot == slots[i, pl.ds(place + e, 1), :] for e in range(experts)]
        select = jnp.where(jnp.concatenate(select, axis=0), 1.0, 0.0).astype(BF16)
        rows = jnp.dot(select, block[:, :width], preferred_element_type=F32).astype(BF16)
        for e in range(experts):
            picked[e, i * CAP : (i + 1) * CAP, :] = rows[e * CAP : (e + 1) * CAP]

    sent_back = []
    for slab in range(per_device):
        expert, part = slab // slabs, slab % slabs
        if slab == 0:
            gate_up, down = first_up, first_down
        else:
            for copy in weights(slab):
                copy.wait()
            gate_up, down = ups.at[slab % 2], downs.at[slab % 2]
        projected = jnp.dot(picked[expert], gate_up[...], preferred_element_type=F32)
        gate_part = projected[:, :HALF]
        up_part = projected[:, HALF:]
        hidden = (gate_part * jax.nn.sigmoid(1.702 * gate_part) * (up_part + 1.0)).astype(BF16)
        value = jnp.dot(hidden, down[...], preferred_element_type=F32)
        if slab >= 1:
            begin(slab + 2)
        if part < slabs - 1:
            total_ref[...] = value if part == 0 else total_ref[...] + value
            continue
        if part > 0:
            value += total_ref[...]
        for i in range(2 * lines):
            owner = shard_of(place_ref, i // 2, i % 2, lines)
            results[expert, owner] = value[i * CAP : (i + 1) * CAP].astype(BF16)
        copy = pltpu.make_async_copy(results.at[expert], out_ref.at[:, expert], sems.at[4 + expert])
        copy.start()
        sent_back.append(copy)
    for copy in sent_back:
        copy.wait()


def run_experts(place, blocks, first, gate_up, down_proj):
    seq_count = len(blocks)
    tok_count, sent = blocks[0].shape
    per_device, width, gate_width = gate_up.shape
    experts = per_device // 2
    return pl.pallas_call(
        functools.partial(experts_kernel, seq_count // 2),
        out_shape=pltpu.HBM((seq_count, experts, CAP, width), BF16),
        in_specs=[SMEM] + [VMEM] * (seq_count + 2) + [HBM] * 2,
        out_specs=HBM,
        scratch_shapes=[
            pltpu.VMEM((experts, seq_count * CAP, width), BF16),
            pltpu.VMEM((seq_count, sent - width, tok_count), F32),
            pltpu.VMEM((seq_count * CAP, width), F32),
            pltpu.VMEM((2, width, gate_width), BF16),
            pltpu.VMEM((2, down_proj.shape[1], width), BF16),
            pltpu.VMEM((experts, seq_count, CAP, width), BF16),
            pltpu.SemaphoreType.DMA((4 + experts,)),
        ],
        compiler_params=pltpu.CompilerParams(vmem_limit_bytes=36 << 20),
        name="experts",
    )(place, *blocks, *first, gate_up, down_proj)


def stack_kernel(*refs):
    *parts, out_ref, sems = refs
    copies = []
    for i, part in enumerate(parts):
        copy = pltpu.make_async_copy(part, out_ref.at[i], sems.at[i])
        copy.start()
        copies.append(copy)
    for copy in copies:
        copy.wait()


def stacked(parts):
    return pl.pallas_call(
        stack_kernel,
        out_shape=pltpu.HBM((len(parts),) + parts[0].shape, parts[0].dtype),
        in_specs=[pl.BlockSpec(memory_space=pl.ANY)] * len(parts),
        out_specs=HBM,
        scratch_shapes=[pltpu.SemaphoreType.DMA((len(parts),))],
        compiler_params=pltpu.CompilerParams(vmem_limit_bytes=1 << 20),
    )(*parts)


def in_hbm(parts):
    return [pltpu.with_memory_space_constraint(part, pltpu.HBM) for part in parts]


def start_copies(parts, held, sems, first):
    half = held.shape[1] // 2
    copies = []
    for i, part in enumerate(parts):
        target = held.at[i // 2, pl.ds(i % 2 * half, half)]
        source = part.at[:, :, pl.ds(first, held.shape[3])]
        copy = pltpu.make_async_copy(source, target, sems.at[i])
        copy.start()
        copies.append(copy)
    return [copies[i : i + 2] for i in range(0, len(copies), 2)]


def block_step(slot, lines):
    half = lines // 2
    return slot % half * 2 + slot // half


def shard_of(place_ref, step, flip, lines):
    line, bit = 0, 1
    while bit < lines:
        line += (place_ref[0] // bit + step // bit) % 2 * bit
        bit *= 2
    return line * 2 + (place_ref[1] + flip) % 2


def quarter_of(place_ref, group_flip, pipe_flip):
    return (place_ref[2] + group_flip) % 2 * 2 + (place_ref[3] + pipe_flip) % 2


def columns_of(held, slices, place_ref, first, copies, out_ref):
    tok_count, lines = slices.shape[1], held.shape[1]
    columns = out_ref.shape[1] // 4
    for pair in range(4):
        total = jnp.zeros((tok_count, columns), F32)
        for flip in range(2):
            for copy in copies[pair * 2 + flip] if copies else ():
                copy.wait()
            for step in range(lines):
                total += jnp.dot(
                    slices[shard_of(place_ref, block_step(step, lines), flip, lines)],
                    held[pair * 2 + flip, step, :, first : first + columns],
                    preferred_element_type=F32,
                )
        start = quarter_of(place_ref, pair % 2, pair // 2) * columns
        out_ref[:, pl.ds(pl.multiple_of(start, 128), columns)] = total.astype(BF16)


def pairs_kernel(
    rows, place_ref, tables_ref, residual_ref, coarse_ref, fine_ref, gain_ref, *rest
):
    parts, (pairs_ref, slices, hidden_ref, held, sems) = rest[:16], rest[16:]
    copies = start_copies(parts, held, sems, 0)
    table = tables_ref[...]
    mixed = jnp.dot(coarse_ref[...], table, preferred_element_type=F32)
    mixed += jnp.dot(fine_ref[...], table, preferred_element_type=F32)
    hidden = (residual_ref[...].astype(F32) + mixed).astype(BF16)
    hidden_ref[...] = hidden
    value = hidden.astype(F32)
    mean_square = jnp.mean(value * value, axis=-1, keepdims=True)
    normed = (value * lax.rsqrt(mean_square + eps) * gain_ref[...][None, :]).astype(BF16)
    slices[...] = jnp.zeros_like(slices)
    for s in range(slices.shape[0]):
        slices[s, :, :rows] = normed[:, s * rows : (s + 1) * rows]
    columns_of(held, slices, place_ref, held.shape[3] - pairs_ref.shape[1] // 4, copies, pairs_ref)


def project_pairs(place, tables, residual, coarse, fine, gain, parts, rows, columns):
    tok_count, width = residual.shape
    half, padded, both = parts[0].shape
    lines = 2 * half
    return pl.pallas_call(
        functools.partial(pairs_kernel, rows),
        out_shape=(
            jax.ShapeDtypeStruct((tok_count, 4 * columns), BF16),
            jax.ShapeDtypeStruct((2 * lines, tok_count, padded), BF16),
            jax.ShapeDtypeStruct((tok_count, width), BF16),
            pltpu.VMEM((8, lines, padded, both), BF16),
        ),
        in_specs=[SMEM] + [VMEM] * 5 + [HBM] * 16,
        out_specs=(VMEM,) * 4,
        scratch_shapes=[pltpu.SemaphoreType.DMA((16,))],
        compiler_params=pltpu.CompilerParams(vmem_limit_bytes=20 << 20),
        name="pairs",
    )(place, tables, residual, coarse, fine, gain, *in_hbm(parts))


def queries_kernel(place_ref, slices, hidden_ref, held, queries_ref, turned_ref):
    turned_ref[...] = hidden_ref[...].astype(F32).T.astype(BF16)
    columns_of(held, slices, place_ref, 0, None, queries_ref)


def project_queries(place, slices, hidden, held, columns):
    tok_count, width = hidden.shape
    return pl.pallas_call(
        queries_kernel,
        out_shape=(
            jax.ShapeDtypeStruct((tok_count, 4 * columns), BF16),
            jax.ShapeDtypeStruct((width, tok_count), BF16),
        ),
        in_specs=[SMEM] + [VMEM] * 3,
        out_specs=(VMEM, VMEM),
        compiler_params=pltpu.CompilerParams(vmem_limit_bytes=20 << 20),
        name="queries",
    )(place, slices, hidden, held)


def attention_kernel(
    place_ref, sink_ref, packed_ref, pairs_ref, halo_ref, hidden_ref, *rest
):
    parts, (out_ref, held, mixed, total_ref, sems) = rest[:16], rest[16:]
    lines, quarter_rows, depth = held.shape[1:]
    copies = start_copies(parts, held, sems, 0)
    tok_count = packed_ref.shape[0]
    pair_width = 2 * HEAD_SIZE
    kv_width = KEY_VALUE_HEADS * HEAD_SIZE
    query_groups = QUERY_HEADS // KEY_VALUE_HEADS
    span = halo_ref.shape[0]
    query_pos = lax.broadcasted_iota(jnp.int32, (tok_count, span), 0)
    key_pos = lax.broadcasted_iota(jnp.int32, (tok_count, span), 1)
    inside = key_pos <= query_pos
    halo_valid = place_ref[0] + place_ref[1] + place_ref[3] > 0
    usable = key_pos < jnp.where(halo_valid, span, 0)
    left = lax.broadcasted_iota(jnp.int32, (span + tok_count, pair_width), 1) < HEAD_SIZE
    scale = float(HEAD_SIZE) ** (-0.5)

    def sides(start, head, factor):
        lanes = pl.ds(start + head // 2 * pair_width, pair_width)
        both = jnp.concatenate([halo_ref[:, lanes], pairs_ref[:, lanes]], axis=0)
        both = both.astype(F32) * factor
        turned = pltpu.roll(both, HEAD_SIZE, 1)
        low, high = (both, turned) if head % 2 == 0 else (turned, both)
        low = jnp.where(left, low, 0.0).astype(BF16)
        high = jnp.where(left, 0.0, high).astype(BF16)
        return low, high

    pairs = query_groups // 2
    for head in range(KEY_VALUE_HEADS):
        keys, values = sides(0, head, scale), sides(kv_width, head, 1.0)
        base = head * pairs * pair_width
        stacked = jnp.concatenate(
            [packed_ref[:, base + j * pair_width : base + (j + 1) * pair_width] for j in range(pairs)],
            axis=0,
        )
        outcome = None
        for side in range(2):
            scores = lax.dot_general(
                stacked, keys[side], (((1,), (1,)), ((), ())), preferred_element_type=F32
            )
            probs = []
            for j in range(pairs):
                piece = scores[j * tok_count : (j + 1) * tok_count]
                weights = jnp.exp(jnp.where(inside, piece[:, span:], piece[:, :span]))
                weights = jnp.where(inside | usable, weights, 0.0)
                sink = sink_ref[head * query_groups + 2 * j + side]
                sums = jnp.sum(weights, axis=-1, keepdims=True) + sink
                share = weights * (1.0 / sums)
                ahead = jnp.where(inside, 0.0, share).astype(BF16)
                own = jnp.where(inside, share, 0.0).astype(BF16)
                probs.append(jnp.concatenate([ahead, own], axis=1))
            part = jnp.dot(
                jnp.concatenate(probs, axis=0), values[side], preferred_element_type=F32
            )
            outcome = part if outcome is None else outcome + part
        for j in range(pairs):
            column = base + j * pair_width
            mixed[column // depth, :, column % depth : column % depth + pair_width] = outcome[
                j * tok_count : (j + 1) * tok_count
            ].astype(BF16)

    for pair in range(4):
        total = jnp.zeros((quarter_rows, tok_count), F32)
        for flip in range(2):
            for copy in copies[pair * 2 + flip]:
                copy.wait()
            for step in range(lines):
                total += lax.dot_general(
                    held[pair * 2 + flip, step],
                    mixed[shard_of(place_ref, block_step(step, lines), flip, lines)],
                    (((1,), (1,)), ((), ())),
                    preferred_element_type=F32,
                )
        start = quarter_of(place_ref, pair % 2, pair // 2) * quarter_rows
        total_ref[pl.ds(pl.multiple_of(start, 8), quarter_rows), :] = total
    out_ref[...] = (hidden_ref[...].astype(F32) + total_ref[...]).astype(BF16)


def attend_and_project(place, sinks, queries, pairs, halo, hidden_t, parts):
    width, tok_count = hidden_t.shape
    half, quarter_rows, depth = parts[0].shape
    lines = 2 * half
    return pl.pallas_call(
        attention_kernel,
        out_shape=jax.ShapeDtypeStruct((width, tok_count), BF16),
        in_specs=[SMEM] * 2 + [VMEM] * 4 + [HBM] * 16,
        out_specs=VMEM,
        scratch_shapes=[
            pltpu.VMEM((8, lines, quarter_rows, depth), BF16),
            pltpu.VMEM((2 * lines, tok_count, depth), BF16),
            pltpu.VMEM((width, tok_count), F32),
            pltpu.SemaphoreType.DMA((16,)),
        ],
        compiler_params=pltpu.CompilerParams(vmem_limit_bytes=24 << 20),
        name="attention",
    )(place, sinks, queries, pairs, halo, hidden_t, *in_hbm(parts))


def place_of():
    seq_index = lax.axis_index("seq")
    return jnp.stack(
        [seq_index // 2, seq_index % 2, lax.axis_index("groups") % 2, lax.axis_index("pipe")]
    ).astype(jnp.int32)


def own_quarters(qkv_proj, out_proj):
    rows, qkv_width = qkv_proj.shape
    quarter = lax.axis_index("groups") % 2 * 2 + lax.axis_index("pipe")
    query_width = QUERY_HEADS * HEAD_SIZE
    qw, pw, ow = query_width // 4, (qkv_width - query_width) // 4, out_proj.shape[1] // 4
    mine_queries = lax.dynamic_slice_in_dim(qkv_proj, quarter * qw, qw, 1)
    mine_pairs = lax.dynamic_slice_in_dim(qkv_proj, query_width + quarter * pw, pw, 1)
    mine_qkv = jnp.concatenate([mine_queries, mine_pairs], axis=1)
    mine_out = lax.dynamic_slice_in_dim(out_proj.T, quarter * ow, ow, 0)
    return jnp.pad(mine_qkv, ((0, -rows % 8), (0, 0))), mine_out


def flipped(value, bit):
    count = lax.axis_size("seq")
    return lax.ppermute(value, "seq", [(i, i ^ bit * 2) for i in range(count)])


def far_blocks(block, lines):
    bit = lines // 2
    found = {0: block}
    while bit > 1:
        for step in list(found):
            found[step + bit] = flipped(found[step], bit)
        bit //= 2
    return [found[step] for step in range(0, lines, 2)]


def gather_quarters(mine, lines, last_axis):
    far = far_blocks(mine, lines)
    even = stacked(far)
    odd = flipped(even, 1)
    even_mate, even_across = swapped(even, "seq"), swapped(even, "groups")
    odd_mate, odd_across = swapped(odd, "seq"), swapped(odd, "groups")
    even_last = swapped(even_mate, "groups")
    odd_last = swapped(odd_across if last_axis == "seq" else odd_mate, last_axis)
    parts = [even, odd, even_mate, odd_mate, even_across, odd_across, even_last, odd_last]
    return parts + [swapped(part, "pipe") for part in parts]


def fused_body(
    tokens, routes, route_weights, moe_gain, gate_up, down_proj, attn_gain, qkv_proj, sinks, out_proj
):
    seq_count = lax.axis_size("seq")
    tok_count, width = tokens.shape[1:]
    rows, qkv_width = qkv_proj.shape
    tokens_t, routes_t, scale_t = tokens[0].T, routes[0].T, route_weights[0].T
    place = place_of()

    block = prepare(tokens_t, routes_t, moe_gain)
    lines = seq_count // 2
    evens = far_blocks(block, lines)
    blocks = []
    for even in evens:
        odd = flipped(even, 1)
        for value in (even, odd):
            blocks += [value, swapped(value, "seq")]
    mine_qkv, mine_out = own_quarters(qkv_proj, out_proj)
    gate_up, down_proj, place, masses, mine_qkv, mine_out = lax.optimization_barrier(
        (gate_up, down_proj, place, jnp.exp(sinks), mine_qkv, mine_out)
    )
    qkv_parts = gather_quarters(mine_qkv, lines, "groups")
    out_parts = gather_quarters(mine_out, lines, "seq")

    gate_up, down_proj = in_hbm([gate_up, down_proj])
    first = [pltpu.with_memory_space_constraint(w, pltpu.VMEM) for w in fetch_first(gate_up, down_proj)]
    finished = run_experts(place, blocks, first, gate_up, down_proj)
    summed = lax.all_to_all(finished, "seq", split_axis=0, concat_axis=0, tiled=True)
    residual, coarse, fine = returns(tokens_t, routes_t, scale_t)

    summed = summed.reshape(E * CAP, width)
    query_width = QUERY_HEADS * HEAD_SIZE
    pairs, slices, hidden, held = project_pairs(
        place, summed, residual, coarse, fine, attn_gain, qkv_parts, rows, (qkv_width - query_width) // 4
    )
    halo = halo_exchange(pairs[tok_count - WINDOW_SPAN :])
    queries, hidden_t = project_queries(place, slices, hidden, held, query_width // 4)
    out_t = attend_and_project(place, masses, queries, pairs, halo, hidden_t, out_parts)
    return out_t.T[None]


def swapped(value, axis):
    return lax.ppermute(value, axis, [(i, i ^ 1) for i in range(lax.axis_size(axis))])


def rms_scale(value_matrix, gain):
    widened = value_matrix.astype(jnp.float32)
    mean_square = jnp.mean(widened * widened, axis=-1, keepdims=True)
    return (widened * lax.rsqrt(mean_square + eps) * gain).astype(jnp.bfloat16)


def routing_tables(route_rows, route_scale):
    tok_count = route_rows.shape[0]
    experts = jnp.arange(E, dtype=jnp.int32)
    named = route_rows[None, :, :] == experts[:, None, None]
    member = jnp.any(named, axis=2)
    scale = jnp.sum(jnp.where(named, route_scale[None, :, :], 0.0), axis=2)
    token = jnp.arange(tok_count, dtype=jnp.int32)
    before = (token[:, None] < token[None, :]).astype(jnp.bfloat16)
    rank = jnp.dot(member.astype(jnp.bfloat16), before, preferred_element_type=jnp.float32)
    slot = jnp.arange(CAP, dtype=jnp.float32)
    chosen = member[:, None, :] & (rank[:, None, :] == slot[None, :, None])
    select = chosen.reshape(E * CAP, tok_count).astype(jnp.bfloat16)
    weighted = jnp.where(chosen, scale[:, None, :], 0.0).reshape(E * CAP, tok_count)
    return select, weighted


def neighbour_relay(block, seq_count):
    rounds = seq_count // 2
    up = [(i, i + 2) for i in range(seq_count - 2)]
    down = [(i + 2, i) for i in range(seq_count - 2)]
    rising, falling = [block], [block]
    for _ in range(rounds - 1):
        rising.append(lax.ppermute(rising[-1], "seq", up))
        falling.append(lax.ppermute(falling[-1], "seq", down))
    line = lax.axis_index("seq") // 2
    blocks = [block]
    for k in range(1, rounds):
        blocks.append(jnp.where(line >= k, rising[k], falling[rounds - k]))
    return blocks


def gather_weights(qkv_proj, out_proj):
    seq_count = lax.axis_size("seq")
    rows, qkv_width = qkv_proj.shape
    depth, width = out_proj.shape
    group_bit = lax.axis_index("groups") % 2
    pipe_bit = lax.axis_index("pipe")
    quarter = group_bit * 2 + pipe_bit
    qw, ow = qkv_width // 4, width // 4
    fold = ow // rows
    mine_qkv = lax.dynamic_slice_in_dim(qkv_proj, quarter * qw, qw, 1)
    mine_out = lax.dynamic_slice_in_dim(out_proj.T, quarter * ow, ow, 0)
    block = jnp.concatenate(
        [mine_qkv] + [mine_out[i * rows : (i + 1) * rows] for i in range(fold)], axis=1
    )
    blocks = neighbour_relay(block, seq_count)
    lines = seq_count // 2
    line = lax.axis_index("seq") // 2
    stacked = jnp.stack(blocks)
    column = jnp.stack(
        [lax.dynamic_index_in_dim(stacked, (line - j) % lines, 0, keepdims=False) for j in range(lines)]
    )
    other = swapped(column, "seq")
    odd = lax.axis_index("seq") % 2 == 1
    both = jnp.stack([jnp.where(odd, other, column), jnp.where(odd, column, other)], axis=1)
    both = both.reshape(seq_count, rows, block.shape[1])
    across = swapped(both, "groups")
    high = group_bit == 1
    halves = jnp.stack([jnp.where(high, across, both), jnp.where(high, both, across)])
    beside = swapped(halves, "pipe")
    second = pipe_bit == 1
    whole = jnp.stack([jnp.where(second, beside, halves), jnp.where(second, halves, beside)], axis=1)
    whole = whole.reshape(4, seq_count, rows, block.shape[1])
    qkv_full = whole[..., :qw].transpose(1, 2, 0, 3).reshape(seq_count * rows, qkv_width)
    out_full = whole[..., qw:].reshape(4, seq_count, rows, fold, depth)
    out_full = out_full.transpose(1, 4, 0, 3, 2).reshape(seq_count * depth, width)
    return qkv_full, out_full


def expert_layer(local, route_rows, route_scale, moe_gain, gate_up, down_proj):
    _, width = local.shape
    seq_count = lax.axis_size("seq")
    per_device = gate_up.shape[0]
    normed = rms_scale(local, moe_gain)
    select, weighted = routing_tables(route_rows, route_scale)
    table = jnp.dot(select, normed, preferred_element_type=jnp.float32).astype(jnp.bfloat16)
    by_expert = table.reshape(E, CAP, width)
    experts = max(1, per_device // 2)
    slabs = per_device // experts
    if slabs == 1:
        by_expert = jnp.repeat(by_expert, 2, axis=0)
    outgoing = by_expert.reshape(seq_count, experts, CAP, width)
    received = lax.all_to_all(outgoing, "seq", split_axis=0, concat_axis=0, tiled=True)
    rows = received.transpose(1, 0, 2, 3).reshape(experts, seq_count * CAP, width)
    gate_up = gate_up.reshape(experts, slabs, width, 2 * HALF)
    down_proj = down_proj.reshape(experts, slabs, HALF, width)
    projected = jnp.einsum("erd,ekdh->ekrh", rows, gate_up, preferred_element_type=jnp.float32)
    gate_part = projected[..., :HALF]
    up_part = projected[..., HALF:]
    hidden = (gate_part * jax.nn.sigmoid(1.702 * gate_part) * (up_part + 1.0)).astype(jnp.bfloat16)
    partial_value = jnp.einsum(
        "ekrh,ekhd->erd", hidden, down_proj, preferred_element_type=jnp.float32
    ).reshape(experts, seq_count, CAP, width)
    partial_value = partial_value.transpose(1, 0, 2, 3)
    if slabs == 2:
        finished = partial_value.astype(jnp.bfloat16)
    else:
        first = lax.axis_index("seq") % 2 == 0
        lower_rows = partial_value[:, :, : CAP // 2]
        upper_rows = partial_value[:, :, CAP // 2 :]
        kept = jnp.where(first, lower_rows, upper_rows)
        given = jnp.where(first, upper_rows, lower_rows)
        partner_part = swapped(given.astype(jnp.bfloat16), "seq").astype(given.dtype)
        finished = (kept + partner_part).astype(jnp.bfloat16)
    summed = lax.all_to_all(finished, "seq", split_axis=0, concat_axis=0, tiled=True).reshape(
        E * CAP, width
    )
    coarse = weighted.astype(jnp.bfloat16)
    fine = (weighted - coarse.astype(jnp.float32)).astype(jnp.bfloat16)
    dims = (((0,), (0,)), ((), ()))
    mixed = lax.dot_general(coarse, summed, dims, preferred_element_type=jnp.float32)
    mixed += lax.dot_general(fine, summed, dims, preferred_element_type=jnp.float32)
    return (local.astype(jnp.float32) + mixed).astype(jnp.bfloat16)


def attend(query_matrix, keys_extended, values_extended, head_sink_logits, halo_valid):
    tok_count = query_matrix.shape[0]
    query_groups = QUERY_HEADS // KEY_VALUE_HEADS
    scale = float(HEAD_SIZE) ** (-0.5)
    sink_mass_total = jnp.exp(head_sink_logits).reshape(KEY_VALUE_HEADS, query_groups, 1, 1)
    block_queries = query_matrix.reshape(tok_count, KEY_VALUE_HEADS, query_groups, HEAD_SIZE)
    block_keys = keys_extended.reshape(tok_count + WINDOW_SPAN, KEY_VALUE_HEADS, HEAD_SIZE)
    block_values = values_extended.reshape(tok_count + WINDOW_SPAN, KEY_VALUE_HEADS, HEAD_SIZE)
    scores = (
        jnp.einsum("qhgd,khd->hgqk", block_queries, block_keys, preferred_element_type=jnp.float32)
        * scale
    )
    query_pos = jnp.arange(tok_count, dtype=jnp.int32)[:, None] + WINDOW_SPAN
    key_pos = jnp.arange(tok_count + WINDOW_SPAN, dtype=jnp.int32)[None, :]
    distance = query_pos - key_pos
    allowed = (distance >= 0) & (distance < WINDOW_SPAN) & ((key_pos >= WINDOW_SPAN) | halo_valid)
    weights = jnp.where(allowed, jnp.exp(scores), 0.0)
    probs = (weights / (jnp.sum(weights, axis=-1, keepdims=True) + sink_mass_total)).astype(
        jnp.bfloat16
    )
    mixed = jnp.einsum("hgqk,khd->qhgd", probs, block_values, preferred_element_type=jnp.float32)
    return mixed.reshape(tok_count, QUERY_HEADS * HEAD_SIZE).astype(jnp.bfloat16)


def halo_exchange(pairs):
    seq_count, pipe_count = lax.axis_size("seq"), lax.axis_size("pipe")
    order = [s * pipe_count + p for p in range(pipe_count) for s in range(seq_count)]
    return lax.ppermute(pairs, ("seq", "pipe"), list(zip(order[:-1], order[1:])))


def body(
    tokens,
    routes,
    route_weights,
    moe_gain,
    gate_up,
    down_proj,
    attn_gain,
    qkv_proj,
    head_sink_logits,
    out_proj,
):
    if gate_up.shape[0] % 2 == 0 and out_proj.shape[0] % 128 == 0 and tokens.shape[1] == WINDOW_SPAN:
        return fused_body(
            tokens,
            routes,
            route_weights,
            moe_gain,
            gate_up,
            down_proj,
            attn_gain,
            qkv_proj,
            head_sink_logits,
            out_proj,
        )
    qkv_full, out_full = gather_weights(qkv_proj, out_proj)
    hidden = expert_layer(tokens[0], routes[0], route_weights[0], moe_gain, gate_up, down_proj)
    tok_count, _ = hidden.shape
    normed = rms_scale(hidden, attn_gain)
    seq_index = lax.axis_index("seq")
    pipe_index = lax.axis_index("pipe")
    halo_valid = (seq_index > 0) | (pipe_index > 0)
    query_width = QUERY_HEADS * HEAD_SIZE
    width_of_pair = KEY_VALUE_HEADS * HEAD_SIZE
    packed_heads = jnp.dot(normed, qkv_full, preferred_element_type=jnp.float32).astype(
        jnp.bfloat16
    )
    own_pairs = packed_heads[:, query_width:]
    halo_pairs = halo_exchange(own_pairs[tok_count - WINDOW_SPAN :])
    query_matrix = packed_heads[:, :query_width]
    pairs_ext = jnp.concatenate([halo_pairs, own_pairs], axis=0)
    keys_extended = pairs_ext[:, :width_of_pair]
    values_extended = pairs_ext[:, width_of_pair:]
    attended = attend(query_matrix, keys_extended, values_extended, head_sink_logits, halo_valid)
    projected = jnp.dot(attended, out_full, preferred_element_type=jnp.float32)
    return (hidden.astype(jnp.float32) + projected).astype(jnp.bfloat16)[None]


def solution(mesh):
    in_specs = (
        P("pipe", ("groups", "seq"), None),
        P("pipe", ("groups", "seq"), None),
        P("pipe", ("groups", "seq"), None),
        P(),
        P("seq", None, None),
        P("seq", None, None),
        P(),
        P("seq", None),
        P(),
        P("seq", None),
    )
    out_specs = P("pipe", ("groups", "seq"), None)
    return jax.shard_map(body, mesh=mesh, in_specs=in_specs, out_specs=out_specs, check_vma=False)
```

```python
import functools

import jax
import jax.numpy as jnp
from jax import lax
from jax.experimental import pallas as pl
from jax.experimental.pallas import tpu as pltpu
from jax.sharding import PartitionSpec as P


E = 16
QUERY_HEADS = 32
KEY_VALUE_HEADS = 4
HEAD_SIZE = 64
WINDOW_SPAN = 128
HALF = 720
CAP = 48


eps = 1e-05


F32 = jnp.float32
BF16 = jnp.bfloat16
VMEM = pl.BlockSpec(memory_space=pltpu.VMEM)
SMEM = pl.BlockSpec(memory_space=pltpu.SMEM)
HBM = pl.BlockSpec(memory_space=pltpu.HBM)
ANY = pl.BlockSpec(memory_space=pl.ANY)


def route_slots(routes_ref):
    tok_count = routes_ref.shape[1]
    expert = lax.broadcasted_iota(jnp.int32, (E, tok_count), 0)
    member = jnp.zeros((E, tok_count), jnp.bool_)
    for k in range(routes_ref.shape[0]):
        member = member | (routes_ref[k : k + 1, :] == expert)
    first = lax.broadcasted_iota(jnp.int32, (tok_count, tok_count), 0)
    second = lax.broadcasted_iota(jnp.int32, (tok_count, tok_count), 1)
    before = jnp.where(first < second, 1.0, 0.0).astype(BF16)
    flags = jnp.where(member, 1.0, 0.0)
    rank = jnp.dot(flags.astype(BF16), before, preferred_element_type=F32)
    return flags, jnp.where(flags > 0.0, rank, -1.0)


def slot_lanes(width):
    spare = -width % 128
    return spare if spare >= E else spare + 128


def prepare_kernel(tokens_ref, routes_ref, gain_ref, block_ref):
    width, tok_count = tokens_ref.shape
    value = tokens_ref[...].astype(F32).T
    mean_square = jnp.mean(value * value, axis=-1, keepdims=True)
    normed = value * lax.rsqrt(mean_square + eps) * gain_ref[...][None, :]
    block_ref[:, :width] = normed.astype(BF16)
    _, rank = route_slots(routes_ref)
    spare = block_ref.shape[1] - width
    unused = jnp.full((spare - E, tok_count), -1.0, F32)
    block_ref[:, width:] = jnp.concatenate([rank, unused], axis=0).T.astype(BF16)


def prepare(tokens_t, routes_t, gain):
    width, tok_count = tokens_t.shape
    return pl.pallas_call(
        prepare_kernel,
        out_shape=jax.ShapeDtypeStruct((tok_count, width + slot_lanes(width)), BF16),
        in_specs=[VMEM] * 3,
        out_specs=VMEM,
        name="prepare",
    )(tokens_t, routes_t, gain)


def returns_kernel(tokens_ref, routes_ref, scale_ref, residual_ref, coarse_ref, fine_ref):
    tok_count = tokens_ref.shape[1]
    residual_ref[...] = tokens_ref[...].astype(F32).T.astype(BF16)
    _, rank = route_slots(routes_ref)
    expert_index = lax.broadcasted_iota(jnp.int32, (E, tok_count), 0)
    scale = jnp.zeros((E, tok_count), F32)
    for k in range(routes_ref.shape[0]):
        scale += jnp.where(routes_ref[k : k + 1, :] == expert_index, scale_ref[k : k + 1, :], 0.0)
    slot = lax.broadcasted_iota(jnp.int32, (CAP, tok_count), 0).astype(F32)
    rows = []
    for expert in range(E):
        hit = slot == rank[expert : expert + 1, :]
        rows.append(jnp.where(hit, scale[expert : expert + 1, :], 0.0))
    weighted = jnp.concatenate(rows, axis=0).T
    coarse = weighted.astype(BF16)
    coarse_ref[...] = coarse
    fine_ref[...] = (weighted - coarse.astype(F32)).astype(BF16)


def returns(tokens_t, routes_t, scale_t):
    width, tok_count = tokens_t.shape
    return pl.pallas_call(
        returns_kernel,
        out_shape=(
            pltpu.VMEM((tok_count, width), BF16),
            pltpu.VMEM((tok_count, E * CAP), BF16),
            pltpu.VMEM((tok_count, E * CAP), BF16),
        ),
        in_specs=[VMEM] * 3,
        out_specs=(VMEM,) * 3,
        name="returns",
    )(tokens_t, routes_t, scale_t)


def fetch_kernel(gate_up_ref, down_ref, gate_up_out, down_out, sems):
    copies = [
        pltpu.make_async_copy(gate_up_ref.at[0], gate_up_out, sems.at[0]),
        pltpu.make_async_copy(down_ref.at[0], down_out, sems.at[1]),
    ]
    for copy in copies:
        copy.start()
    for copy in copies:
        copy.wait()


def fetch_first(gate_up, down_proj):
    return pl.pallas_call(
        fetch_kernel,
        out_shape=(pltpu.VMEM(gate_up.shape[1:], BF16), pltpu.VMEM(down_proj.shape[1:], BF16)),
        in_specs=[HBM] * 2,
        out_specs=(VMEM, VMEM),
        scratch_shapes=[pltpu.SemaphoreType.DMA((2,))],
        compiler_params=pltpu.CompilerParams(vmem_limit_bytes=4 << 20),
        name="fetch",
    )(gate_up, down_proj)


def experts_kernel(lines, place_ref, *refs):
    blocks = refs[: 2 * lines]
    first_up, first_down, gate_up_ref, down_ref, out_ref = refs[2 * lines : 2 * lines + 5]
    picked, slots, total_ref, ups, downs, results, sems = refs[2 * lines + 5 :]
    experts, _, width = picked.shape
    per_device = gate_up_ref.shape[0]
    slabs = per_device // experts
    tok_count, _ = blocks[0].shape

    def weights(slab):
        spot = slab % 2
        return [
            pltpu.make_async_copy(gate_up_ref.at[slab], ups.at[spot], sems.at[spot]),
            pltpu.make_async_copy(down_ref.at[slab], downs.at[spot], sems.at[2 + spot]),
        ]

    def begin(slab):
        if slab < per_device:
            for copy in weights(slab):
                copy.start()

    begin(1)
    begin(2)
    place = shard_of(place_ref, 0, 0, lines) * experts
    slot = lax.broadcasted_iota(jnp.int32, (CAP, tok_count), 0).astype(F32)
    for i, block in enumerate(blocks):
        slots[i] = block[:, width:].astype(F32).T
        select = [slot == slots[i, pl.ds(place + e, 1), :] for e in range(experts)]
        select = jnp.where(jnp.concatenate(select, axis=0), 1.0, 0.0).astype(BF16)
        rows = jnp.dot(select, block[:, :width], preferred_element_type=F32).astype(BF16)
        for e in range(experts):
            picked[e, i * CAP : (i + 1) * CAP, :] = rows[e * CAP : (e + 1) * CAP]

    sent_back = []
    for slab in range(per_device):
        expert, part = slab // slabs, slab % slabs
        if slab == 0:
            gate_up, down = first_up, first_down
        else:
            for copy in weights(slab):
                copy.wait()
            gate_up, down = ups.at[slab % 2], downs.at[slab % 2]
        projected = jnp.dot(picked[expert], gate_up[...], preferred_element_type=F32)
        gate_part = projected[:, :HALF]
        up_part = projected[:, HALF:]
        hidden = (gate_part * jax.nn.sigmoid(1.702 * gate_part) * (up_part + 1.0)).astype(BF16)
        value = jnp.dot(hidden, down[...], preferred_element_type=F32)
        if slab >= 1:
            begin(slab + 2)
        if part < slabs - 1:
            total_ref[...] = value if part == 0 else total_ref[...] + value
            continue
        if part > 0:
            value += total_ref[...]
        for i in range(2 * lines):
            owner = shard_of(place_ref, i // 2, i % 2, lines)
            results[expert, owner] = value[i * CAP : (i + 1) * CAP].astype(BF16)
        copy = pltpu.make_async_copy(results.at[expert], out_ref.at[:, expert], sems.at[4 + expert])
        copy.start()
        sent_back.append(copy)
    for copy in sent_back:
        copy.wait()


def run_experts(place, blocks, first, gate_up, down_proj):
    seq_count = len(blocks)
    tok_count, sent = blocks[0].shape
    per_device, width, gate_width = gate_up.shape
    experts = per_device // 2
    return pl.pallas_call(
        functools.partial(experts_kernel, seq_count // 2),
        out_shape=pltpu.HBM((seq_count, experts, CAP, width), BF16),
        in_specs=[SMEM] + [VMEM] * (seq_count + 2) + [HBM] * 2,
        out_specs=HBM,
        scratch_shapes=[
            pltpu.VMEM((experts, seq_count * CAP, width), BF16),
            pltpu.VMEM((seq_count, sent - width, tok_count), F32),
            pltpu.VMEM((seq_count * CAP, width), F32),
            pltpu.VMEM((2, width, gate_width), BF16),
            pltpu.VMEM((2, down_proj.shape[1], width), BF16),
            pltpu.VMEM((experts, seq_count, CAP, width), BF16),
            pltpu.SemaphoreType.DMA((4 + experts,)),
        ],
        compiler_params=pltpu.CompilerParams(vmem_limit_bytes=36 << 20),
        name="experts",
    )(place, *blocks, *first, gate_up, down_proj)


def stack_kernel(*refs):
    *parts, out_ref, sems = refs
    copies = []
    for i, part in enumerate(parts):
        copy = pltpu.make_async_copy(part, out_ref.at[i], sems.at[i])
        copy.start()
        copies.append(copy)
    for copy in copies:
        copy.wait()


def stacked(parts):
    return pl.pallas_call(
        stack_kernel,
        out_shape=pltpu.HBM((len(parts),) + parts[0].shape, parts[0].dtype),
        in_specs=[pl.BlockSpec(memory_space=pl.ANY)] * len(parts),
        out_specs=HBM,
        scratch_shapes=[pltpu.SemaphoreType.DMA((len(parts),))],
        compiler_params=pltpu.CompilerParams(vmem_limit_bytes=1 << 20),
    )(*parts)


def in_hbm(parts):
    return [pltpu.with_memory_space_constraint(part, pltpu.HBM) for part in parts]


def start_copies(parts, held, sems, first):
    half = held.shape[1] // 2
    copies = []
    for i, part in enumerate(parts):
        target = held.at[i // 2, pl.ds(i % 2 * half, half)]
        source = part.at[:, :, pl.ds(first, held.shape[3])]
        copy = pltpu.make_async_copy(source, target, sems.at[i])
        copy.start()
        copies.append(copy)
    return [copies[i : i + 2] for i in range(0, len(copies), 2)]


def block_step(slot, lines):
    half = lines // 2
    return slot % half * 2 + slot // half


def shard_of(place_ref, step, flip, lines):
    line, bit = 0, 1
    while bit < lines:
        line += (place_ref[0] // bit + step // bit) % 2 * bit
        bit *= 2
    return line * 2 + (place_ref[1] + flip) % 2


def quarter_of(place_ref, group_flip, pipe_flip):
    return (place_ref[2] + group_flip) % 2 * 2 + (place_ref[3] + pipe_flip) % 2


def columns_of(held, slices, place_ref, first, copies, out_ref):
    tok_count, lines = slices.shape[1], held.shape[1]
    columns = out_ref.shape[1] // 4
    for pair in range(4):
        total = jnp.zeros((tok_count, columns), F32)
        for flip in range(2):
            for copy in copies[pair * 2 + flip] if copies else ():
                copy.wait()
            for step in range(lines):
                total += jnp.dot(
                    slices[shard_of(place_ref, block_step(step, lines), flip, lines)],
                    held[pair * 2 + flip, step, :, first : first + columns],
                    preferred_element_type=F32,
                )
        start = quarter_of(place_ref, pair % 2, pair // 2) * columns
        out_ref[:, pl.ds(pl.multiple_of(start, 128), columns)] = total.astype(BF16)


def pairs_kernel(
    rows, place_ref, tables_ref, residual_ref, coarse_ref, fine_ref, gain_ref, *rest
):
    parts, (pairs_ref, slices, hidden_ref, held, sems) = rest[:16], rest[16:]
    copies = start_copies(parts, held, sems, 0)
    table = tables_ref[...]
    mixed = jnp.dot(coarse_ref[...], table, preferred_element_type=F32)
    mixed += jnp.dot(fine_ref[...], table, preferred_element_type=F32)
    hidden = (residual_ref[...].astype(F32) + mixed).astype(BF16)
    hidden_ref[...] = hidden
    value = hidden.astype(F32)
    mean_square = jnp.mean(value * value, axis=-1, keepdims=True)
    normed = (value * lax.rsqrt(mean_square + eps) * gain_ref[...][None, :]).astype(BF16)
    slices[:, :, rows:] = jnp.zeros(slices.shape[:2] + (slices.shape[2] - rows,), BF16)
    for s in range(slices.shape[0]):
        slices[s, :, :rows] = normed[:, s * rows : (s + 1) * rows]
    columns_of(held, slices, place_ref, held.shape[3] - pairs_ref.shape[1] // 4, copies, pairs_ref)


def project_pairs(place, tables, residual, coarse, fine, gain, parts, rows, columns):
    tok_count, width = residual.shape
    half, padded, both = parts[0].shape
    lines = 2 * half
    return pl.pallas_call(
        functools.partial(pairs_kernel, rows),
        out_shape=(
            jax.ShapeDtypeStruct((tok_count, 4 * columns), BF16),
            jax.ShapeDtypeStruct((2 * lines, tok_count, padded), BF16),
            jax.ShapeDtypeStruct((tok_count, width), BF16),
            pltpu.VMEM((8, lines, padded, both), BF16),
        ),
        in_specs=[SMEM] + [VMEM] * 5 + [HBM] * 16,
        out_specs=(VMEM,) * 4,
        scratch_shapes=[pltpu.SemaphoreType.DMA((16,))],
        compiler_params=pltpu.CompilerParams(vmem_limit_bytes=20 << 20),
        name="pairs",
    )(place, tables, residual, coarse, fine, gain, *in_hbm(parts))


def queries_kernel(place_ref, slices, hidden_ref, held, queries_ref, turned_ref):
    turned_ref[...] = hidden_ref[...].astype(F32).T.astype(BF16)
    columns_of(held, slices, place_ref, 0, None, queries_ref)


def project_queries(place, slices, hidden, held, columns):
    tok_count, width = hidden.shape
    return pl.pallas_call(
        queries_kernel,
        out_shape=(
            jax.ShapeDtypeStruct((tok_count, 4 * columns), BF16),
            jax.ShapeDtypeStruct((width, tok_count), BF16),
        ),
        in_specs=[SMEM] + [VMEM] * 3,
        out_specs=(VMEM, VMEM),
        compiler_params=pltpu.CompilerParams(vmem_limit_bytes=20 << 20),
        name="queries",
    )(place, slices, hidden, held)


def attention_kernel(
    place_ref, sink_ref, packed_ref, pairs_ref, halo_ref, hidden_ref, *rest
):
    parts, (out_ref, held, mixed, total_ref, sems) = rest[:16], rest[16:]
    lines, quarter_rows, depth = held.shape[1:]
    copies = start_copies(parts, held, sems, 0)
    tok_count = packed_ref.shape[0]
    pair_width = 2 * HEAD_SIZE
    kv_width = KEY_VALUE_HEADS * HEAD_SIZE
    query_groups = QUERY_HEADS // KEY_VALUE_HEADS
    span = halo_ref.shape[0]
    query_pos = lax.broadcasted_iota(jnp.int32, (tok_count, span), 0)
    key_pos = lax.broadcasted_iota(jnp.int32, (tok_count, span), 1)
    inside = key_pos <= query_pos
    halo_valid = place_ref[0] + place_ref[1] + place_ref[3] > 0
    usable = key_pos < jnp.where(halo_valid, span, 0)
    left = lax.broadcasted_iota(jnp.int32, (span + tok_count, pair_width), 1) < HEAD_SIZE
    scale = float(HEAD_SIZE) ** (-0.5)

    def sides(start, head, factor):
        lanes = pl.ds(start + head // 2 * pair_width, pair_width)
        both = jnp.concatenate([halo_ref[:, lanes], pairs_ref[:, lanes]], axis=0)
        both = both.astype(F32) * factor
        turned = pltpu.roll(both, HEAD_SIZE, 1)
        low, high = (both, turned) if head % 2 == 0 else (turned, both)
        low = jnp.where(left, low, 0.0).astype(BF16)
        high = jnp.where(left, 0.0, high).astype(BF16)
        return low, high

    pairs = query_groups // 2
    for head in range(KEY_VALUE_HEADS):
        keys, values = sides(0, head, scale), sides(kv_width, head, 1.0)
        base = head * pairs * pair_width
        stacked = jnp.concatenate(
            [packed_ref[:, base + j * pair_width : base + (j + 1) * pair_width] for j in range(pairs)],
            axis=0,
        )
        outcome = None
        for side in range(2):
            scores = lax.dot_general(
                stacked, keys[side], (((1,), (1,)), ((), ())), preferred_element_type=F32
            )
            probs = []
            for j in range(pairs):
                piece = scores[j * tok_count : (j + 1) * tok_count]
                weights = jnp.exp(jnp.where(inside, piece[:, span:], piece[:, :span]))
                weights = jnp.where(inside | usable, weights, 0.0)
                sink = sink_ref[head * query_groups + 2 * j + side]
                sums = jnp.sum(weights, axis=-1, keepdims=True) + sink
                share = weights * (1.0 / sums)
                ahead = jnp.where(inside, 0.0, share).astype(BF16)
                own = jnp.where(inside, share, 0.0).astype(BF16)
                probs.append(jnp.concatenate([ahead, own], axis=1))
            part = jnp.dot(
                jnp.concatenate(probs, axis=0), values[side], preferred_element_type=F32
            )
            outcome = part if outcome is None else outcome + part
        for j in range(pairs):
            column = base + j * pair_width
            mixed[column // depth, :, column % depth : column % depth + pair_width] = outcome[
                j * tok_count : (j + 1) * tok_count
            ].astype(BF16)

    for pair in range(4):
        total = jnp.zeros((quarter_rows, tok_count), F32)
        for flip in range(2):
            for copy in copies[pair * 2 + flip]:
                copy.wait()
            for step in range(lines):
                total += lax.dot_general(
                    held[pair * 2 + flip, step],
                    mixed[shard_of(place_ref, block_step(step, lines), flip, lines)],
                    (((1,), (1,)), ((), ())),
                    preferred_element_type=F32,
                )
        start = quarter_of(place_ref, pair % 2, pair // 2) * quarter_rows
        total_ref[pl.ds(pl.multiple_of(start, 8), quarter_rows), :] = total
    out_ref[...] = (hidden_ref[...].astype(F32) + total_ref[...]).astype(BF16)


def attend_and_project(place, sinks, queries, pairs, halo, hidden_t, parts):
    width, tok_count = hidden_t.shape
    half, quarter_rows, depth = parts[0].shape
    lines = 2 * half
    return pl.pallas_call(
        attention_kernel,
        out_shape=jax.ShapeDtypeStruct((width, tok_count), BF16),
        in_specs=[SMEM] * 2 + [VMEM] * 4 + [HBM] * 14 + [ANY] * 2,
        out_specs=VMEM,
        scratch_shapes=[
            pltpu.VMEM((8, lines, quarter_rows, depth), BF16),
            pltpu.VMEM((2 * lines, tok_count, depth), BF16),
            pltpu.VMEM((width, tok_count), F32),
            pltpu.SemaphoreType.DMA((16,)),
        ],
        compiler_params=pltpu.CompilerParams(vmem_limit_bytes=24 << 20),
        name="attention",
    )(place, sinks, queries, pairs, halo, hidden_t, *in_hbm(parts[:14]), *parts[14:])


def place_of():
    seq_index = lax.axis_index("seq")
    return jnp.stack(
        [seq_index // 2, seq_index % 2, lax.axis_index("groups") % 2, lax.axis_index("pipe")]
    ).astype(jnp.int32)


def own_quarters(qkv_proj, out_proj):
    rows, qkv_width = qkv_proj.shape
    quarter = lax.axis_index("groups") % 2 * 2 + lax.axis_index("pipe")
    query_width = QUERY_HEADS * HEAD_SIZE
    qw, pw, ow = query_width // 4, (qkv_width - query_width) // 4, out_proj.shape[1] // 4
    mine_queries = lax.dynamic_slice_in_dim(qkv_proj, quarter * qw, qw, 1)
    mine_pairs = lax.dynamic_slice_in_dim(qkv_proj, query_width + quarter * pw, pw, 1)
    mine_qkv = jnp.concatenate([mine_queries, mine_pairs], axis=1)
    mine_out = lax.dynamic_slice_in_dim(out_proj.T, quarter * ow, ow, 0)
    return jnp.pad(mine_qkv, ((0, -rows % 8), (0, 0))), mine_out


def flipped(value, bit):
    count = lax.axis_size("seq")
    return lax.ppermute(value, "seq", [(i, i ^ bit * 2) for i in range(count)])


def far_blocks(block, lines):
    bit = lines // 2
    found = {0: block}
    while bit > 1:
        for step in list(found):
            found[step + bit] = flipped(found[step], bit)
        bit //= 2
    return [found[step] for step in range(0, lines, 2)]


def gather_quarters(mine, lines, last_axis):
    far = far_blocks(mine, lines)
    even = stacked(far)
    odd = flipped(even, 1)
    even_mate, even_across = swapped(even, "seq"), swapped(even, "groups")
    odd_mate, odd_across = swapped(odd, "seq"), swapped(odd, "groups")
    even_last = swapped(even_mate, "groups")
    odd_last = swapped(odd_across if last_axis == "seq" else odd_mate, last_axis)
    parts = [even, odd, even_mate, odd_mate, even_across, odd_across, even_last, odd_last]
    return parts + [swapped(part, "pipe") for part in parts]


def fused_body(
    tokens, routes, route_weights, moe_gain, gate_up, down_proj, attn_gain, qkv_proj, sinks, out_proj
):
    seq_count = lax.axis_size("seq")
    tok_count, width = tokens.shape[1:]
    rows, qkv_width = qkv_proj.shape
    tokens_t, routes_t, scale_t = tokens[0].T, routes[0].T, route_weights[0].T
    place = place_of()

    block = prepare(tokens_t, routes_t, moe_gain)
    lines = seq_count // 2
    evens = far_blocks(block, lines)
    blocks = []
    for even in evens:
        odd = flipped(even, 1)
        for value in (even, odd):
            blocks += [value, swapped(value, "seq")]
    mine_qkv, mine_out = own_quarters(qkv_proj, out_proj)
    gate_up, down_proj, place, masses, mine_qkv, mine_out = lax.optimization_barrier(
        (gate_up, down_proj, place, jnp.exp(sinks), mine_qkv, mine_out)
    )
    qkv_parts = gather_quarters(mine_qkv, lines, "groups")
    out_parts = gather_quarters(mine_out, lines, "seq")

    gate_up, down_proj = in_hbm([gate_up, down_proj])
    first = [pltpu.with_memory_space_constraint(w, pltpu.VMEM) for w in fetch_first(gate_up, down_proj)]
    finished = run_experts(place, blocks, first, gate_up, down_proj)
    summed = lax.all_to_all(finished, "seq", split_axis=0, concat_axis=0, tiled=True)
    residual, coarse, fine = returns(tokens_t, routes_t, scale_t)

    summed = summed.reshape(E * CAP, width)
    query_width = QUERY_HEADS * HEAD_SIZE
    pairs, slices, hidden, held = project_pairs(
        place, summed, residual, coarse, fine, attn_gain, qkv_parts, rows, (qkv_width - query_width) // 4
    )
    halo = halo_exchange(pairs[tok_count - WINDOW_SPAN :])
    queries, hidden_t = project_queries(place, slices, hidden, held, query_width // 4)
    out_t = attend_and_project(place, masses, queries, pairs, halo, hidden_t, out_parts)
    return out_t.T[None]


def swapped(value, axis):
    return lax.ppermute(value, axis, [(i, i ^ 1) for i in range(lax.axis_size(axis))])


def rms_scale(value_matrix, gain):
    widened = value_matrix.astype(jnp.float32)
    mean_square = jnp.mean(widened * widened, axis=-1, keepdims=True)
    return (widened * lax.rsqrt(mean_square + eps) * gain).astype(jnp.bfloat16)


def routing_tables(route_rows, route_scale):
    tok_count = route_rows.shape[0]
    experts = jnp.arange(E, dtype=jnp.int32)
    named = route_rows[None, :, :] == experts[:, None, None]
    member = jnp.any(named, axis=2)
    scale = jnp.sum(jnp.where(named, route_scale[None, :, :], 0.0), axis=2)
    token = jnp.arange(tok_count, dtype=jnp.int32)
    before = (token[:, None] < token[None, :]).astype(jnp.bfloat16)
    rank = jnp.dot(member.astype(jnp.bfloat16), before, preferred_element_type=jnp.float32)
    slot = jnp.arange(CAP, dtype=jnp.float32)
    chosen = member[:, None, :] & (rank[:, None, :] == slot[None, :, None])
    select = chosen.reshape(E * CAP, tok_count).astype(jnp.bfloat16)
    weighted = jnp.where(chosen, scale[:, None, :], 0.0).reshape(E * CAP, tok_count)
    return select, weighted


def neighbour_relay(block, seq_count):
    rounds = seq_count // 2
    up = [(i, i + 2) for i in range(seq_count - 2)]
    down = [(i + 2, i) for i in range(seq_count - 2)]
    rising, falling = [block], [block]
    for _ in range(rounds - 1):
        rising.append(lax.ppermute(rising[-1], "seq", up))
        falling.append(lax.ppermute(falling[-1], "seq", down))
    line = lax.axis_index("seq") // 2
    blocks = [block]
    for k in range(1, rounds):
        blocks.append(jnp.where(line >= k, rising[k], falling[rounds - k]))
    return blocks


def gather_weights(qkv_proj, out_proj):
    seq_count = lax.axis_size("seq")
    rows, qkv_width = qkv_proj.shape
    depth, width = out_proj.shape
    group_bit = lax.axis_index("groups") % 2
    pipe_bit = lax.axis_index("pipe")
    quarter = group_bit * 2 + pipe_bit
    qw, ow = qkv_width // 4, width // 4
    fold = ow // rows
    mine_qkv = lax.dynamic_slice_in_dim(qkv_proj, quarter * qw, qw, 1)
    mine_out = lax.dynamic_slice_in_dim(out_proj.T, quarter * ow, ow, 0)
    block = jnp.concatenate(
        [mine_qkv] + [mine_out[i * rows : (i + 1) * rows] for i in range(fold)], axis=1
    )
    blocks = neighbour_relay(block, seq_count)
    lines = seq_count // 2
    line = lax.axis_index("seq") // 2
    stacked = jnp.stack(blocks)
    column = jnp.stack(
        [lax.dynamic_index_in_dim(stacked, (line - j) % lines, 0, keepdims=False) for j in range(lines)]
    )
    other = swapped(column, "seq")
    odd = lax.axis_index("seq") % 2 == 1
    both = jnp.stack([jnp.where(odd, other, column), jnp.where(odd, column, other)], axis=1)
    both = both.reshape(seq_count, rows, block.shape[1])
    across = swapped(both, "groups")
    high = group_bit == 1
    halves = jnp.stack([jnp.where(high, across, both), jnp.where(high, both, across)])
    beside = swapped(halves, "pipe")
    second = pipe_bit == 1
    whole = jnp.stack([jnp.where(second, beside, halves), jnp.where(second, halves, beside)], axis=1)
    whole = whole.reshape(4, seq_count, rows, block.shape[1])
    qkv_full = whole[..., :qw].transpose(1, 2, 0, 3).reshape(seq_count * rows, qkv_width)
    out_full = whole[..., qw:].reshape(4, seq_count, rows, fold, depth)
    out_full = out_full.transpose(1, 4, 0, 3, 2).reshape(seq_count * depth, width)
    return qkv_full, out_full


def expert_layer(local, route_rows, route_scale, moe_gain, gate_up, down_proj):
    _, width = local.shape
    seq_count = lax.axis_size("seq")
    per_device = gate_up.shape[0]
    normed = rms_scale(local, moe_gain)
    select, weighted = routing_tables(route_rows, route_scale)
    table = jnp.dot(select, normed, preferred_element_type=jnp.float32).astype(jnp.bfloat16)
    by_expert = table.reshape(E, CAP, width)
    experts = max(1, per_device // 2)
    slabs = per_device // experts
    if slabs == 1:
        by_expert = jnp.repeat(by_expert, 2, axis=0)
    outgoing = by_expert.reshape(seq_count, experts, CAP, width)
    received = lax.all_to_all(outgoing, "seq", split_axis=0, concat_axis=0, tiled=True)
    rows = received.transpose(1, 0, 2, 3).reshape(experts, seq_count * CAP, width)
    gate_up = gate_up.reshape(experts, slabs, width, 2 * HALF)
    down_proj = down_proj.reshape(experts, slabs, HALF, width)
    projected = jnp.einsum("erd,ekdh->ekrh", rows, gate_up, preferred_element_type=jnp.float32)
    gate_part = projected[..., :HALF]
    up_part = projected[..., HALF:]
    hidden = (gate_part * jax.nn.sigmoid(1.702 * gate_part) * (up_part + 1.0)).astype(jnp.bfloat16)
    partial_value = jnp.einsum(
        "ekrh,ekhd->erd", hidden, down_proj, preferred_element_type=jnp.float32
    ).reshape(experts, seq_count, CAP, width)
    partial_value = partial_value.transpose(1, 0, 2, 3)
    if slabs == 2:
        finished = partial_value.astype(jnp.bfloat16)
    else:
        first = lax.axis_index("seq") % 2 == 0
        lower_rows = partial_value[:, :, : CAP // 2]
        upper_rows = partial_value[:, :, CAP // 2 :]
        kept = jnp.where(first, lower_rows, upper_rows)
        given = jnp.where(first, upper_rows, lower_rows)
        partner_part = swapped(given.astype(jnp.bfloat16), "seq").astype(given.dtype)
        finished = (kept + partner_part).astype(jnp.bfloat16)
    summed = lax.all_to_all(finished, "seq", split_axis=0, concat_axis=0, tiled=True).reshape(
        E * CAP, width
    )
    coarse = weighted.astype(jnp.bfloat16)
    fine = (weighted - coarse.astype(jnp.float32)).astype(jnp.bfloat16)
    dims = (((0,), (0,)), ((), ()))
    mixed = lax.dot_general(coarse, summed, dims, preferred_element_type=jnp.float32)
    mixed += lax.dot_general(fine, summed, dims, preferred_element_type=jnp.float32)
    return (local.astype(jnp.float32) + mixed).astype(jnp.bfloat16)


def attend(query_matrix, keys_extended, values_extended, head_sink_logits, halo_valid):
    tok_count = query_matrix.shape[0]
    query_groups = QUERY_HEADS // KEY_VALUE_HEADS
    scale = float(HEAD_SIZE) ** (-0.5)
    sink_mass_total = jnp.exp(head_sink_logits).reshape(KEY_VALUE_HEADS, query_groups, 1, 1)
    block_queries = query_matrix.reshape(tok_count, KEY_VALUE_HEADS, query_groups, HEAD_SIZE)
    block_keys = keys_extended.reshape(tok_count + WINDOW_SPAN, KEY_VALUE_HEADS, HEAD_SIZE)
    block_values = values_extended.reshape(tok_count + WINDOW_SPAN, KEY_VALUE_HEADS, HEAD_SIZE)
    scores = (
        jnp.einsum("qhgd,khd->hgqk", block_queries, block_keys, preferred_element_type=jnp.float32)
        * scale
    )
    query_pos = jnp.arange(tok_count, dtype=jnp.int32)[:, None] + WINDOW_SPAN
    key_pos = jnp.arange(tok_count + WINDOW_SPAN, dtype=jnp.int32)[None, :]
    distance = query_pos - key_pos
    allowed = (distance >= 0) & (distance < WINDOW_SPAN) & ((key_pos >= WINDOW_SPAN) | halo_valid)
    weights = jnp.where(allowed, jnp.exp(scores), 0.0)
    probs = (weights / (jnp.sum(weights, axis=-1, keepdims=True) + sink_mass_total)).astype(
        jnp.bfloat16
    )
    mixed = jnp.einsum("hgqk,khd->qhgd", probs, block_values, preferred_element_type=jnp.float32)
    return mixed.reshape(tok_count, QUERY_HEADS * HEAD_SIZE).astype(jnp.bfloat16)


def halo_exchange(pairs):
    seq_count, pipe_count = lax.axis_size("seq"), lax.axis_size("pipe")
    order = [s * pipe_count + p for p in range(pipe_count) for s in range(seq_count)]
    return lax.ppermute(pairs, ("seq", "pipe"), list(zip(order[:-1], order[1:])))


def body(
    tokens,
    routes,
    route_weights,
    moe_gain,
    gate_up,
    down_proj,
    attn_gain,
    qkv_proj,
    head_sink_logits,
    out_proj,
):
    if gate_up.shape[0] % 2 == 0 and out_proj.shape[0] % 128 == 0 and tokens.shape[1] == WINDOW_SPAN:
        return fused_body(
            tokens,
            routes,
            route_weights,
            moe_gain,
            gate_up,
            down_proj,
            attn_gain,
            qkv_proj,
            head_sink_logits,
            out_proj,
        )
    qkv_full, out_full = gather_weights(qkv_proj, out_proj)
    hidden = expert_layer(tokens[0], routes[0], route_weights[0], moe_gain, gate_up, down_proj)
    tok_count, _ = hidden.shape
    normed = rms_scale(hidden, attn_gain)
    seq_index = lax.axis_index("seq")
    pipe_index = lax.axis_index("pipe")
    halo_valid = (seq_index > 0) | (pipe_index > 0)
    query_width = QUERY_HEADS * HEAD_SIZE
    width_of_pair = KEY_VALUE_HEADS * HEAD_SIZE
    packed_heads = jnp.dot(normed, qkv_full, preferred_element_type=jnp.float32).astype(
        jnp.bfloat16
    )
    own_pairs = packed_heads[:, query_width:]
    halo_pairs = halo_exchange(own_pairs[tok_count - WINDOW_SPAN :])
    query_matrix = packed_heads[:, :query_width]
    pairs_ext = jnp.concatenate([halo_pairs, own_pairs], axis=0)
    keys_extended = pairs_ext[:, :width_of_pair]
    values_extended = pairs_ext[:, width_of_pair:]
    attended = attend(query_matrix, keys_extended, values_extended, head_sink_logits, halo_valid)
    projected = jnp.dot(attended, out_full, preferred_element_type=jnp.float32)
    return (hidden.astype(jnp.float32) + projected).astype(jnp.bfloat16)[None]


def solution(mesh):
    in_specs = (
        P("pipe", ("groups", "seq"), None),
        P("pipe", ("groups", "seq"), None),
        P("pipe", ("groups", "seq"), None),
        P(),
        P("seq", None, None),
        P("seq", None, None),
        P(),
        P("seq", None),
        P(),
        P("seq", None),
    )
    out_specs = P("pipe", ("groups", "seq"), None)
    return jax.shard_map(body, mesh=mesh, in_specs=in_specs, out_specs=out_specs, check_vma=False)
```
